512 devices in a mesh: wide: 64 (over x, y, core), narrow: 8 (over z).
Axes of the slice: x: 4, y: 8, z: 8, core: 2. Of those that a mesh axis runs over, the one named last changes fastest.
Arguments:
- solution: float32 [640, 320, 320], P('wide', 'narrow'), may hold values from -6 to 6
- residual: float32 [640, 320, 320], P('wide', 'narrow'), may hold values from -45 to 45
- direction: float32 [640, 320, 320], P('wide', 'narrow'), may hold values from -14 to 14
- previous_product: float32 [1], replicated, may hold values from 9830400 to 98304000
- basis_x: float32 [640, 640], P('wide'), may hold values from -0.25 to 0.25
- basis_y: float32 [320, 320], P('narrow'), may hold values from -0.3125 to 0.3125
- basis_z: float32 [320, 320], P('narrow'), may hold values from -0.3125 to 0.3125
- eigen_x: float32 [640], replicated, may hold values from 0.2 to 4
- eigen_y: float32 [320], replicated, may hold values from 0.2 to 4
- eigen_z: float32 [320], replicated, may hold values from 0.2 to 4
Outputs:
- solution: float32 [640, 320, 320], P('wide', 'narrow')
- residual: float32 [640, 320, 320], P('wide', 'narrow')
- direction: float32 [640, 320, 320], P('wide', 'narrow')
The draws below stay inside these ranges and needn't reach their ends.
All inputs are finite; a program needn't handle non-finite values.
Results may differ from the reference program's by a relative error of at most 0.00021.
Values sent between devices are 32-bit elements; how exact they have to be, the bound alone decides.
A program may use at most 64 MiB of HBM per device.

```python
import math
import jax
import jax.numpy as jnp
from jax import lax

NX = 640
NY = 320
NZ = 320
ITERS = 1


def scaled_field(key, amplitude):
    noise_key = jax.random.fold_in(key, 0)
    along_x = jnp.arange(NX, dtype=jnp.float32) / (NX - 1)
    along_y = jnp.arange(NY, dtype=jnp.float32) / (NY - 1)
    ramp = (0.5 + along_x)[:, None, None] * (0.7 + 0.6 * along_y)[None, :, None]
    values = jax.random.truncated_normal(noise_key, -4.0, 4.0, (NX, NY, NZ), jnp.float32) * ramp
    return (amplitude * values).astype(jnp.float32)


def draw_residual(key, part):
    return scaled_field(jax.random.fold_in(key, 11), 1.0)


def draw_direction(key, part):
    return scaled_field(jax.random.fold_in(key, 23), 0.3)


def steps_of(key, extent, cuts, smallest, largest):
    loudness = 1.0
    for axis_at, shards_of in cuts:
        heights = jax.random.uniform(jax.random.fold_in(jax.random.fold_in(key, 6), axis_at), (shards_of,), jnp.float32, smallest / len(cuts), largest / len(cuts))
        loudness = loudness * jnp.repeat(jnp.exp(heights), extent[axis_at] // shards_of).reshape((-1,) + (1,) * (len(extent) - 1 - axis_at))
    return loudness


def centred(own_key, dims, scale, limit, shards=(), kind=jnp.bfloat16):
    loudness = steps_of(own_key, dims, shards, -0.22, 0.18) if shards else 1.0
    drawn = jax.random.normal(own_key, dims, jnp.float32) * scale * loudness
    return jnp.minimum(jnp.maximum(drawn, -limit), limit).astype(kind)


def setup_inputs(seed: int = 0) -> dict:
    arg_keys = jax.random.split(jax.random.key(seed), 11)
    return {
        "solution": centred(arg_keys[0], (NX, NY, NZ), 1.0, 6.0, ((0, 64), (1, 8)), jnp.float32),
        "residual": draw_residual(jax.random.fold_in(arg_keys[10], 71), 0),
        "direction": draw_direction(jax.random.fold_in(arg_keys[10], 71), 0),
        "previous_product": jnp.clip(jnp.exp(jax.random.uniform(arg_keys[3], (1,), jnp.float32, math.log(9830400), math.log(98304000))), 9830400, 98304000),
        "basis_x": centred(arg_keys[4], (NX, NX), NX ** -0.5, 0.25, ((0, 64),), jnp.float32),
        "basis_y": centred(arg_keys[5], (NY, NY), NY ** -0.5, 0.3125, ((0, 8),), jnp.float32),
        "basis_z": centred(arg_keys[6], (NZ, NZ), NZ ** -0.5, 0.3125, ((0, 8),), jnp.float32),
        "eigen_x": jnp.clip(jnp.exp(jax.random.uniform(arg_keys[7], (NX,), jnp.float32, math.log(0.2), math.log(4.0))), 0.2, 4.0),
        "eigen_y": jnp.clip(jnp.exp(jax.random.uniform(arg_keys[8], (NY,), jnp.float32, math.log(0.2), math.log(4.0))), 0.2, 4.0),
        "eigen_z": jnp.clip(jnp.exp(jax.random.uniform(arg_keys[9], (NZ,), jnp.float32, math.log(0.2), math.log(4.0))), 0.2, 4.0),
    }


mass_band = (1.0 / 5040.0, 1.0 / 42.0, 397.0 / 1680.0, 151.0 / 315.0, 397.0 / 1680.0, 1.0 / 42.0, 1.0 / 5040.0)
stiff_band = (-1.0 / 120.0, -0.2, -0.125, 2.0 / 3.0, -0.125, -0.2, -1.0 / 120.0)
highest = lax.Precision.HIGHEST


def banded(field, coeffs, axis, length):
    total = coeffs[0] * lax.slice_in_dim(field, 0, length, axis=axis)
    for offset in range(1, 7):
        total = total + coeffs[offset] * lax.slice_in_dim(field, offset, offset + length, axis=axis)
    return total


def apply_padded(padded, length_x, length_y):
    length_z = padded.shape[2]
    along_z = jnp.pad(padded, ((0, 0), (0, 0), (3, 3)))
    mass_z = banded(along_z, mass_band, 2, length_z)
    stiff_z = banded(along_z, stiff_band, 2, length_z)
    first = banded(mass_z, mass_band, 1, length_y)
    second = banded(mass_z, stiff_band, 1, length_y) + banded(stiff_z, mass_band, 1, length_y)
    return banded(first, stiff_band, 0, length_x) + banded(second, mass_band, 0, length_x)


def precondition(field, basis_x, basis_y, basis_z, eigen_x, eigen_y, eigen_z):
    spectral = jnp.einsum('xyz,zc->xyc', field, basis_z, precision=highest)
    spectral = jnp.einsum('xyc,yb->xbc', spectral, basis_y, precision=highest)
    spectral = jnp.einsum('xbc,xa->abc', spectral, basis_x, precision=highest)
    spectral = spectral / (eigen_x[:, None, None] + eigen_y[None, :, None] + eigen_z[None, None, :])
    spectral = jnp.einsum('abc,xa->xbc', spectral, basis_x, precision=highest)
    spectral = jnp.einsum('xbc,yb->xyc', spectral, basis_y, precision=highest)
    return jnp.einsum('xyc,zc->xyz', spectral, basis_z, precision=highest)


def reference(solution, residual, direction, previous_product, basis_x, basis_y, basis_z, eigen_x, eigen_y, eigen_z):
    product_before = previous_product[0]
    for iteration in range(ITERS):
        precond = precondition(residual, basis_x, basis_y, basis_z, eigen_x, eigen_y, eigen_z)
        product_now = jnp.sum(residual * precond)
        direction = precond + (product_now / product_before) * direction
        image = apply_padded(jnp.pad(direction, ((3, 3), (3, 3), (0, 0))), NX, NY)
        alpha = product_now / jnp.sum(direction * image)
        solution = solution + alpha * direction
        residual = residual - alpha * image
        product_before = product_now
    return solution, residual, direction
```

```python
import functools

import jax
import jax.numpy as jnp
from jax import lax
from jax.experimental import pallas as pl
from jax.experimental.pallas import tpu as pltpu
from jax.sharding import PartitionSpec as P

MASS = (151.0 / 315.0, 397.0 / 1680.0, 1.0 / 42.0, 1.0 / 5040.0)
STIFF = (2.0 / 3.0, -0.125, -0.2, -1.0 / 120.0)
MESH = pl.DeviceIdType.MESH
NW, NN = 64, 8
CX, CY, NZ, NX = 10, 40, 320, 640
TILES = 100


def dot(a, b, ca, cb):
    return lax.dot_general(
        a,
        b,
        (((ca,), (cb,)), ((), ())),
        precision=lax.Precision.HIGHEST,
        preferred_element_type=jnp.float32,
    )


def has_second(v):
    return (lax.rem(v, 2) == 0) | (lax.rem(v, 16) == 1)


def second_tile(v):
    odd = lax.rem(v, 2)
    return 64 + (1 - odd) * lax.div(v, 2) + odd * (32 + lax.div(v, 16))


def band(coeffs):
    gap = jnp.abs(
        lax.broadcasted_iota(jnp.int32, (NZ, NZ), 0) - lax.broadcasted_iota(jnp.int32, (NZ, NZ), 1)
    )
    out = jnp.zeros((NZ, NZ), jnp.float32)
    for o in range(4):
        out = jnp.where(gap == o, coeffs[o], out)
    return out


def total(a, b):
    return jnp.sum(jnp.sum(a * b, axis=0, keepdims=True), axis=1, keepdims=True)


def stencil(padded, my, ky, first, second, bands, out):
    def along_y(p, carry):
        c = padded[p, 8:48, :]
        m = MASS[0] * c
        k = STIFF[0] * c
        for o in (1, 2, 3):
            s = padded[p, 8 - o : 48 - o, :] + padded[p, 8 + o : 48 + o, :]
            m += MASS[o] * s
            k += STIFF[o] * s
        my[p] = m
        ky[p] = k
        return carry

    lax.fori_loop(0, CX + 6, along_y, 0)

    def along_x(q, carry):
        a = my[q + 3]
        f = MASS[0] * a
        g = STIFF[0] * a + MASS[0] * ky[q + 3]
        for o in (1, 2, 3):
            s = my[q + 3 - o] + my[q + 3 + o]
            t = ky[q + 3 - o] + ky[q + 3 + o]
            f += MASS[o] * s
            g += STIFF[o] * s + MASS[o] * t
        first[q] = g
        second[q] = f
        return carry

    lax.fori_loop(0, CX, along_x, 0)
    g = first[...].reshape(CX * CY, NZ)
    f = second[...].reshape(CX * CY, NZ)
    out[...] = dot(g, bands[0], 1, 0) + dot(f, bands[1], 1, 0)


def kernel(
    ez_ref,
    sol_ref,
    res_ref,
    dir_ref,
    prev_ref,
    bx_ref,
    by_ref,
    bz_ref,
    ex_ref,
    ey_ref,
    sol_out,
    res_out,
    dir_out,
    wx,
    wy,
    wz,
    bands,
    exc,
    vd,
    vp,
    my,
    ky,
    first,
    second,
    image,
    fresh,
    n1s,
    n1r,
    lines,
    t2,
    s1,
    u0,
    u1,
    v0,
    v1,
    s2,
    n2s,
    n2r,
    red,
    rb1,
    rb2,
    lsem,
    wxs,
    wxr,
    wyzs,
    wyr,
    wzr,
    hs,
    hr,
    n1ss,
    n1rs,
    us0,
    us1,
    ur0,
    ur1,
    vs0,
    vs1,
    vr0,
    vr1,
    n2ss,
    n2rs,
    rs1,
    rr1,
    rs2,
    rr2,
):
    w = lax.axis_index("wide")
    n = lax.axis_index("narrow")
    wup, wdn = lax.rem(w + 1, NW), lax.rem(w + NW - 1, NW)
    nup, ndn = lax.rem(n + 1, NN), lax.rem(n + NN - 1, NN)
    barrier = pltpu.get_barrier_semaphore()

    for v in (vd, vp):
        for p in (0, 1, 2, 13, 14, 15):
            v[p] = jnp.zeros((56, NZ), jnp.float32)
        for p in range(3, 13):
            v[p, 0:8, :] = jnp.zeros((8, NZ), jnp.float32)
            v[p, 48:56, :] = jnp.zeros((8, NZ), jnp.float32)
    u1[...] = jnp.zeros_like(u1)

    def greet(d, carry):
        pl.semaphore_signal(
            barrier, inc=1, device_id={"wide": lax.rem(w + d, NW)}, device_id_type=MESH
        )
        return carry

    lax.fori_loop(1, NW, greet, 0)
    for d in range(1, NN):
        pl.semaphore_signal(
            barrier, inc=1, device_id={"narrow": lax.rem(n + d, NN)}, device_id_type=MESH
        )
    for a in (wup, wdn):
        for b in (nup, ndn):
            pl.semaphore_signal(
                barrier, inc=1, device_id={"wide": a, "narrow": b}, device_id_type=MESH
            )

    vd[3:13, 8:48, :] = dir_ref[...]
    bands[0] = band(MASS)
    bands[1] = band(STIFF)
    exc[...] = jnp.transpose(jnp.broadcast_to(ex_ref[...], (128, NX)))

    pl.semaphore_wait(barrier, NW - 1 + NN - 1 + 4)

    def send(src, dst, ssem, rsem, where):
        c = pltpu.make_async_remote_copy(
            src_ref=src,
            dst_ref=dst,
            send_sem=ssem,
            recv_sem=rsem,
            device_id=where,
            device_id_type=MESH,
        )
        c.start()

    def done(ref, sem):
        pltpu.make_async_copy(ref, ref, sem).wait()

    ownz = pltpu.make_async_copy(bz_ref, wz.at[pl.ds(n * CY, CY)], lsem.at[0])
    owny = pltpu.make_async_copy(by_ref, wy.at[pl.ds(n * CY, CY)], lsem.at[1])
    ownx = pltpu.make_async_copy(bx_ref, wx.at[w], lsem.at[2])
    ownz.start()
    owny.start()
    ownx.start()
    for d in range(1, NN):
        at = {"narrow": lax.rem(n + d, NN)}
        send(bz_ref, wz.at[pl.ds(n * CY, CY)], wyzs.at[0], wzr, at)
    for d in range(1, NN):
        at = {"narrow": lax.rem(n + d, NN)}
        send(by_ref, wy.at[pl.ds(n * CY, CY)], wyzs.at[1], wyr, at)

    has = {"xu": w < NW - 1, "xd": w > 0, "yu": n < NN - 1, "yd": n > 0}
    spans = {
        "": (pl.ds(3, 10), pl.ds(3, 10)),
        "xu": (pl.ds(10, 3), pl.ds(0, 3)),
        "xd": (pl.ds(3, 3), pl.ds(13, 3)),
    }
    rows = {
        "": (pl.ds(8, 40), pl.ds(8, 40)),
        "yu": (pl.ds(40, 8), pl.ds(0, 8)),
        "yd": (pl.ds(8, 8), pl.ds(48, 8)),
    }
    opposite = {"": "", "xu": "xd", "xd": "xu", "yu": "yd", "yd": "yu"}
    ways = [
        ("xu", ""),
        ("xd", ""),
        ("", "yu"),
        ("", "yd"),
        ("xu", "yu"),
        ("xu", "yd"),
        ("xd", "yu"),
        ("xd", "yd"),
    ]

    def exists(a, b):
        if a and b:
            return has[a] & has[b]
        return has[a or b]

    def start_halo(v, field):
        for i, (a, b) in enumerate(ways):

            @pl.when(exists(a, b))
            def _(i=i, a=a, b=b):
                at = {}
                if a:
                    at["wide"] = wup if a == "xu" else wdn
                if b:
                    at["narrow"] = nup if b == "yu" else ndn
                send(
                    v.at[spans[a][0], rows[b][0]],
                    v.at[spans[a][1], rows[b][1]],
                    hs.at[field, i],
                    hr.at[field, i],
                    at,
                )

    def wait_halo(v, field):
        for i, (a, b) in enumerate(ways):

            @pl.when(exists(opposite[a], opposite[b]))
            def _(i=i, a=a, b=b):
                done(v.at[spans[a][1], rows[b][1]], hr.at[field, i])

    def drain_halo(v, field):
        for i, (a, b) in enumerate(ways):

            @pl.when(exists(a, b))
            def _(i=i, a=a, b=b):
                done(v.at[spans[a][0], rows[b][0]], hs.at[field, i])

    start_halo(vd, 0)

    def send_wx(d, carry):
        send(bx_ref, wx.at[w], wxs, wxr, {"wide": lax.rem(w + d, NW)})
        return carry

    lax.fori_loop(1, NW, send_wx, 0)

    ownz.wait()
    done(wz.at[pl.ds(0, 280)], wzr)
    res2 = res_ref[...].reshape(CX * CY, NZ)
    n1s[...] = dot(wz[...], res2, 0, 1)
    own1 = pltpu.make_async_copy(n1s.at[pl.ds(n * CY, CY)], n1r.at[n], n1rs.at[n])
    own1.start()
    for d in range(1, NN):
        v = lax.rem(n + d, NN)
        send(n1s.at[pl.ds(v * CY, CY)], n1r.at[n], n1ss, n1rs.at[n], {"narrow": v})

    wait_halo(vd, 0)
    stencil(vd, my, ky, first, second, bands, image)

    for m in range(NN):
        done(n1r.at[m], n1rs.at[m])
        for x in range(CX):
            lines[x * CY : x * CY + CY, m * CY : m * CY + CY] = n1r[m, :, x * CY : x * CY + CY]

    owny.wait()
    done(wy.at[pl.ds(0, 280)], wyr)
    t2[...] = dot(lines[...], wy[...], 1, 0)
    for x in range(CX):
        for j in range(2):
            s1[pl.ds(j * 400 + x, 40, stride=10), :] = t2[
                x * CY : x * CY + CY, 128 * j : 128 * j + 128
            ]
        s1[pl.ds(800 + x, 20, stride=10), :] = jnp.concatenate(
            [t2[x * CY : x * CY + 20, 256:320], t2[x * CY + 20 : x * CY + CY, 256:320]], axis=1
        )

    mine2 = second_tile(w)
    two = has_second(w)
    one = jnp.logical_not(two)
    here = pl.ds(w * CX, CX)

    def send_u(d, carry):
        v = lax.rem(w + d, NW)
        send(s1.at[pl.ds(v * CX, CX)], u0.at[here], us0, ur0, {"wide": v})

        @pl.when(has_second(v))
        def _():
            send(s1.at[pl.ds(second_tile(v) * CX, CX)], u1.at[here], us1, ur1, {"wide": v})

        return carry

    lax.fori_loop(1, NW, send_u, 0)
    own_u0 = pltpu.make_async_copy(s1.at[here], u0.at[here], lsem.at[3])
    own_u0.start()

    @pl.when(two)
    def _():
        c = pltpu.make_async_copy(s1.at[pl.ds(mine2 * CX, CX)], u1.at[here], lsem.at[4])
        c.start()
        c.wait()

    def shift_row(t):
        j = lax.div(t, 40)
        c = t - j * 40
        row = jnp.where(j == 0, ey_ref[:, 0:128], ey_ref[:, 128:256])
        tail = ey_ref[:, 256:320]
        row = jnp.where(j == 2, jnp.concatenate([tail, tail], axis=1), row)
        late = c + 20 * lax.div(j, 2)
        low = lax.broadcasted_iota(jnp.int32, (1, 128), 1) < 64
        return row + jnp.where(low, ez_ref[n * CY + c], ez_ref[n * CY + late])

    shift = jnp.concatenate([shift_row(w), shift_row(mine2)], axis=1)
    ownx.wait()
    done(wx.at[pl.ds(0, 63)], wxr)
    full = wx[...].reshape(NX, NX)
    own_u0.wait()
    done(u0.at[pl.ds(0, 630)], ur0)

    @pl.when(two)
    def _():
        done(u1.at[pl.ds(0, 630)], ur1)

    both = jnp.concatenate([u0[...], u1[...]], axis=1)
    spectral = dot(full, both, 0, 0)
    cols = jnp.concatenate([exc[...], exc[...]], axis=1)
    inverse = dot(full, spectral / (cols + shift), 1, 0)
    v0[...] = inverse[:, 0:128]
    v1[...] = inverse[:, 128:256]

    def send_v(d, carry):
        v = lax.rem(w + d, NW)
        send(v0.at[pl.ds(v * CX, CX)], s2.at[here], vs0, vr0, {"wide": v})
        return carry

    lax.fori_loop(1, NW, send_v, 0)
    own_v0 = pltpu.make_async_copy(v0.at[here], s2.at[here], lsem.at[5])
    own_v0.start()
    there = pl.ds(mine2 * CX, CX)

    @pl.when(two)
    def _():
        def send_v1(d, carry):
            v = lax.rem(w + d, NW)
            send(v1.at[pl.ds(v * CX, CX)], s2.at[there], vs1, vr1, {"wide": v})
            return carry

        lax.fori_loop(1, NW, send_v1, 0)
        c = pltpu.make_async_copy(v1.at[here], s2.at[there], lsem.at[6])
        c.start()
        c.wait()

    own_v0.wait()
    done(s2.at[pl.ds(0, 630)], vr0)

    @pl.when(two)
    def _():
        done(s2.at[pl.ds(0, 350)], vr1)

    @pl.when(one)
    def _():
        done(s2.at[pl.ds(0, 360)], vr1)

    for x in range(CX):
        r = x * CY
        for j in range(2):
            t2[r : r + CY, 128 * j : 128 * j + 128] = s2[pl.ds(j * 400 + x, 40, stride=10), :]
        b = s2[pl.ds(800 + x, 20, stride=10), :]
        t2[r : r + 20, 256:320] = b[:, 0:64]
        t2[r + 20 : r + CY, 256:320] = b[:, 64:128]
    lines[...] = dot(t2[...], wy[...], 1, 1)
    for m in range(NN):
        for x in range(CX):
            n2s[m * CY : m * CY + CY, x * CY : x * CY + CY] = lines[
                x * CY : x * CY + CY, m * CY : m * CY + CY
            ]
    own2 = pltpu.make_async_copy(
        n2s.at[pl.ds(n * CY, CY)], n2r.at[pl.ds(n * CY, CY)], lsem.at[7]
    )
    own2.start()
    for d in range(1, NN):
        v = lax.rem(n + d, NN)
        send(n2s.at[pl.ds(v * CY, CY)], n2r.at[pl.ds(n * CY, CY)], n2ss, n2rs, {"narrow": v})
    own2.wait()
    done(n2r.at[pl.ds(0, 280)], n2rs)
    precond = dot(n2r[...], wz[...], 0, 1)
    vp[3:13, 8:48, :] = precond.reshape(CX, CY, NZ)
    start_halo(vp, 1)
    wait_halo(vp, 1)
    stencil(vp, my, ky, first, second, bands, fresh)

    precond = vp[3:13, 8:48, :].reshape(CX * CY, NZ)
    direction = dir_ref[...].reshape(CX * CY, NZ)
    res2 = res_ref[...].reshape(CX * CY, NZ)
    items = (
        total(res2, precond),
        total(precond, fresh[...]),
        total(precond, image[...]),
        total(direction, image[...]),
    )
    lane = lax.broadcasted_iota(jnp.int32, (1, 128), 1)
    row = jnp.zeros((1, 128), jnp.float32)
    for i, item in enumerate(items):
        row = jnp.where(lane == i, item, row)
    red[0] = row
    rb1[n] = row
    for d in range(1, NN):
        send(red.at[0], rb1.at[n], rs1, rr1, {"narrow": lax.rem(n + d, NN)})
    done(rb1.at[pl.ds(0, 7)], rr1)
    row = jnp.sum(rb1[...], axis=0)
    red[1] = row
    rb2[w] = row

    def send_r(d, carry):
        send(red.at[1], rb2.at[w], rs2, rr2, {"wide": lax.rem(w + d, NW)})
        return carry

    lax.fori_loop(1, NW, send_r, 0)
    done(rb2.at[pl.ds(0, 63)], rr2)
    row = jnp.sum(rb2[...], axis=0)
    now, self_term, cross, curvature = (
        jnp.sum(jnp.where(lane == i, row, 0.0), axis=1, keepdims=True) for i in range(4)
    )
    ratio = now / prev_ref[...]
    curvature = self_term + 2.0 * ratio * cross + ratio * ratio * curvature
    alpha = now / curvature
    direction = precond + ratio * direction
    new_image = fresh[...] + ratio * image[...]
    sol2 = sol_ref[...].reshape(CX * CY, NZ)
    dir_out[...] = direction.reshape(CX, CY, NZ)
    sol_out[...] = (sol2 + alpha * direction).reshape(CX, CY, NZ)
    res_out[...] = (res2 - alpha * new_image).reshape(CX, CY, NZ)

    for i in range(2):
        done(wz.at[pl.ds(0, 280)], wyzs.at[i])
    done(wx.at[pl.ds(0, 63)], wxs)
    drain_halo(vd, 0)
    drain_halo(vp, 1)
    done(n1s.at[pl.ds(0, 280)], n1ss)
    done(n2s.at[pl.ds(0, 280)], n2ss)
    done(s1.at[pl.ds(0, 630)], us0)
    done(v0.at[pl.ds(0, 630)], vs0)

    @pl.when(two)
    def _():
        done(s1.at[pl.ds(0, 350)], us1)
        done(v1.at[pl.ds(0, 630)], vs1)

    @pl.when(one)
    def _():
        done(s1.at[pl.ds(0, 360)], us1)

    done(rb1.at[pl.ds(0, 7)], rs1)
    done(rb2.at[pl.ds(0, 63)], rs2)


def per_device(sol, res, direction, prev, bx, by, bz, ex, ey, ez):
    f32 = jnp.float32
    brick = jax.ShapeDtypeStruct((CX, CY, NZ), f32)
    vmem = pl.BlockSpec(memory_space=pltpu.VMEM)
    smem = pl.BlockSpec(memory_space=pltpu.SMEM)
    dma = pltpu.SemaphoreType.DMA
    shapes = [
        (NW, CX, NX),
        (NZ, NZ),
        (NZ, NZ),
        (2, NZ, NZ),
        (NX, 128),
        (16, 56, NZ),
        (16, 56, NZ),
        (16, CY, NZ),
        (16, CY, NZ),
        (CX, CY, NZ),
        (CX, CY, NZ),
        (400, NZ),
        (400, NZ),
        (NZ, 400),
        (NN, CY, 400),
        (400, NZ),
        (400, NZ),
        (1000, 128),
        (NX, 128),
        (NX, 128),
        (NX, 128),
        (NX, 128),
        (1000, 128),
        (NZ, 400),
        (NZ, 400),
        (2, 1, 128),
        (NN, 1, 128),
        (NW, 1, 128),
    ]
    sems = [
        (8,),
        (),
        (),
        (2,),
        (),
        (),
        (2, 8),
        (2, 8),
        (),
        (8,),
        (),
        (),
        (),
        (),
        (),
        (),
        (),
        (),
        (),
        (),
        (),
        (),
        (),
        (),
    ]
    return pl.pallas_call(
        kernel,
        out_shape=(brick, brick, brick),
        in_specs=[smem] + [vmem] * 9,
        out_specs=(vmem, vmem, vmem),
        scratch_shapes=[pltpu.VMEM(s, f32) for s in shapes] + [dma(s) for s in sems],
        compiler_params=pltpu.CompilerParams(
            collective_id=0, has_side_effects=True, vmem_limit_bytes=56 << 20
        ),
        name="iterate",
    )(
        ez,
        sol,
        res,
        direction,
        prev.reshape(1, 1),
        bx,
        by,
        bz,
        ex.reshape(1, NX),
        ey.reshape(1, NZ),
    )


def solution(mesh):
    field = P("wide", "narrow", None)
    in_specs = (
        field,
        field,
        field,
        P(),
        P("wide", None),
        P("narrow", None),
        P("narrow", None),
        P(),
        P(),
        P(),
    )
    return jax.shard_map(
        per_device, mesh=mesh, in_specs=in_specs, out_specs=(field, field, field), check_vma=False
    )
```

```python
import functools

import jax
import jax.numpy as jnp
from jax import lax
from jax.experimental import pallas as pl
from jax.experimental.pallas import tpu as pltpu
from jax.sharding import PartitionSpec as P

MASS = (151.0 / 315.0, 397.0 / 1680.0, 1.0 / 42.0, 1.0 / 5040.0)
STIFF = (2.0 / 3.0, -0.125, -0.2, -1.0 / 120.0)
MESH = pl.DeviceIdType.MESH
NW, NN = 64, 8
CX, CY, NZ, NX = 10, 40, 320, 640
TILES = 100


def dot(a, b, ca, cb):
    return lax.dot_general(
        a,
        b,
        (((ca,), (cb,)), ((), ())),
        precision=lax.Precision.HIGH,
        preferred_element_type=jnp.float32,
    )


def has_second(v):
    return (lax.rem(v, 2) == 0) | (lax.rem(v, 16) == 1)


def second_tile(v):
    odd = lax.rem(v, 2)
    return 64 + (1 - odd) * lax.div(v, 2) + odd * (32 + lax.div(v, 16))


def band(coeffs):
    gap = jnp.abs(
        lax.broadcasted_iota(jnp.int32, (NZ, NZ), 0) - lax.broadcasted_iota(jnp.int32, (NZ, NZ), 1)
    )
    out = jnp.zeros((NZ, NZ), jnp.float32)
    for o in range(4):
        out = jnp.where(gap == o, coeffs[o], out)
    return out


def total(a, b):
    return jnp.sum(jnp.sum(a * b, axis=0, keepdims=True), axis=1, keepdims=True)


def stencil(padded, my, ky, first, second, bands, out):
    def along_y(p, carry):
        c = padded[p, 8:48, :]
        m = MASS[0] * c
        k = STIFF[0] * c
        for o in (1, 2, 3):
            s = padded[p, 8 - o : 48 - o, :] + padded[p, 8 + o : 48 + o, :]
            m += MASS[o] * s
            k += STIFF[o] * s
        my[p] = m
        ky[p] = k
        return carry

    lax.fori_loop(0, CX + 6, along_y, 0)

    def along_x(q, carry):
        a = my[q + 3]
        f = MASS[0] * a
        g = STIFF[0] * a + MASS[0] * ky[q + 3]
        for o in (1, 2, 3):
            s = my[q + 3 - o] + my[q + 3 + o]
            t = ky[q + 3 - o] + ky[q + 3 + o]
            f += MASS[o] * s
            g += STIFF[o] * s + MASS[o] * t
        first[q] = g
        second[q] = f
        return carry

    lax.fori_loop(0, CX, along_x, 0)
    g = first[...].reshape(CX * CY, NZ)
    f = second[...].reshape(CX * CY, NZ)
    out[...] = dot(g, bands[0], 1, 0) + dot(f, bands[1], 1, 0)


def kernel(
    ez_ref,
    prev_ref,
    ex_ref,
    ey_ref,
    res_ref,
    dir_ref,
    bx_ref,
    by_ref,
    bz_ref,
    pre_out,
    img_out,
    scal_out,
    res,
    wx,
    wy,
    wz,
    bands,
    exc,
    vd,
    vp,
    my,
    ky,
    first,
    second,
    image,
    fresh,
    n1s,
    n1r,
    lines,
    t2,
    s1,
    u0,
    u1,
    v0,
    v1,
    s2,
    n2s,
    n2r,
    red,
    rb1,
    rb2,
    lsem,
    xs,
    xr,
    ybs,
    ybr,
    yfs,
    yfr,
    zbs,
    zbr,
    zfs,
    zfr,
    hs,
    hr,
    n1ss,
    n1rs,
    us0,
    us1,
    ur0,
    ur1,
    vs0,
    vs1,
    vr0,
    vr1,
    n2ss,
    n2rs,
    rs1,
    rr1,
    rs2,
    rr2,
):
    w = lax.axis_index("wide")
    n = lax.axis_index("narrow")
    wup, wdn = lax.rem(w + 1, NW), lax.rem(w + NW - 1, NW)
    nup, ndn = lax.rem(n + 1, NN), lax.rem(n + NN - 1, NN)
    core = lax.rem(w, 2)
    sibling = w + 1 - 2 * core
    gx, gy = lax.div(w, 16), lax.rem(lax.div(w, 2), 8)
    barrier = pltpu.get_barrier_semaphore()
    get_res = pltpu.make_async_copy(res_ref, res, lsem.at[8])
    get_dir = pltpu.make_async_copy(dir_ref, vd.at[pl.ds(3, CX), pl.ds(8, CY)], lsem.at[9])
    get_res.start()
    get_dir.start()

    for v in (vd, vp):
        for p in (0, 1, 2, 13, 14, 15):
            v[p] = jnp.zeros((56, NZ), jnp.float32)
        for p in range(3, 13):
            v[p, 0:8, :] = jnp.zeros((8, NZ), jnp.float32)
            v[p, 48:56, :] = jnp.zeros((8, NZ), jnp.float32)
    u1[...] = jnp.zeros_like(u1)

    def greet(d, carry):
        pl.semaphore_signal(
            barrier, inc=1, device_id={"wide": lax.rem(w + d, NW)}, device_id_type=MESH
        )
        return carry

    lax.fori_loop(1, NW, greet, 0)
    for d in range(1, NN):
        pl.semaphore_signal(
            barrier, inc=1, device_id={"narrow": lax.rem(n + d, NN)}, device_id_type=MESH
        )
    for a in (wup, wdn):
        for b in (nup, ndn):
            pl.semaphore_signal(
                barrier, inc=1, device_id={"wide": a, "narrow": b}, device_id_type=MESH
            )

    bands[0] = band(MASS)
    bands[1] = band(STIFF)
    exc[...] = jnp.transpose(jnp.broadcast_to(ex_ref[...].reshape(1, NX), (128, NX)))

    pl.semaphore_wait(barrier, NW - 1 + NN - 1 + 4)

    def send(src, dst, ssem, rsem, where):
        c = pltpu.make_async_remote_copy(
            src_ref=src,
            dst_ref=dst,
            send_sem=ssem,
            recv_sem=rsem,
            device_id=where,
            device_id_type=MESH,
        )
        c.start()

    def done(ref, sem):
        pltpu.make_async_copy(ref, ref, sem).wait()

    def near(d):
        return core == (d + 1) % 2

    def rows_of(v):
        return pl.ds(pl.multiple_of(v * CY, 8), CY)

    def share(own, whole, ssem, rsem):
        for d in range(1, NN):

            @pl.when(near(d))
            def _(d=d):
                at = {"narrow": lax.rem(n + d, NN)}
                send(own, whole.at[rows_of(n)], ssem, rsem.at[d], at)

    def hand_over(whole, rsem, fsem, gsem):
        for d in range(1, NN):

            @pl.when(near(d))
            def _(d=d):
                m = rows_of(lax.rem(n + NN - d, NN))
                done(whole.at[m], rsem.at[d])
                send(whole.at[m], whole.at[m], fsem, gsem, {"wide": sibling})

    def by_core(whole, sem, first_rows):
        @pl.when(core == 0)
        def _():
            done(whole.at[pl.ds(0, first_rows)], sem)

        @pl.when(core == 1)
        def _():
            done(whole.at[pl.ds(0, 280 - first_rows)], sem)

    ownz = pltpu.make_async_copy(bz_ref, wz.at[rows_of(n)], lsem.at[0])
    owny = pltpu.make_async_copy(by_ref, wy.at[rows_of(n)], lsem.at[1])
    ownx = pltpu.make_async_copy(bx_ref, wx.at[gx, gy, core], lsem.at[2])
    ownz.start()
    owny.start()
    ownx.start()
    share(bz_ref, wz, zbs, zbr)
    share(by_ref, wy, ybs, ybr)

    for d in range(1, 8):
        at = {"wide": gx * 16 + lax.rem(gy + d, 8) * 2 + core}
        send(bx_ref, wx.at[gx, gy, core], xs.at[0], xr.at[0], at)

    has = {"xu": w < NW - 1, "xd": w > 0, "yu": n < NN - 1, "yd": n > 0}
    spans = {
        "": (pl.ds(3, 10), pl.ds(3, 10)),
        "xu": (pl.ds(10, 3), pl.ds(0, 3)),
        "xd": (pl.ds(3, 3), pl.ds(13, 3)),
    }
    rows = {
        "": (pl.ds(8, 40), pl.ds(8, 40)),
        "yu": (pl.ds(40, 8), pl.ds(0, 8)),
        "yd": (pl.ds(8, 8), pl.ds(48, 8)),
    }
    opposite = {"": "", "xu": "xd", "xd": "xu", "yu": "yd", "yd": "yu"}
    ways = [
        ("xu", ""),
        ("xd", ""),
        ("", "yu"),
        ("", "yd"),
        ("xu", "yu"),
        ("xu", "yd"),
        ("xd", "yu"),
        ("xd", "yd"),
    ]

    def exists(a, b):
        if a and b:
            return has[a] & has[b]
        return has[a or b]

    def start_halo(v, field):
        for i, (a, b) in enumerate(ways):

            @pl.when(exists(a, b))
            def _(i=i, a=a, b=b):
                at = {}
                if a:
                    at["wide"] = wup if a == "xu" else wdn
                if b:
                    at["narrow"] = nup if b == "yu" else ndn
                send(
                    v.at[spans[a][0], rows[b][0]],
                    v.at[spans[a][1], rows[b][1]],
                    hs.at[field, i],
                    hr.at[field, i],
                    at,
                )

    def wait_halo(v, field):
        for i, (a, b) in enumerate(ways):

            @pl.when(exists(opposite[a], opposite[b]))
            def _(i=i, a=a, b=b):
                done(v.at[spans[a][1], rows[b][1]], hr.at[field, i])

    def drain_halo(v, field):
        for i, (a, b) in enumerate(ways):

            @pl.when(exists(a, b))
            def _(i=i, a=a, b=b):
                done(v.at[spans[a][0], rows[b][0]], hs.at[field, i])

    hand_over(wz, zbr, zfs, zfr)
    get_res.wait()
    res2 = res[...].reshape(CX * CY, NZ)
    ownz.wait()
    by_core(wz, zfr, 120)
    n1s[...] = dot(wz[...], res2, 0, 1)
    own1 = pltpu.make_async_copy(n1s.at[pl.ds(n * CY, CY)], n1r.at[n], n1rs.at[n])
    own1.start()
    for d in range(1, NN):
        v = lax.rem(n + d, NN)
        send(n1s.at[pl.ds(v * CY, CY)], n1r.at[n], n1ss, n1rs.at[n], {"narrow": v})

    hand_over(wy, ybr, yfs, yfr)
    get_dir.wait()
    start_halo(vd, 0)
    ownx.wait()
    done(wx.at[0, pl.ds(0, 7), 0], xr.at[0])
    for e in range(1, 4):
        at = {"wide": lax.rem(gx + e, 4) * 16 + gy * 2 + core}
        send(wx.at[gx, :, core], wx.at[gx, :, core], xs.at[1], xr.at[1], at)

    for m in range(NN):
        done(n1r.at[m], n1rs.at[m])
        for x in range(CX):
            lines[x * CY : x * CY + CY, m * CY : m * CY + CY] = n1r[m, :, x * CY : x * CY + CY]

    owny.wait()
    by_core(wy, yfr, 120)
    t2[...] = dot(lines[...], wy[...], 1, 0)
    for x in range(CX):
        for j in range(2):
            s1[pl.ds(j * 400 + x, 40, stride=10), :] = t2[
                x * CY : x * CY + CY, 128 * j : 128 * j + 128
            ]
        s1[pl.ds(800 + x, 20, stride=10), :] = jnp.concatenate(
            [t2[x * CY : x * CY + 20, 256:320], t2[x * CY + 20 : x * CY + CY, 256:320]], axis=1
        )

    mine2 = second_tile(w)
    two = has_second(w)
    one = jnp.logical_not(two)
    here = pl.ds(w * CX, CX)

    def send_u(d, carry):
        v = lax.rem(w + d, NW)
        send(s1.at[pl.ds(v * CX, CX)], u0.at[here], us0, ur0, {"wide": v})

        @pl.when(has_second(v))
        def _():
            send(s1.at[pl.ds(second_tile(v) * CX, CX)], u1.at[here], us1, ur1, {"wide": v})

        return carry

    lax.fori_loop(1, NW, send_u, 0)
    own_u0 = pltpu.make_async_copy(s1.at[here], u0.at[here], lsem.at[3])
    own_u0.start()

    @pl.when(two)
    def _():
        c = pltpu.make_async_copy(s1.at[pl.ds(mine2 * CX, CX)], u1.at[here], lsem.at[4])
        c.start()
        c.wait()

    ey = ey_ref[...].reshape(1, NZ)

    def shift_row(t):
        j = lax.div(t, 40)
        c = t - j * 40
        row = jnp.where(j == 0, ey[:, 0:128], ey[:, 128:256])
        tail = ey[:, 256:320]
        row = jnp.where(j == 2, jnp.concatenate([tail, tail], axis=1), row)
        late = c + 20 * lax.div(j, 2)
        low = lax.broadcasted_iota(jnp.int32, (1, 128), 1) < 64
        return row + jnp.where(low, ez_ref[n * CY + c], ez_ref[n * CY + late])

    shift = jnp.concatenate([shift_row(w), shift_row(mine2)], axis=1)
    done(wx.at[pl.ds(0, 3), :, 0], xr.at[1])
    send(wx.at[:, :, core], wx.at[:, :, core], xs.at[2], xr.at[2], {"wide": sibling})

    wait_halo(vd, 0)
    stencil(vd, my, ky, first, second, bands, image)

    done(wx.at[:, :, 0], xr.at[2])
    full = wx[...].reshape(NX, NX)
    own_u0.wait()
    done(u0.at[pl.ds(0, 630)], ur0)

    @pl.when(two)
    def _():
        done(u1.at[pl.ds(0, 630)], ur1)

    both = jnp.concatenate([u0[...], u1[...]], axis=1)
    spectral = dot(full, both, 0, 0)
    cols = jnp.concatenate([exc[...], exc[...]], axis=1)
    inverse = dot(full, spectral / (cols + shift), 1, 0)
    v0[...] = inverse[:, 0:128]
    v1[...] = inverse[:, 128:256]

    def send_v(d, carry):
        v = lax.rem(w + d, NW)
        send(v0.at[pl.ds(v * CX, CX)], s2.at[here], vs0, vr0, {"wide": v})
        return carry

    lax.fori_loop(1, NW, send_v, 0)
    own_v0 = pltpu.make_async_copy(v0.at[here], s2.at[here], lsem.at[5])
    own_v0.start()
    there = pl.ds(mine2 * CX, CX)

    @pl.when(two)
    def _():
        def send_v1(d, carry):
            v = lax.rem(w + d, NW)
            send(v1.at[pl.ds(v * CX, CX)], s2.at[there], vs1, vr1, {"wide": v})
            return carry

        lax.fori_loop(1, NW, send_v1, 0)
        c = pltpu.make_async_copy(v1.at[here], s2.at[there], lsem.at[6])
        c.start()
        c.wait()

    own_v0.wait()
    done(s2.at[pl.ds(0, 630)], vr0)

    @pl.when(two)
    def _():
        done(s2.at[pl.ds(0, 350)], vr1)

    @pl.when(one)
    def _():
        done(s2.at[pl.ds(0, 360)], vr1)

    for x in range(CX):
        r = x * CY
        for j in range(2):
            t2[r : r + CY, 128 * j : 128 * j + 128] = s2[pl.ds(j * 400 + x, 40, stride=10), :]
        b = s2[pl.ds(800 + x, 20, stride=10), :]
        t2[r : r + 20, 256:320] = b[:, 0:64]
        t2[r + 20 : r + CY, 256:320] = b[:, 64:128]
    lines[...] = dot(t2[...], wy[...], 1, 1)
    for m in range(NN):
        for x in range(CX):
            n2s[m * CY : m * CY + CY, x * CY : x * CY + CY] = lines[
                x * CY : x * CY + CY, m * CY : m * CY + CY
            ]
    own2 = pltpu.make_async_copy(
        n2s.at[pl.ds(n * CY, CY)], n2r.at[pl.ds(n * CY, CY)], lsem.at[7]
    )
    own2.start()
    for d in range(1, NN):
        v = lax.rem(n + d, NN)
        send(n2s.at[pl.ds(v * CY, CY)], n2r.at[pl.ds(n * CY, CY)], n2ss, n2rs, {"narrow": v})
    own2.wait()
    done(n2r.at[pl.ds(0, 280)], n2rs)
    precond = dot(n2r[...], wz[...], 0, 1)
    vp[3:13, 8:48, :] = precond.reshape(CX, CY, NZ)
    start_halo(vp, 1)
    wait_halo(vp, 1)
    stencil(vp, my, ky, first, second, bands, fresh)

    precond = vp[3:13, 8:48, :].reshape(CX * CY, NZ)
    direction = vd[3:13, 8:48, :].reshape(CX * CY, NZ)
    res2 = res[...].reshape(CX * CY, NZ)
    items = (
        total(res2, precond),
        total(precond, fresh[...]),
        total(precond, image[...]),
        total(direction, image[...]),
    )
    lane = lax.broadcasted_iota(jnp.int32, (1, 128), 1)
    row = jnp.zeros((1, 128), jnp.float32)
    for i, item in enumerate(items):
        row = jnp.where(lane == i, item, row)
    red[0] = row
    rb1[n] = row
    for d in range(1, NN):
        send(red.at[0], rb1.at[n], rs1, rr1, {"narrow": lax.rem(n + d, NN)})
    done(rb1.at[pl.ds(0, 7)], rr1)
    row = jnp.sum(rb1[...], axis=0)
    red[1] = row
    rb2[w] = row

    def send_r(d, carry):
        send(red.at[1], rb2.at[w], rs2, rr2, {"wide": lax.rem(w + d, NW)})
        return carry

    lax.fori_loop(1, NW, send_r, 0)
    done(rb2.at[pl.ds(0, 63)], rr2)
    row = jnp.sum(rb2[...], axis=0)
    now, self_term, cross, curvature = (
        jnp.sum(jnp.where(lane == i, row, 0.0), axis=1, keepdims=True) for i in range(4)
    )
    ratio = now / prev_ref[0]
    curvature = self_term + 2.0 * ratio * cross + ratio * ratio * curvature
    alpha = now / curvature
    pre_out[...] = precond.reshape(CX, CY, NZ)
    img_out[...] = (fresh[...] + ratio * image[...]).reshape(CX, CY, NZ)
    scal_out[...] = jnp.where(lane == 0, ratio, alpha)

    by_core(wz, zbs, 160)
    by_core(wz, zfs, 160)
    by_core(wy, ybs, 160)
    by_core(wy, yfs, 160)
    done(wx.at[0, pl.ds(0, 7), 0], xs.at[0])
    done(wx.at[pl.ds(0, 3), :, 0], xs.at[1])
    done(wx.at[:, :, 0], xs.at[2])
    drain_halo(vd, 0)
    drain_halo(vp, 1)
    done(n1s.at[pl.ds(0, 280)], n1ss)
    done(n2s.at[pl.ds(0, 280)], n2ss)
    done(s1.at[pl.ds(0, 630)], us0)
    done(v0.at[pl.ds(0, 630)], vs0)

    @pl.when(two)
    def _():
        done(s1.at[pl.ds(0, 350)], us1)
        done(v1.at[pl.ds(0, 630)], vs1)

    @pl.when(one)
    def _():
        done(s1.at[pl.ds(0, 360)], us1)

    done(rb1.at[pl.ds(0, 7)], rs1)
    done(rb2.at[pl.ds(0, 63)], rs2)


def per_device(sol, res, direction, prev, bx, by, bz, ex, ey, ez):
    f32 = jnp.float32
    brick = jax.ShapeDtypeStruct((CX, CY, NZ), f32)
    vmem = pl.BlockSpec(memory_space=pltpu.VMEM)
    smem = pl.BlockSpec(memory_space=pltpu.SMEM)
    hbm = pl.BlockSpec(memory_space=pltpu.HBM)
    dma = pltpu.SemaphoreType.DMA
    shapes = [
        (CX, CY, NZ),
        (4, 8, 2, CX, NX),
        (NZ, NZ),
        (NZ, NZ),
        (2, NZ, NZ),
        (NX, 128),
        (16, 56, NZ),
        (16, 56, NZ),
        (16, CY, NZ),
        (16, CY, NZ),
        (CX, CY, NZ),
        (CX, CY, NZ),
        (400, NZ),
        (400, NZ),
        (NZ, 400),
        (NN, CY, 400),
        (400, NZ),
        (400, NZ),
        (1000, 128),
        (NX, 128),
        (NX, 128),
        (NX, 128),
        (NX, 128),
        (1000, 128),
        (NZ, 400),
        (NZ, 400),
        (2, 1, 128),
        (NN, 1, 128),
        (NW, 1, 128),
    ]
    sems = [(10,), (3,), (3,), (), (8,), (), (), (), (8,), (), ()]
    sems += [(2, 8), (2, 8), (), (8,)] + [()] * 14
    precond, image, scal = pl.pallas_call(
        kernel,
        out_shape=(brick, brick, jax.ShapeDtypeStruct((1, 128), f32)),
        in_specs=[smem, smem, vmem, vmem] + [hbm] * 5,
        out_specs=(vmem, vmem, vmem),
        scratch_shapes=[pltpu.VMEM(s, f32) for s in shapes] + [dma(s) for s in sems],
        compiler_params=pltpu.CompilerParams(
            collective_id=0, has_side_effects=True, vmem_limit_bytes=56 << 20
        ),
        name="iterate",
    )(ez, prev, ex, ey, res, direction, bx, by, bz)
    ratio, alpha = scal[0, 0], scal[0, 1]
    direction = precond + ratio * direction
    return sol + alpha * direction, res - alpha * image, direction


def solution(mesh):
    field = P("wide", "narrow", None)
    in_specs = (
        field,
        field,
        field,
        P(),
        P("wide", None),
        P("narrow", None),
        P("narrow", None),
        P(),
        P(),
        P(),
    )
    return jax.shard_map(
        per_device, mesh=mesh, in_specs=in_specs, out_specs=(field, field, field), check_vma=False
    )
```

```python
import functools

import jax
import jax.numpy as jnp
from jax import lax
from jax.experimental import pallas as pl
from jax.experimental.pallas import tpu as pltpu
from jax.sharding import PartitionSpec as P

MASS = (151.0 / 315.0, 397.0 / 1680.0, 1.0 / 42.0, 1.0 / 5040.0)
STIFF = (2.0 / 3.0, -0.125, -0.2, -1.0 / 120.0)
MESH = pl.DeviceIdType.MESH
NW, NN = 64, 8
CX, CY, NZ, NX = 10, 40, 320, 640
CHUNKS = ((0, 5), (5, 5))


def dot(a, b, ca, cb):
    return lax.dot_general(
        a,
        b,
        (((ca,), (cb,)), ((), ())),
        precision=lax.Precision.HIGH,
        preferred_element_type=jnp.float32,
    )


def has_second(v):
    return (lax.rem(v, 2) == 0) | (lax.rem(v, 16) == 1)


def second_tile(v):
    odd = lax.rem(v, 2)
    return 64 + (1 - odd) * lax.div(v, 2) + odd * (32 + lax.div(v, 16))


def band(coeffs):
    gap = jnp.abs(
        lax.broadcasted_iota(jnp.int32, (NZ, NZ), 0) - lax.broadcasted_iota(jnp.int32, (NZ, NZ), 1)
    )
    out = jnp.zeros((NZ, NZ), jnp.float32)
    for o in range(4):
        out = jnp.where(gap == o, coeffs[o], out)
    return out


def total(a, b):
    return jnp.sum(jnp.sum(a * b, axis=0, keepdims=True), axis=1, keepdims=True)


def stencil(padded, my, ky, first, second, bands, out):
    def along_y(p, carry):
        c = padded[p, 8:48, :]
        m = MASS[0] * c
        k = STIFF[0] * c
        for o in (1, 2, 3):
            s = padded[p, 8 - o : 48 - o, :] + padded[p, 8 + o : 48 + o, :]
            m += MASS[o] * s
            k += STIFF[o] * s
        my[p] = m
        ky[p] = k
        return carry

    lax.fori_loop(0, CX + 6, along_y, 0)

    def along_x(q, carry):
        a = my[q + 3]
        f = MASS[0] * a
        g = STIFF[0] * a + MASS[0] * ky[q + 3]
        for o in (1, 2, 3):
            s = my[q + 3 - o] + my[q + 3 + o]
            t = ky[q + 3 - o] + ky[q + 3 + o]
            f += MASS[o] * s
            g += STIFF[o] * s + MASS[o] * t
        first[q] = g
        second[q] = f
        return carry

    lax.fori_loop(0, CX, along_x, 0)
    g = first[...].reshape(CX * CY, NZ)
    f = second[...].reshape(CX * CY, NZ)
    out[...] = dot(g, bands[0], 1, 0) + dot(f, bands[1], 1, 0)


def kernel(
    prev_ref,
    ex_hbm,
    ey_hbm,
    ez_hbm,
    sol_ref,
    res_ref,
    dir_ref,
    bx_ref,
    by_ref,
    bz_ref,
    sol_out,
    res_out,
    dir_out,
    ex_ref,
    ey_ref,
    ez_ref,
    sol,
    res,
    wx,
    wy,
    wz,
    bands,
    exc,
    vd,
    vp,
    my,
    ky,
    first,
    second,
    image,
    fresh,
    n1s,
    n1r,
    wxp,
    lines,
    t2,
    s1,
    u0,
    u1,
    v0,
    v1,
    s2,
    n2s,
    n2r,
    red,
    rb1,
    rb2,
    lsem,
    xs,
    xr,
    ybs,
    ybr,
    yfs,
    yfr,
    zbs,
    zbr,
    zfs,
    zfr,
    hs,
    hr,
    n1ss,
    n1rs,
    us0,
    us1,
    ur0,
    ur1,
    vs0,
    vs1,
    vr0,
    vr1,
    n2ss,
    n2rs,
    rs1,
    rr1,
    rs2,
    rr2,
):
    w = lax.axis_index("wide")
    n = lax.axis_index("narrow")
    wup, wdn = lax.rem(w + 1, NW), lax.rem(w + NW - 1, NW)
    nup, ndn = lax.rem(n + 1, NN), lax.rem(n + NN - 1, NN)
    core = lax.rem(w, 2)
    sibling = w + 1 - 2 * core
    gx, gy = lax.div(w, 16), lax.rem(lax.div(w, 2), 8)
    barrier = pltpu.get_barrier_semaphore()
    get_res = pltpu.make_async_copy(res_ref, res, lsem.at[8])
    get_dir = pltpu.make_async_copy(dir_ref, vd.at[pl.ds(3, CX), pl.ds(8, CY)], lsem.at[9])
    get_sol = pltpu.make_async_copy(sol_ref, sol, lsem.at[10])
    small = [
        pltpu.make_async_copy(a, b, lsem.at[11 + i])
        for i, (a, b) in enumerate(
            ((ex_hbm, ex_ref), (ey_hbm, ey_ref), (ez_hbm, ez_ref))
        )
    ]
    for c in [get_res, get_dir, *small, get_sol]:
        c.start()

    for v in (vd, vp):
        for p in (0, 1, 2, 13, 14, 15):
            v[p] = jnp.zeros((56, NZ), jnp.float32)
        for p in range(3, 13):
            v[p, 0:8, :] = jnp.zeros((8, NZ), jnp.float32)
            v[p, 48:56, :] = jnp.zeros((8, NZ), jnp.float32)
    u1[...] = jnp.zeros_like(u1)

    def greet(d, carry):
        pl.semaphore_signal(
            barrier, inc=1, device_id={"wide": lax.rem(w + d, NW)}, device_id_type=MESH
        )
        return carry

    lax.fori_loop(1, NW, greet, 0)
    for d in range(1, NN):
        pl.semaphore_signal(
            barrier, inc=1, device_id={"narrow": lax.rem(n + d, NN)}, device_id_type=MESH
        )
    for a in (wup, wdn):
        for b in (nup, ndn):
            pl.semaphore_signal(
                barrier, inc=1, device_id={"wide": a, "narrow": b}, device_id_type=MESH
            )

    bands[0] = band(MASS)
    bands[1] = band(STIFF)
    for c in small:
        c.wait()
    exc[...] = jnp.transpose(jnp.broadcast_to(ex_ref[...].reshape(1, NX), (128, NX)))

    pl.semaphore_wait(barrier, NW - 1 + NN - 1 + 4)

    def send(src, dst, ssem, rsem, where):
        c = pltpu.make_async_remote_copy(
            src_ref=src,
            dst_ref=dst,
            send_sem=ssem,
            recv_sem=rsem,
            device_id=where,
            device_id_type=MESH,
        )
        c.start()

    def done(ref, sem):
        pltpu.make_async_copy(ref, ref, sem).wait()

    def near(d):
        return core == (d + 1) % 2

    def rows_of(v):
        return pl.ds(pl.multiple_of(v * CY, 8), CY)

    def share(own, whole, ssem, rsem):
        for d in range(1, NN):

            @pl.when(near(d))
            def _(d=d):
                at = {"narrow": lax.rem(n + d, NN)}
                send(own, whole.at[rows_of(n)], ssem, rsem.at[d], at)

    def hand_over(whole, rsem, fsem, gsem):
        for d in range(1, NN):

            @pl.when(near(d))
            def _(d=d):
                m = rows_of(lax.rem(n + NN - d, NN))
                done(whole.at[m], rsem.at[d])
                send(whole.at[m], whole.at[m], fsem, gsem, {"wide": sibling})

    def by_core(whole, sem, first_rows):
        @pl.when(core == 0)
        def _():
            done(whole.at[pl.ds(0, first_rows)], sem)

        @pl.when(core == 1)
        def _():
            done(whole.at[pl.ds(0, 280 - first_rows)], sem)

    ownz = pltpu.make_async_copy(bz_ref, wz.at[rows_of(n)], lsem.at[0])
    owny = pltpu.make_async_copy(by_ref, wy.at[rows_of(n)], lsem.at[1])
    ownx = pltpu.make_async_copy(bx_ref, wx.at[gx, gy, core], lsem.at[2])
    ownz.start()
    owny.start()
    ownx.start()
    share(bz_ref, wz, zbs, zbr)
    share(by_ref, wy, ybs, ybr)

    for d in range(1, 8):
        at = {"wide": gx * 16 + lax.rem(gy + d, 8) * 2 + core}
        send(bx_ref, wx.at[gx, gy, core], xs.at[0], xr.at[0], at)

    has = {"xu": w < NW - 1, "xd": w > 0, "yu": n < NN - 1, "yd": n > 0}
    spans = {
        "": (pl.ds(3, 10), pl.ds(3, 10)),
        "xu": (pl.ds(10, 3), pl.ds(0, 3)),
        "xd": (pl.ds(3, 3), pl.ds(13, 3)),
    }
    rows = {
        "": (pl.ds(8, 40), pl.ds(8, 40)),
        "yu": (pl.ds(40, 8), pl.ds(0, 8)),
        "yd": (pl.ds(8, 8), pl.ds(48, 8)),
    }
    opposite = {"": "", "xu": "xd", "xd": "xu", "yu": "yd", "yd": "yu"}
    ways = [
        ("xu", ""),
        ("xd", ""),
        ("", "yu"),
        ("", "yd"),
        ("xu", "yu"),
        ("xu", "yd"),
        ("xd", "yu"),
        ("xd", "yd"),
    ]

    def exists(a, b):
        if a and b:
            return has[a] & has[b]
        return has[a or b]

    def start_halo(v, field):
        for i, (a, b) in enumerate(ways):

            @pl.when(exists(a, b))
            def _(i=i, a=a, b=b):
                at = {}
                if a:
                    at["wide"] = wup if a == "xu" else wdn
                if b:
                    at["narrow"] = nup if b == "yu" else ndn
                send(
                    v.at[spans[a][0], rows[b][0]],
                    v.at[spans[a][1], rows[b][1]],
                    hs.at[field, i],
                    hr.at[field, i],
                    at,
                )

    def wait_halo(v, field):
        for i, (a, b) in enumerate(ways):

            @pl.when(exists(opposite[a], opposite[b]))
            def _(i=i, a=a, b=b):
                done(v.at[spans[a][1], rows[b][1]], hr.at[field, i])

    def drain_halo(v, field):
        for i, (a, b) in enumerate(ways):

            @pl.when(exists(a, b))
            def _(i=i, a=a, b=b):
                done(v.at[spans[a][0], rows[b][0]], hs.at[field, i])

    hand_over(wz, zbr, zfs, zfr)
    get_res.wait()
    ownz.wait()
    by_core(wz, zfr, 120)
    for i, (x0, p) in enumerate(CHUNKS):
        n1s[i][...] = dot(wz[...], res[x0 : x0 + p].reshape(p * CY, NZ), 0, 1)
        pltpu.make_async_copy(n1s[i].at[rows_of(n)], n1r[i].at[n], n1rs.at[i, n]).start()
        for d in range(1, NN):
            v = lax.rem(n + d, NN)
            at = {"narrow": v}
            send(n1s[i].at[rows_of(v)], n1r[i].at[n], n1ss.at[i], n1rs.at[i, n], at)

    hand_over(wy, ybr, yfs, yfr)
    get_dir.wait()
    start_halo(vd, 0)
    ownx.wait()
    done(wx.at[0, pl.ds(0, 7), 0], xr.at[0])
    for e in range(1, 4):
        at = {"wide": lax.rem(gx + e, 4) * 16 + gy * 2 + core}
        send(wx.at[gx, :, core], wx.at[gx, :, core], xs.at[1], xr.at[1], at)

    mine2 = second_tile(w)
    two = has_second(w)
    one = jnp.logical_not(two)

    for i, (x0, p) in enumerate(CHUNKS):
        for m in range(NN):
            done(n1r[i].at[m], n1rs.at[i, m])
            for x in range(p):
                r = (x0 + x) * CY
                lines[r : r + CY, m * CY : m * CY + CY] = n1r[i][m, :, x * CY : x * CY + CY]
        if i == 0:
            owny.wait()
            by_core(wy, yfr, 120)
        span = slice(x0 * CY, (x0 + p) * CY)
        t2[span, :] = dot(lines[span, :], wy[...], 1, 0)
        for x in range(x0, x0 + p):
            r = x * CY
            for j in range(2):
                s1[pl.ds(j * 400 + x, 40, stride=10), :] = t2[
                    r : r + CY, 128 * j : 128 * j + 128
                ]
            s1[pl.ds(800 + x, 20, stride=10), :] = jnp.concatenate(
                [t2[r : r + 20, 256:320], t2[r + 20 : r + CY, 256:320]], axis=1
            )
        here = pl.ds(64 * x0 + w * p, p)

        def send_u(d, carry, i=i, x0=x0, p=p, here=here):
            v = lax.rem(w + d, NW)
            at = {"wide": v}
            send(s1.at[pl.ds(v * CX + x0, p)], u0.at[here], us0.at[i], ur0.at[i], at)

            @pl.when(has_second(v))
            def _():
                src = s1.at[pl.ds(second_tile(v) * CX + x0, p)]
                send(src, u1.at[here], us1.at[i], ur1.at[i], at)

            return carry

        lax.fori_loop(1, NW, send_u, 0, unroll=3)
        own = pltpu.make_async_copy(s1.at[pl.ds(w * CX + x0, p)], u0.at[here], lsem.at[3])
        own.start()
        own.wait()

        @pl.when(two)
        def _(x0=x0, p=p, here=here):
            c = pltpu.make_async_copy(
                s1.at[pl.ds(mine2 * CX + x0, p)], u1.at[here], lsem.at[4]
            )
            c.start()
            c.wait()

    ey = ey_ref[...].reshape(1, NZ)

    def shift_row(t):
        j = lax.div(t, 40)
        c = t - j * 40
        row = jnp.where(j == 0, ey[:, 0:128], ey[:, 128:256])
        tail = ey[:, 256:320]
        row = jnp.where(j == 2, jnp.concatenate([tail, tail], axis=1), row)
        late = c + 20 * lax.div(j, 2)
        low = lax.broadcasted_iota(jnp.int32, (1, 128), 1) < 64
        return row + jnp.where(low, ez_ref[n * CY + c], ez_ref[n * CY + late])

    shift = jnp.concatenate([shift_row(w), shift_row(mine2)], axis=1)
    done(wx.at[pl.ds(0, 3), :, 0], xr.at[1])
    send(wx.at[:, :, core], wx.at[:, :, core], xs.at[2], xr.at[2], {"wide": sibling})
    wait_halo(vd, 0)
    stencil(vd, my, ky, first, second, bands, image)

    done(wx.at[:, :, 0], xr.at[2])
    for x0, p in CHUNKS:
        wxp[64 * x0 : 64 * (x0 + p), :] = wx[:, :, :, x0 : x0 + p, :].reshape(64 * p, NX)
    for i, (x0, p) in enumerate(CHUNKS):
        done(u0.at[pl.ds(0, 63 * p)], ur0.at[i])

        @pl.when(two)
        def _(i=i, p=p):
            done(u1.at[pl.ds(0, 63 * p)], ur1.at[i])

    both = jnp.concatenate([u0[...], u1[...]], axis=1)
    spectral = dot(wxp[...], both, 0, 0)
    cols = jnp.concatenate([exc[...], exc[...]], axis=1)
    spectral = spectral / (cols + shift)
    for i, (x0, p) in enumerate(CHUNKS):
        span = slice(64 * x0, 64 * (x0 + p))
        inverse = dot(wxp[span, :], spectral, 1, 0)
        v0[span, :] = inverse[:, 0:128]
        v1[span, :] = inverse[:, 128:256]
        mine = pl.ds(64 * x0 + w * p, p)
        here = pl.ds(w * CX + x0, p)
        there = pl.ds(mine2 * CX + x0, p)

        def send_v(d, carry, i=i, x0=x0, p=p, here=here):
            v = lax.rem(w + d, NW)
            src = v0.at[pl.ds(64 * x0 + v * p, p)]
            send(src, s2.at[here], vs0.at[i], vr0.at[i], {"wide": v})
            return carry

        lax.fori_loop(1, NW, send_v, 0, unroll=3)
        own = pltpu.make_async_copy(v0.at[mine], s2.at[here], lsem.at[5])
        own.start()
        own.wait()

        @pl.when(two)
        def _(i=i, x0=x0, p=p, there=there, mine=mine):
            def send_v1(d, carry):
                v = lax.rem(w + d, NW)
                src = v1.at[pl.ds(64 * x0 + v * p, p)]
                send(src, s2.at[there], vs1.at[i], vr1.at[i], {"wide": v})
                return carry

            lax.fori_loop(1, NW, send_v1, 0, unroll=3)
            c = pltpu.make_async_copy(v1.at[mine], s2.at[there], lsem.at[6])
            c.start()
            c.wait()

    for i, (x0, p) in enumerate(CHUNKS):
        done(s2.at[pl.ds(0, 63 * p)], vr0.at[i])

        @pl.when(two)
        def _(i=i, p=p):
            done(s2.at[pl.ds(0, 35 * p)], vr1.at[i])

        @pl.when(one)
        def _(i=i, p=p):
            done(s2.at[pl.ds(0, 36 * p)], vr1.at[i])

        for x in range(x0, x0 + p):
            r = x * CY
            for j in range(2):
                t2[r : r + CY, 128 * j : 128 * j + 128] = s2[pl.ds(j * 400 + x, 40, stride=10), :]
            b = s2[pl.ds(800 + x, 20, stride=10), :]
            t2[r : r + 20, 256:320] = b[:, 0:64]
            t2[r + 20 : r + CY, 256:320] = b[:, 64:128]
        span = slice(x0 * CY, (x0 + p) * CY)
        lines[span, :] = dot(t2[span, :], wy[...], 1, 1)
        for m in range(NN):
            for x in range(p):
                r = (x0 + x) * CY
                n2s[i][m * CY : m * CY + CY, x * CY : x * CY + CY] = lines[
                    r : r + CY, m * CY : m * CY + CY
                ]
        own = pltpu.make_async_copy(n2s[i].at[rows_of(n)], n2r[i].at[rows_of(n)], lsem.at[7])
        own.start()
        for d in range(1, NN):
            v = lax.rem(n + d, NN)
            at = {"narrow": v}
            send(n2s[i].at[rows_of(v)], n2r[i].at[rows_of(n)], n2ss.at[i], n2rs.at[i], at)
        own.wait()

    for i, (x0, p) in enumerate(CHUNKS):
        done(n2r[i].at[pl.ds(0, 280)], n2rs.at[i])
        piece = dot(n2r[i][...], wz[...], 0, 1).reshape(p, CY, NZ)
        vp[3 + x0 : 3 + x0 + p, 8:48, :] = piece
    start_halo(vp, 1)
    wait_halo(vp, 1)
    stencil(vp, my, ky, first, second, bands, fresh)

    precond = vp[3:13, 8:48, :].reshape(CX * CY, NZ)
    direction = vd[3:13, 8:48, :].reshape(CX * CY, NZ)
    res2 = res[...].reshape(CX * CY, NZ)
    items = (
        total(res2, precond),
        total(precond, fresh[...]),
        total(precond, image[...]),
        total(direction, image[...]),
    )
    lane = lax.broadcasted_iota(jnp.int32, (1, 128), 1)
    row = jnp.zeros((1, 128), jnp.float32)
    for i, item in enumerate(items):
        row = jnp.where(lane == i, item, row)
    red[0] = row
    rb1[n] = row
    for d in range(1, NN):
        send(red.at[0], rb1.at[n], rs1, rr1, {"narrow": lax.rem(n + d, NN)})
    done(rb1.at[pl.ds(0, 7)], rr1)
    row = jnp.sum(rb1[...], axis=0)
    red[1] = row
    rb2[w] = row

    def send_r(d, carry):
        send(red.at[1], rb2.at[w], rs2, rr2, {"wide": lax.rem(w + d, NW)})
        return carry

    lax.fori_loop(1, NW, send_r, 0)
    done(rb2.at[pl.ds(0, 63)], rr2)
    row = jnp.sum(rb2[...], axis=0)
    now, self_term, cross, curvature = (
        jnp.sum(jnp.where(lane == i, row, 0.0), axis=1, keepdims=True) for i in range(4)
    )
    ratio = now / prev_ref[0]
    curvature = self_term + 2.0 * ratio * cross + ratio * ratio * curvature
    alpha = now / curvature
    get_sol.wait()
    sol2 = sol[...].reshape(CX * CY, NZ)
    direction = precond + ratio * direction
    new_image = fresh[...] + ratio * image[...]
    sol_out[...] = (sol2 + alpha * direction).reshape(CX, CY, NZ)
    res_out[...] = (res2 - alpha * new_image).reshape(CX, CY, NZ)
    dir_out[...] = direction.reshape(CX, CY, NZ)

    by_core(wz, zbs, 160)
    by_core(wz, zfs, 160)
    by_core(wy, ybs, 160)
    by_core(wy, yfs, 160)
    done(wx.at[0, pl.ds(0, 7), 0], xs.at[0])
    done(wx.at[pl.ds(0, 3), :, 0], xs.at[1])
    done(wx.at[:, :, 0], xs.at[2])
    drain_halo(vd, 0)
    drain_halo(vp, 1)
    for i, (x0, p) in enumerate(CHUNKS):
        done(n1s[i].at[pl.ds(0, 280)], n1ss.at[i])
        done(n2s[i].at[pl.ds(0, 280)], n2ss.at[i])
        done(s1.at[pl.ds(0, 63 * p)], us0.at[i])
        done(v0.at[pl.ds(0, 63 * p)], vs0.at[i])

        @pl.when(two)
        def _(i=i, p=p):
            done(s1.at[pl.ds(0, 35 * p)], us1.at[i])
            done(v1.at[pl.ds(0, 63 * p)], vs1.at[i])

        @pl.when(one)
        def _(i=i, p=p):
            done(s1.at[pl.ds(0, 36 * p)], us1.at[i])

    done(rb1.at[pl.ds(0, 7)], rs1)
    done(rb2.at[pl.ds(0, 63)], rs2)


def finish(sol, res, direction, sol_out, res_out, dir_out):
    sol_out[...] = sol[...]
    res_out[...] = res[...]
    dir_out[...] = direction[...]


def per_device(sol, res, direction, prev, bx, by, bz, ex, ey, ez):
    f32 = jnp.float32
    brick = jax.ShapeDtypeStruct((CX, CY, NZ), f32)
    vmem = pl.BlockSpec(memory_space=pltpu.VMEM)
    hbm = pl.BlockSpec(memory_space=pltpu.HBM)
    dma = pltpu.SemaphoreType.DMA
    shapes = [
        (CX, CY, NZ),
        (CX, CY, NZ),
        (4, 8, 2, CX, NX),
        (NZ, NZ),
        (NZ, NZ),
        (2, NZ, NZ),
        (NX, 128),
        (16, 56, NZ),
        (16, 56, NZ),
        (16, CY, NZ),
        (16, CY, NZ),
        (CX, CY, NZ),
        (CX, CY, NZ),
        (400, NZ),
        (400, NZ),
        tuple((NZ, p * CY) for _, p in CHUNKS),
        tuple((NN, CY, p * CY) for _, p in CHUNKS),
        (NX, NX),
        (400, NZ),
        (400, NZ),
        (1000, 128),
        (NX, 128),
        (NX, 128),
        (NX, 128),
        (NX, 128),
        (1000, 128),
        tuple((NZ, p * CY) for _, p in CHUNKS),
        tuple((NZ, p * CY) for _, p in CHUNKS),
        (2, 1, 128),
        (NN, 1, 128),
        (NW, 1, 128),
    ]
    sems = [(15,), (3,), (3,), (), (8,), (), (), (), (8,), (), ()]
    k = len(CHUNKS)
    sems += [(2, 8), (2, 8), (k,), (k, 8)] + [(k,)] * 10 + [()] * 4

    def space(s):
        if isinstance(s[0], tuple):
            return [pltpu.VMEM(t, f32) for t in s]
        return pltpu.VMEM(s, f32)

    far = [
        pltpu.with_memory_space_constraint(a, pltpu.HBM)
        for a in (ex, ey, ez, sol, res, direction, bx, by, bz)
    ]
    outs = pl.pallas_call(
        kernel,
        out_shape=(brick, brick, brick),
        in_specs=[pl.BlockSpec(memory_space=pltpu.SMEM)] + [hbm] * 9,
        out_specs=(vmem, vmem, vmem),
        scratch_shapes=[
            pltpu.VMEM((NX,), f32),
            pltpu.VMEM((NZ,), f32),
            pltpu.SMEM((NZ,), f32),
        ]
        + [space(s) for s in shapes]
        + [dma(s) for s in sems],
        compiler_params=pltpu.CompilerParams(
            collective_id=0, has_side_effects=True, vmem_limit_bytes=28 << 20
        ),
        name="iterate",
    )(prev, *far)
    return pl.pallas_call(
        finish,
        out_shape=(brick, brick, brick),
        in_specs=[vmem] * 3,
        out_specs=(vmem, vmem, vmem),
        compiler_params=pltpu.CompilerParams(vmem_limit_bytes=12 << 20),
        name="finish",
    )(*outs)


def solution(mesh):
    field = P("wide", "narrow", None)
    in_specs = (
        field,
        field,
        field,
        P(),
        P("wide", None),
        P("narrow", None),
        P("narrow", None),
        P(),
        P(),
        P(),
    )
    return jax.shard_map(
        per_device, mesh=mesh, in_specs=in_specs, out_specs=(field, field, field), check_vma=False
    )
```

```python
import functools

import jax
import jax.numpy as jnp
from jax import lax
from jax.experimental import pallas as pl
from jax.experimental.pallas import tpu as pltpu
from jax.sharding import PartitionSpec as P

MASS = (151.0 / 315.0, 397.0 / 1680.0, 1.0 / 42.0, 1.0 / 5040.0)
STIFF = (2.0 / 3.0, -0.125, -0.2, -1.0 / 120.0)
MESH = pl.DeviceIdType.MESH
NW, NN = 64, 8
CX, CY, NZ, NX = 10, 40, 320, 640
CHUNKS = ((0, 3), (3, 3), (6, 4))
ROWS = (40, 40, 56)


def dot(a, b, ca, cb):
    return lax.dot_general(
        a,
        b,
        (((ca,), (cb,)), ((), ())),
        precision=lax.Precision.HIGH,
        preferred_element_type=jnp.float32,
    )


def place(v):
    return lax.div(v, 16), lax.rem(lax.div(v, 8), 2), lax.rem(v, 8)


def device_of(v):
    x, core, y = place(v)
    return x * 16 + y * 2 + core


def has_second(v):
    x, core, y = place(v)
    return (core == 0) | (y == 2 * x)


def second_tile(v):
    x, core, y = place(v)
    return 64 + (1 - core) * (x * 8 + y) + core * (32 + x)


def band(coeffs):
    gap = jnp.abs(
        lax.broadcasted_iota(jnp.int32, (NZ, NZ), 0) - lax.broadcasted_iota(jnp.int32, (NZ, NZ), 1)
    )
    out = jnp.zeros((NZ, NZ), jnp.float32)
    for o in range(4):
        out = jnp.where(gap == o, coeffs[o], out)
    return out


def total(a, b):
    return jnp.sum(jnp.sum(a * b, axis=0, keepdims=True), axis=1, keepdims=True)


def along_y(padded, my, ky, start, stop):
    def step(p, carry):
        c = padded[p, 8:48, :]
        m = MASS[0] * c
        k = STIFF[0] * c
        for o in (1, 2, 3):
            s = padded[p, 8 - o : 48 - o, :] + padded[p, 8 + o : 48 + o, :]
            m += MASS[o] * s
            k += STIFF[o] * s
        my[p] = m
        ky[p] = k
        return carry

    lax.fori_loop(start, stop, step, 0)


def along_xz(my, ky, first, second, bands, out):
    def step(q, carry):
        a = my[q + 3]
        f = MASS[0] * a
        g = STIFF[0] * a + MASS[0] * ky[q + 3]
        for o in (1, 2, 3):
            s = my[q + 3 - o] + my[q + 3 + o]
            t = ky[q + 3 - o] + ky[q + 3 + o]
            f += MASS[o] * s
            g += STIFF[o] * s + MASS[o] * t
        first[q] = g
        second[q] = f
        return carry

    lax.fori_loop(0, CX, step, 0)
    g = first[...].reshape(CX * CY, NZ)
    f = second[...].reshape(CX * CY, NZ)
    out[...] = dot(g, bands[0], 1, 0) + dot(f, bands[1], 1, 0)


def pack_plane(dst, m, rows):
    dst[m, 40:56, 0:40] = rows[0:16, :]
    dst[m, 40:56, 40:80] = rows[16:32, :]
    dst[m, 40:48, 80:120] = rows[32:40, :]


def kernel(
    prev_ref,
    ex_hbm,
    ey_hbm,
    ez_hbm,
    sol_ref,
    res_ref,
    dir_ref,
    bx_ref,
    by_ref,
    bz_ref,
    sol_out,
    res_out,
    dir_out,
    ex_ref,
    ey_ref,
    ez_ref,
    sol,
    res,
    wx,
    wy,
    wz,
    bands,
    exc,
    vd,
    vp,
    my,
    ky,
    first,
    second,
    image,
    fresh,
    n1s,
    n1r,
    wxp,
    wide4,
    lines,
    t2,
    s1,
    u0,
    u1,
    v0,
    v1,
    s2,
    n2s,
    n2r,
    red,
    rb1,
    rb2,
    lsem,
    xs,
    xr,
    ybs,
    ybr,
    yfs,
    yfr,
    zbs,
    zbr,
    zfs,
    zfr,
    hs,
    hr,
    n1ss,
    n1rs,
    us0,
    us1,
    ur0,
    ur1,
    vs0,
    vs1,
    vr0,
    vr1,
    n2ss,
    n2rs,
    rs1,
    rr1,
    rs2,
    rr2,
):
    w = lax.axis_index("wide")
    n = lax.axis_index("narrow")
    wup, wdn = lax.rem(w + 1, NW), lax.rem(w + NW - 1, NW)
    nup, ndn = lax.rem(n + 1, NN), lax.rem(n + NN - 1, NN)
    core = lax.rem(w, 2)
    sibling = w + 1 - 2 * core
    gx, gy = lax.div(w, 16), lax.rem(lax.div(w, 2), 8)
    me = gx * 16 + core * 8 + gy
    barrier = pltpu.get_barrier_semaphore()
    get_res = pltpu.make_async_copy(res_ref, res, lsem.at[8])
    get_dir = pltpu.make_async_copy(dir_ref, vd.at[pl.ds(3, CX), pl.ds(8, CY)], lsem.at[9])
    get_sol = pltpu.make_async_copy(sol_ref, sol, lsem.at[10])
    small = [
        pltpu.make_async_copy(a, b, lsem.at[11 + i])
        for i, (a, b) in enumerate(
            ((ex_hbm, ex_ref), (ey_hbm, ey_ref), (ez_hbm, ez_ref))
        )
    ]
    for c in [get_res, get_dir, *small, get_sol]:
        c.start()

    for v in (vd, vp):
        for p in (0, 1, 2, 13, 14, 15):
            v[p] = jnp.zeros((56, NZ), jnp.float32)
        for p in range(3, 13):
            v[p, 0:8, :] = jnp.zeros((8, NZ), jnp.float32)
            v[p, 48:56, :] = jnp.zeros((8, NZ), jnp.float32)
    u1[...] = jnp.zeros_like(u1)

    def greet(d, carry):
        pl.semaphore_signal(
            barrier, inc=1, device_id={"wide": lax.rem(w + d, NW)}, device_id_type=MESH
        )
        return carry

    lax.fori_loop(1, NW, greet, 0)
    for d in range(1, NN):
        pl.semaphore_signal(
            barrier, inc=1, device_id={"narrow": lax.rem(n + d, NN)}, device_id_type=MESH
        )
    for a in (wup, wdn):
        for b in (nup, ndn):
            pl.semaphore_signal(
                barrier, inc=1, device_id={"wide": a, "narrow": b}, device_id_type=MESH
            )

    bands[0] = band(MASS)
    bands[1] = band(STIFF)
    for c in small:
        c.wait()
    exc[...] = jnp.transpose(jnp.broadcast_to(ex_ref[...].reshape(1, NX), (128, NX)))

    pl.semaphore_wait(barrier, NW - 1 + NN - 1 + 4)

    def send(src, dst, ssem, rsem, where):
        c = pltpu.make_async_remote_copy(
            src_ref=src,
            dst_ref=dst,
            send_sem=ssem,
            recv_sem=rsem,
            device_id=where,
            device_id_type=MESH,
        )
        c.start()

    def done(ref, sem):
        pltpu.make_async_copy(ref, ref, sem).wait()

    def near(d):
        return core == (d + 1) % 2

    def rows_of(v):
        return pl.ds(pl.multiple_of(v * CY, 8), CY)

    def share(own, whole, ssem, rsem):
        for d in range(1, NN):

            @pl.when(near(d))
            def _(d=d):
                at = {"narrow": lax.rem(n + d, NN)}
                send(own, whole.at[rows_of(n)], ssem, rsem.at[d], at)

    def hand_over(whole, rsem, fsem, gsem):
        for d in range(1, NN):

            @pl.when(near(d))
            def _(d=d):
                m = rows_of(lax.rem(n + NN - d, NN))
                done(whole.at[m], rsem.at[d])
                send(whole.at[m], whole.at[m], fsem, gsem, {"wide": sibling})

    def by_core(whole, sem, first_rows):
        @pl.when(core == 0)
        def _():
            done(whole.at[pl.ds(0, first_rows)], sem)

        @pl.when(core == 1)
        def _():
            done(whole.at[pl.ds(0, 280 - first_rows)], sem)

    ownz = pltpu.make_async_copy(bz_ref, wz.at[rows_of(n)], lsem.at[0])
    owny = pltpu.make_async_copy(by_ref, wy.at[rows_of(n)], lsem.at[1])
    rows_x = pl.ds(gy * CX, CX)
    for k in range(5):
        pltpu.make_async_copy(
            bx_ref.at[:, pl.ds(128 * k, 128)], wx.at[k, gx, core, rows_x], lsem.at[2]
        ).start()
    ownz.start()
    owny.start()
    share(bz_ref, wz, zbs, zbr)
    share(by_ref, wy, ybs, ybr)

    done(wx.at[:, gx, core, rows_x], lsem.at[2])
    for d in range(1, 8):
        at = {"wide": gx * 16 + lax.rem(gy + d, 8) * 2 + core}
        block = wx.at[:, gx, core, rows_x]
        send(block, block, xs.at[0], xr.at[0], at)

    has = {"xu": w < NW - 1, "xd": w > 0, "yu": n < NN - 1, "yd": n > 0}
    spans = {
        "": (pl.ds(3, 10), pl.ds(3, 10)),
        "xu": (pl.ds(10, 3), pl.ds(0, 3)),
        "xd": (pl.ds(3, 3), pl.ds(13, 3)),
    }
    rows = {
        "": (pl.ds(8, 40), pl.ds(8, 40)),
        "yu": (pl.ds(45, 3), pl.ds(5, 3)),
        "yd": (pl.ds(8, 3), pl.ds(48, 3)),
    }
    opposite = {"": "", "xu": "xd", "xd": "xu", "yu": "yd", "yd": "yu"}
    whole_way = [
        ("xu", "", None),
        ("xd", "", None),
        ("xu", "yu", None),
        ("xu", "yd", None),
        ("xd", "yu", None),
        ("xd", "yd", None),
        ("", "yu", (3, 10)),
        ("", "yd", (3, 10)),
    ]
    ways = {"old": whole_way}
    for i, (x0, p) in enumerate(CHUNKS):
        side = "xd" if i == 0 else "xu" if i == len(CHUNKS) - 1 else None
        ways[i, "x"] = [(side, b, None) for b in ("", "yu", "yd") if side]
        ways[i, "y"] = [("", b, (3 + x0, p)) for b in ("yu", "yd")]
    slots = {}
    for key, items in ways.items():
        if key != "old":
            for item in items:
                slots[item] = len(slots)

    def slot(key, item, j):
        return (0, j) if key == "old" else (1, slots[item])

    def exists(a, b):
        if a and b:
            return has[a] & has[b]
        return has[a or b]

    def side_of(a, planes, end):
        return pl.ds(*planes) if planes else spans[a][end]

    def start_halo(v, key):
        for j, item in enumerate(ways[key]):
            a, b, planes = item

            @pl.when(exists(a, b))
            def _(key=key, item=item, j=j, a=a, b=b, planes=planes):
                at = {}
                if a:
                    at["wide"] = wup if a == "xu" else wdn
                if b:
                    at["narrow"] = nup if b == "yu" else ndn
                send(
                    v.at[side_of(a, planes, 0), rows[b][0]],
                    v.at[side_of(a, planes, 1), rows[b][1]],
                    hs.at[slot(key, item, j)],
                    hr.at[slot(key, item, j)],
                    at,
                )

    def wait_halo(v, key):
        for j, item in enumerate(ways[key]):
            a, b, planes = item

            @pl.when(exists(opposite[a], opposite[b]))
            def _(key=key, item=item, j=j, a=a, b=b, planes=planes):
                done(v.at[side_of(a, planes, 1), rows[b][1]], hr.at[slot(key, item, j)])

    def drain_halo(v, key):
        for j, item in enumerate(ways[key]):
            a, b, planes = item

            @pl.when(exists(a, b))
            def _(key=key, item=item, j=j, a=a, b=b, planes=planes):
                done(v.at[side_of(a, planes, 0), rows[b][0]], hs.at[slot(key, item, j)])

    hand_over(wz, zbr, zfs, zfr)
    done(wx.at[:, 0, 0, pl.ds(0, 70)], xr.at[0])
    for e in range(1, 4):
        at = {"wide": lax.rem(gx + e, 4) * 16 + gy * 2 + core}
        send(wx.at[:, gx, core], wx.at[:, gx, core], xs.at[1], xr.at[1], at)

    get_res.wait()
    ownz.wait()
    by_core(wz, zfr, 120)
    for i, (x0, p) in enumerate(CHUNKS):
        flat = dot(wz[...], res[x0 : x0 + p].reshape(p * CY, NZ), 0, 1)
        n1s[i][:, 0:40, :] = flat[:, 0:120].reshape(NN, CY, 120)
        if p == 4:
            for m in range(NN):
                pack_plane(n1s[i], m, flat[m * CY : m * CY + CY, 120:160])
        pltpu.make_async_copy(n1s[i].at[n], n1r[i].at[n], n1rs.at[i, n]).start()
        for d in range(1, NN):
            v = lax.rem(n + d, NN)
            at = {"narrow": v}
            send(n1s[i].at[v], n1r[i].at[n], n1ss.at[i], n1rs.at[i, n], at)

    hand_over(wy, ybr, yfs, yfr)
    get_dir.wait()
    start_halo(vd, "old")
    mine2 = second_tile(me)
    two = has_second(me)
    one = jnp.logical_not(two)

    for i, (x0, p) in enumerate(CHUNKS):
        for m in range(NN):
            done(n1r[i].at[m], n1rs.at[i, m])
            cols = slice(m * CY, m * CY + CY)
            for x in range(3):
                r = (x0 + x) * CY
                lines[r : r + CY, cols] = n1r[i][m, 0:40, x * CY : x * CY + CY]
            if p == 4:
                r = (x0 + 3) * CY
                lines[r : r + 16, cols] = n1r[i][m, 40:56, 0:40]
                lines[r + 16 : r + 32, cols] = n1r[i][m, 40:56, 40:80]
                lines[r + 32 : r + 40, cols] = n1r[i][m, 40:48, 80:120]
        if i == 0:
            owny.wait()
            by_core(wy, yfr, 120)
        span = slice(x0 * CY, (x0 + p) * CY)
        t2[span, :] = dot(lines[span, :], wy[...], 1, 0)
        for x in range(x0, x0 + p):
            r = x * CY
            for j in range(2):
                s1[pl.ds(j * 400 + x, 40, stride=10), :] = t2[
                    r : r + CY, 128 * j : 128 * j + 128
                ]
            s1[pl.ds(800 + x, 20, stride=10), :] = jnp.concatenate(
                [t2[r : r + 20, 256:320], t2[r + 20 : r + CY, 256:320]], axis=1
            )
        here = pl.ds(64 * x0 + me * p, p)

        def send_u(d, carry, i=i, x0=x0, p=p, here=here):
            v = lax.rem(me + d, NW)
            at = {"wide": device_of(v)}
            send(s1.at[pl.ds(v * CX + x0, p)], u0.at[here], us0.at[i], ur0.at[i], at)

            @pl.when(has_second(v))
            def _():
                src = s1.at[pl.ds(second_tile(v) * CX + x0, p)]
                send(src, u1.at[here], us1.at[i], ur1.at[i], at)

            return carry

        lax.fori_loop(1, NW, send_u, 0, unroll=3)
        own = pltpu.make_async_copy(s1.at[pl.ds(me * CX + x0, p)], u0.at[here], lsem.at[3])
        own.start()
        own.wait()

        @pl.when(two)
        def _(x0=x0, p=p, here=here):
            c = pltpu.make_async_copy(
                s1.at[pl.ds(mine2 * CX + x0, p)], u1.at[here], lsem.at[4]
            )
            c.start()
            c.wait()

    ey = ey_ref[...].reshape(1, NZ)

    def shift_row(t):
        j = lax.div(t, 40)
        c = t - j * 40
        row = jnp.where(j == 0, ey[:, 0:128], ey[:, 128:256])
        tail = ey[:, 256:320]
        row = jnp.where(j == 2, jnp.concatenate([tail, tail], axis=1), row)
        late = c + 20 * lax.div(j, 2)
        low = lax.broadcasted_iota(jnp.int32, (1, 128), 1) < 64
        return row + jnp.where(low, ez_ref[n * CY + c], ez_ref[n * CY + late])

    shift = jnp.concatenate([shift_row(me), shift_row(mine2)], axis=1)
    done(wx.at[:, pl.ds(0, 3), 0], xr.at[1])
    send(wx.at[:, :, core], wx.at[:, :, core], xs.at[2], xr.at[2], {"wide": sibling})
    wait_halo(vd, "old")
    along_y(vd, my, ky, 0, CX + 6)
    along_xz(my, ky, first, second, bands, image)

    done(wx.at[:, :, 0], xr.at[2])
    for x0, p in CHUNKS:
        for x in range(p):
            for k in range(5):
                for g in range(8):
                    wxp[k, pl.ds(64 * x0 + g * 8 * p + x, 8, stride=p), :] = wx[
                        k, g // 2, g % 2, pl.ds(x0 + x, 8, stride=CX), :
                    ]
    for i, (x0, p) in enumerate(CHUNKS):
        done(u0.at[pl.ds(0, 63 * p)], ur0.at[i])

        @pl.when(two)
        def _(i=i, p=p):
            done(u1.at[pl.ds(0, 63 * p)], ur1.at[i])

    both = jnp.concatenate([u0[...], u1[...]], axis=1)
    spectral = dot(jnp.concatenate([wxp[k] for k in range(5)], axis=1), both, 0, 0)
    cols = jnp.concatenate([exc[...], exc[...]], axis=1)
    spectral = spectral / (cols + shift)
    for i, (x0, p) in enumerate(CHUNKS):
        span = slice(64 * x0, 64 * (x0 + p))
        inverse = dot(
            jnp.concatenate([wxp[k, span, :] for k in range(5)], axis=1), spectral, 1, 0
        )
        v0[span, :] = inverse[:, 0:128]
        v1[span, :] = inverse[:, 128:256]
        mine = pl.ds(64 * x0 + me * p, p)
        here = pl.ds(me * CX + x0, p)
        there = pl.ds(mine2 * CX + x0, p)

        def send_v(d, carry, i=i, x0=x0, p=p, here=here):
            v = lax.rem(me + d, NW)
            src = v0.at[pl.ds(64 * x0 + v * p, p)]
            send(src, s2.at[here], vs0.at[i], vr0.at[i], {"wide": device_of(v)})
            return carry

        lax.fori_loop(1, NW, send_v, 0, unroll=3)
        own = pltpu.make_async_copy(v0.at[mine], s2.at[here], lsem.at[5])
        own.start()
        own.wait()

        @pl.when(two)
        def _(i=i, x0=x0, p=p, there=there, mine=mine):
            def send_v1(d, carry):
                v = lax.rem(me + d, NW)
                src = v1.at[pl.ds(64 * x0 + v * p, p)]
                send(src, s2.at[there], vs1.at[i], vr1.at[i], {"wide": device_of(v)})
                return carry

            lax.fori_loop(1, NW, send_v1, 0, unroll=3)
            c = pltpu.make_async_copy(v1.at[mine], s2.at[there], lsem.at[6])
            c.start()
            c.wait()

    for i, (x0, p) in enumerate(CHUNKS):
        done(s2.at[pl.ds(0, 63 * p)], vr0.at[i])

        @pl.when(two)
        def _(i=i, p=p):
            done(s2.at[pl.ds(0, 35 * p)], vr1.at[i])

        @pl.when(one)
        def _(i=i, p=p):
            done(s2.at[pl.ds(0, 36 * p)], vr1.at[i])

        for x in range(x0, x0 + p):
            r = x * CY
            for j in range(2):
                t2[r : r + CY, 128 * j : 128 * j + 128] = s2[pl.ds(j * 400 + x, 40, stride=10), :]
            b = s2[pl.ds(800 + x, 20, stride=10), :]
            t2[r : r + 20, 256:320] = b[:, 0:64]
            t2[r + 20 : r + CY, 256:320] = b[:, 64:128]
        span = slice(x0 * CY, (x0 + p) * CY)
        lines[span, :] = dot(t2[span, :], wy[...], 1, 1)
        for m in range(NN):
            cols = slice(m * CY, m * CY + CY)
            for x in range(3):
                r = (x0 + x) * CY
                n2s[i][m, 0:40, x * CY : x * CY + CY] = lines[r : r + CY, cols]
            if p == 4:
                r = (x0 + 3) * CY
                pack_plane(n2s[i], m, lines[r : r + CY, cols])
        own = pltpu.make_async_copy(n2s[i].at[n], n2r[i].at[n], lsem.at[7])
        own.start()
        for d in range(1, NN):
            v = lax.rem(n + d, NN)
            send(n2s[i].at[v], n2r[i].at[n], n2ss.at[i], n2rs.at[i], {"narrow": v})
        own.wait()

    for i, (x0, p) in enumerate(CHUNKS):
        done(n2r[i].at[pl.ds(0, 7)], n2rs.at[i])
        flat = n2r[i][:, 0:40, :].reshape(NZ, 120)
        if p == 4:
            wide4[:, 0:120] = flat
            for m in range(NN):
                r = m * CY
                wide4[r : r + 16, 120:160] = n2r[i][m, 40:56, 0:40]
                wide4[r + 16 : r + 32, 120:160] = n2r[i][m, 40:56, 40:80]
                wide4[r + 32 : r + 40, 120:160] = n2r[i][m, 40:48, 80:120]
            flat = wide4[...]
        vp[3 + x0 : 3 + x0 + p, 8:48, :] = dot(flat, wz[...], 0, 1).reshape(p, CY, NZ)
        start_halo(vp, (i, "x"))
        start_halo(vp, (i, "y"))
        if i > 0:
            q0, q = CHUNKS[i - 1]
            wait_halo(vp, (i - 1, "y"))
            along_y(vp, my, ky, 3 + q0, 3 + q0 + q)
    last = len(CHUNKS) - 1
    wait_halo(vp, (last, "y"))
    along_y(vp, my, ky, 3 + CHUNKS[last][0], 3 + CX)
    wait_halo(vp, (last, "x"))
    along_y(vp, my, ky, 0, 3)
    wait_halo(vp, (0, "x"))
    along_y(vp, my, ky, CX + 3, CX + 6)
    along_xz(my, ky, first, second, bands, fresh)

    precond = vp[3:13, 8:48, :].reshape(CX * CY, NZ)
    direction = vd[3:13, 8:48, :].reshape(CX * CY, NZ)
    res2 = res[...].reshape(CX * CY, NZ)
    items = (
        total(res2, precond),
        total(precond, fresh[...]),
        total(precond, image[...]),
        total(direction, image[...]),
    )
    lane = lax.broadcasted_iota(jnp.int32, (1, 128), 1)
    row = jnp.zeros((1, 128), jnp.float32)
    for i, item in enumerate(items):
        row = jnp.where(lane == i, item, row)
    red[0] = row
    rb1[n] = row
    for d in range(1, NN):
        send(red.at[0], rb1.at[n], rs1, rr1, {"narrow": lax.rem(n + d, NN)})
    done(rb1.at[pl.ds(0, 7)], rr1)
    row = jnp.sum(rb1[...], axis=0)
    red[1] = row
    rb2[w] = row

    def send_r(d, carry):
        send(red.at[1], rb2.at[w], rs2, rr2, {"wide": lax.rem(w + d, NW)})
        return carry

    lax.fori_loop(1, NW, send_r, 0)
    done(rb2.at[pl.ds(0, 63)], rr2)
    row = jnp.sum(rb2[...], axis=0)
    now, self_term, cross, curvature = (
        jnp.sum(jnp.where(lane == i, row, 0.0), axis=1, keepdims=True) for i in range(4)
    )
    ratio = now / prev_ref[0]
    curvature = self_term + 2.0 * ratio * cross + ratio * ratio * curvature
    alpha = now / curvature
    get_sol.wait()
    sol2 = sol[...].reshape(CX * CY, NZ)
    direction = precond + ratio * direction
    new_image = fresh[...] + ratio * image[...]
    sol_out[...] = (sol2 + alpha * direction).reshape(CX, CY, NZ)
    res_out[...] = (res2 - alpha * new_image).reshape(CX, CY, NZ)
    dir_out[...] = direction.reshape(CX, CY, NZ)

    by_core(wz, zbs, 160)
    by_core(wz, zfs, 160)
    by_core(wy, ybs, 160)
    by_core(wy, yfs, 160)
    done(wx.at[:, 0, 0, pl.ds(0, 70)], xs.at[0])
    done(wx.at[:, pl.ds(0, 3), 0], xs.at[1])
    done(wx.at[:, :, 0], xs.at[2])
    drain_halo(vd, "old")
    for i in range(len(CHUNKS)):
        drain_halo(vp, (i, "x"))
        drain_halo(vp, (i, "y"))
    for i, (x0, p) in enumerate(CHUNKS):
        done(n1s[i].at[pl.ds(0, 7)], n1ss.at[i])
        done(n2s[i].at[pl.ds(0, 7)], n2ss.at[i])
        done(s1.at[pl.ds(0, 63 * p)], us0.at[i])
        done(v0.at[pl.ds(0, 63 * p)], vs0.at[i])

        @pl.when(two)
        def _(i=i, p=p):
            done(s1.at[pl.ds(0, 35 * p)], us1.at[i])
            done(v1.at[pl.ds(0, 63 * p)], vs1.at[i])

        @pl.when(one)
        def _(i=i, p=p):
            done(s1.at[pl.ds(0, 36 * p)], us1.at[i])

    done(rb1.at[pl.ds(0, 7)], rs1)
    done(rb2.at[pl.ds(0, 63)], rs2)


def finish(sol, res, direction, sol_out, res_out, dir_out):
    sol_out[...] = sol[...]
    res_out[...] = res[...]
    dir_out[...] = direction[...]


def per_device(sol, res, direction, prev, bx, by, bz, ex, ey, ez):
    f32 = jnp.float32
    brick = jax.ShapeDtypeStruct((CX, CY, NZ), f32)
    vmem = pl.BlockSpec(memory_space=pltpu.VMEM)
    hbm = pl.BlockSpec(memory_space=pltpu.HBM)
    dma = pltpu.SemaphoreType.DMA
    shapes = [
        (CX, CY, NZ),
        (CX, CY, NZ),
        (5, 4, 2, 80, 128),
        (NZ, NZ),
        (NZ, NZ),
        (2, NZ, NZ),
        (NX, 128),
        (16, 56, NZ),
        (16, 56, NZ),
        (16, CY, NZ),
        (16, CY, NZ),
        (CX, CY, NZ),
        (CX, CY, NZ),
        (400, NZ),
        (400, NZ),
        tuple((NN, r, 120) for r in ROWS),
        tuple((NN, r, 120) for r in ROWS),
        (5, NX, 128),
        (NZ, 160),
        (400, NZ),
        (400, NZ),
        (1000, 128),
        (NX, 128),
        (NX, 128),
        (NX, 128),
        (NX, 128),
        (1000, 128),
        tuple((NN, r, 120) for r in ROWS),
        tuple((NN, r, 120) for r in ROWS),
        (2, 1, 128),
        (NN, 1, 128),
        (NW, 1, 128),
    ]
    sems = [(15,), (3,), (3,), (), (8,), (), (), (), (8,), (), ()]
    k = len(CHUNKS)
    sems += [(2, 12), (2, 12), (k,), (k, 8)] + [(k,)] * 10 + [()] * 4

    def space(s):
        if isinstance(s[0], tuple):
            return [pltpu.VMEM(t, f32) for t in s]
        return pltpu.VMEM(s, f32)

    far = [
        pltpu.with_memory_space_constraint(a, pltpu.HBM)
        for a in (ex, ey, ez, sol, res, direction, bx, by, bz)
    ]
    outs = pl.pallas_call(
        kernel,
        out_shape=(brick, brick, brick),
        in_specs=[pl.BlockSpec(memory_space=pltpu.SMEM)] + [hbm] * 9,
        out_specs=(vmem, vmem, vmem),
        scratch_shapes=[
            pltpu.VMEM((NX,), f32),
            pltpu.VMEM((NZ,), f32),
            pltpu.SMEM((NZ,), f32),
        ]
        + [space(s) for s in shapes]
        + [dma(s) for s in sems],
        compiler_params=pltpu.CompilerParams(
            collective_id=0, has_side_effects=True, vmem_limit_bytes=28 << 20
        ),
        name="iterate",
    )(prev, *far)
    return pl.pallas_call(
        finish,
        out_shape=(brick, brick, brick),
        in_specs=[vmem] * 3,
        out_specs=(vmem, vmem, vmem),
        compiler_params=pltpu.CompilerParams(vmem_limit_bytes=12 << 20),
        name="finish",
    )(*outs)


def solution(mesh):
    field = P("wide", "narrow", None)
    in_specs = (
        field,
        field,
        field,
        P(),
        P("wide", None),
        P("narrow", None),
        P("narrow", None),
        P(),
        P(),
        P(),
    )
    return jax.shard_map(
        per_device, mesh=mesh, in_specs=in_specs, out_specs=(field, field, field), check_vma=False
    )
```

```python
import functools

import jax
import jax.numpy as jnp
from jax import lax
from jax.experimental import pallas as pl
from jax.experimental.pallas import tpu as pltpu
from jax.sharding import PartitionSpec as P

MASS = (151.0 / 315.0, 397.0 / 1680.0, 1.0 / 42.0, 1.0 / 5040.0)
STIFF = (2.0 / 3.0, -0.125, -0.2, -1.0 / 120.0)
MESH = pl.DeviceIdType.MESH
NW, NN = 64, 8
CX, CY, NZ, NX = 10, 40, 320, 640
CHUNKS = ((0, 3), (3, 3), (6, 4))
ROWS = (40, 40, 56)


def dot(a, b, ca, cb):
    return lax.dot_general(
        a,
        b,
        (((ca,), (cb,)), ((), ())),
        precision=lax.Precision.HIGH,
        preferred_element_type=jnp.float32,
    )


def place(v):
    return lax.div(v, 16), lax.rem(lax.div(v, 8), 2), lax.rem(v, 8)


def split(x):
    high = x.astype(jnp.bfloat16)
    return high, (x - high.astype(jnp.float32)).astype(jnp.bfloat16)


def dot3(a, b, ca, cb):
    def one(x, y):
        return lax.dot_general(
            x, y, (((ca,), (cb,)), ((), ())), preferred_element_type=jnp.float32
        )

    return one(a[0], b[0]) + one(a[0], b[1]) + one(a[1], b[0])


def keep(ref, x):
    ref[0], ref[1] = split(x)


def device_of(v):
    x, core, y = place(v)
    return x * 16 + y * 2 + core


def has_second(v):
    x, core, y = place(v)
    return (core == 0) | (y == 2 * x)


def first_tile(v):
    x, core, y = place(v)
    q = x * 8 + y
    return (1 - core) * 2 * q + core * (64 + q + lax.div(q + 9, 10))


def band(coeffs):
    gap = jnp.abs(
        lax.broadcasted_iota(jnp.int32, (NZ, NZ), 0) - lax.broadcasted_iota(jnp.int32, (NZ, NZ), 1)
    )
    out = jnp.zeros((NZ, NZ), jnp.float32)
    for o in range(4):
        out = jnp.where(gap == o, coeffs[o], out)
    return out


def total(a, b):
    return jnp.sum(jnp.sum(a * b, axis=0, keepdims=True), axis=1, keepdims=True)


def along_y(padded, my, ky, start, stop):
    def step(p, carry):
        c = padded[p, 8:48, :]
        m = MASS[0] * c
        k = STIFF[0] * c
        for o in (1, 2, 3):
            s = padded[p, 8 - o : 48 - o, :] + padded[p, 8 + o : 48 + o, :]
            m += MASS[o] * s
            k += STIFF[o] * s
        my[p] = m
        ky[p] = k
        return carry

    lax.fori_loop(start, stop, step, 0)


def along_xz(my, ky, first, second, bands, out):
    def step(q, carry):
        a = my[q + 3]
        f = MASS[0] * a
        g = STIFF[0] * a + MASS[0] * ky[q + 3]
        for o in (1, 2, 3):
            s = my[q + 3 - o] + my[q + 3 + o]
            t = ky[q + 3 - o] + ky[q + 3 + o]
            f += MASS[o] * s
            g += STIFF[o] * s + MASS[o] * t
        first[q] = g
        second[q] = f
        return carry

    lax.fori_loop(0, CX, step, 0)
    g = split(first[...].reshape(CX * CY, NZ))
    f = split(second[...].reshape(CX * CY, NZ))
    m, k = ((bands[i, 0], bands[i, 1]) for i in range(2))
    out[...] = dot3(g, m, 1, 0) + dot3(f, k, 1, 0)


def pack_plane(dst, m, rows):
    dst[m, 40:56, 0:40] = rows[0:16, :]
    dst[m, 40:56, 40:80] = rows[16:32, :]
    dst[m, 40:48, 80:120] = rows[32:40, :]


def kernel(
    prev_ref,
    ex_hbm,
    ey_hbm,
    ez_hbm,
    sol_ref,
    res_ref,
    dir_ref,
    bx_ref,
    by_ref,
    bz_ref,
    sol_out,
    res_out,
    dir_out,
    ex_ref,
    ey_ref,
    ez_ref,
    sol,
    res,
    wx,
    wy,
    wz,
    bands,
    exc,
    vd,
    vp,
    my,
    ky,
    first,
    second,
    image,
    fresh,
    n1s,
    n1r,
    wxp,
    wide4,
    wxr,
    wxc,
    wyr,
    wyc,
    wzc,
    lines,
    t2,
    s1,
    ub,
    vb,
    s2,
    n2s,
    n2r,
    red,
    rb1,
    rb2,
    lsem,
    xs,
    xr,
    ybs,
    ybr,
    yfs,
    yfr,
    zbs,
    zbr,
    zfs,
    zfr,
    hs,
    hr,
    n1ss,
    n1rs,
    us,
    ur,
    vs,
    vr,
    n2ss,
    n2rs,
    rs1,
    rr1,
    rs2,
    rr2,
):
    w = lax.axis_index("wide")
    n = lax.axis_index("narrow")
    wup, wdn = lax.rem(w + 1, NW), lax.rem(w + NW - 1, NW)
    nup, ndn = lax.rem(n + 1, NN), lax.rem(n + NN - 1, NN)
    core = lax.rem(w, 2)
    sibling = w + 1 - 2 * core
    gx, gy = lax.div(w, 16), lax.rem(lax.div(w, 2), 8)
    me = gx * 16 + core * 8 + gy
    barrier = pltpu.get_barrier_semaphore()
    get_res = pltpu.make_async_copy(res_ref, res, lsem.at[8])
    get_dir = pltpu.make_async_copy(dir_ref, vd.at[pl.ds(3, CX), pl.ds(8, CY)], lsem.at[9])
    get_sol = pltpu.make_async_copy(sol_ref, sol, lsem.at[10])
    small = [
        pltpu.make_async_copy(a, b, lsem.at[11 + i])
        for i, (a, b) in enumerate(
            ((ex_hbm, ex_ref), (ey_hbm, ey_ref), (ez_hbm, ez_ref))
        )
    ]
    for c in [get_res, get_dir, *small, get_sol]:
        c.start()

    for v in (vd, vp):
        for p in (0, 1, 2, 13, 14, 15):
            v[p] = jnp.zeros((56, NZ), jnp.float32)
        for p in range(3, 13):
            v[p, 0:8, :] = jnp.zeros((8, NZ), jnp.float32)
            v[p, 48:56, :] = jnp.zeros((8, NZ), jnp.float32)
    ub[...] = jnp.zeros_like(ub)

    def greet(d, carry):
        pl.semaphore_signal(
            barrier, inc=1, device_id={"wide": lax.rem(w + d, NW)}, device_id_type=MESH
        )
        return carry

    lax.fori_loop(1, NW, greet, 0)
    for d in range(1, NN):
        pl.semaphore_signal(
            barrier, inc=1, device_id={"narrow": lax.rem(n + d, NN)}, device_id_type=MESH
        )
    for a in (wup, wdn):
        for b in (nup, ndn):
            pl.semaphore_signal(
                barrier, inc=1, device_id={"wide": a, "narrow": b}, device_id_type=MESH
            )

    keep(bands.at[0], band(MASS))
    keep(bands.at[1], band(STIFF))
    for c in small:
        c.wait()
    exc[...] = jnp.transpose(jnp.broadcast_to(ex_ref[...].reshape(1, NX), (128, NX)))

    pl.semaphore_wait(barrier, NW - 1 + NN - 1 + 4)

    def send(src, dst, ssem, rsem, where):
        c = pltpu.make_async_remote_copy(
            src_ref=src,
            dst_ref=dst,
            send_sem=ssem,
            recv_sem=rsem,
            device_id=where,
            device_id_type=MESH,
        )
        c.start()

    def done(ref, sem):
        pltpu.make_async_copy(ref, ref, sem).wait()

    def near(d):
        return core == (d + 1) % 2

    def rows_of(v):
        return pl.ds(pl.multiple_of(v * CY, 8), CY)

    def share(own, whole, ssem, rsem):
        for d in range(1, NN):

            @pl.when(near(d))
            def _(d=d):
                at = {"narrow": lax.rem(n + d, NN)}
                send(own, whole.at[rows_of(n)], ssem, rsem.at[d], at)

    def hand_over(whole, rsem, fsem, gsem):
        for d in range(1, NN):

            @pl.when(near(d))
            def _(d=d):
                m = rows_of(lax.rem(n + NN - d, NN))
                done(whole.at[m], rsem.at[d])
                send(whole.at[m], whole.at[m], fsem, gsem, {"wide": sibling})

    def by_core(whole, sem, first_rows):
        @pl.when(core == 0)
        def _():
            done(whole.at[pl.ds(0, first_rows)], sem)

        @pl.when(core == 1)
        def _():
            done(whole.at[pl.ds(0, 280 - first_rows)], sem)

    ownz = pltpu.make_async_copy(bz_ref, wz.at[rows_of(n)], lsem.at[0])
    owny = pltpu.make_async_copy(by_ref, wy.at[rows_of(n)], lsem.at[1])
    rows_x = pl.ds(gy * CX, CX)
    for k in range(5):
        pltpu.make_async_copy(
            bx_ref.at[:, pl.ds(128 * k, 128)], wx.at[k, gx, core, rows_x], lsem.at[2]
        ).start()
    ownz.start()
    owny.start()
    share(bz_ref, wz, zbs, zbr)
    share(by_ref, wy, ybs, ybr)

    done(wx.at[:, gx, core, rows_x], lsem.at[2])
    for d in range(1, 8):
        at = {"wide": gx * 16 + lax.rem(gy + d, 8) * 2 + core}
        block = wx.at[:, gx, core, rows_x]
        send(block, block, xs.at[0], xr.at[0], at)

    has = {"xu": w < NW - 1, "xd": w > 0, "yu": n < NN - 1, "yd": n > 0}
    spans = {
        "": (pl.ds(3, 10), pl.ds(3, 10)),
        "xu": (pl.ds(10, 3), pl.ds(0, 3)),
        "xd": (pl.ds(3, 3), pl.ds(13, 3)),
    }
    rows = {
        "": (pl.ds(8, 40), pl.ds(8, 40)),
        "yu": (pl.ds(45, 3), pl.ds(5, 3)),
        "yd": (pl.ds(8, 3), pl.ds(48, 3)),
    }
    opposite = {"": "", "xu": "xd", "xd": "xu", "yu": "yd", "yd": "yu"}
    whole_way = [
        ("xu", "", None),
        ("xd", "", None),
        ("xu", "yu", None),
        ("xu", "yd", None),
        ("xd", "yu", None),
        ("xd", "yd", None),
        ("", "yu", (3, 10)),
        ("", "yd", (3, 10)),
    ]
    ways = {"old": whole_way}
    for i, (x0, p) in enumerate(CHUNKS):
        side = "xd" if i == 0 else "xu" if i == len(CHUNKS) - 1 else None
        ways[i, "x"] = [(side, b, None) for b in ("", "yu", "yd") if side]
        ways[i, "y"] = [("", b, (3 + x0, p)) for b in ("yu", "yd")]
    slots = {}
    for key, items in ways.items():
        if key != "old":
            for item in items:
                slots[item] = len(slots)

    def slot(key, item, j):
        return (0, j) if key == "old" else (1, slots[item])

    def exists(a, b):
        if a and b:
            return has[a] & has[b]
        return has[a or b]

    def side_of(a, planes, end):
        return pl.ds(*planes) if planes else spans[a][end]

    def start_halo(v, key):
        for j, item in enumerate(ways[key]):
            a, b, planes = item

            @pl.when(exists(a, b))
            def _(key=key, item=item, j=j, a=a, b=b, planes=planes):
                at = {}
                if a:
                    at["wide"] = wup if a == "xu" else wdn
                if b:
                    at["narrow"] = nup if b == "yu" else ndn
                send(
                    v.at[side_of(a, planes, 0), rows[b][0]],
                    v.at[side_of(a, planes, 1), rows[b][1]],
                    hs.at[slot(key, item, j)],
                    hr.at[slot(key, item, j)],
                    at,
                )

    def wait_halo(v, key):
        for j, item in enumerate(ways[key]):
            a, b, planes = item

            @pl.when(exists(opposite[a], opposite[b]))
            def _(key=key, item=item, j=j, a=a, b=b, planes=planes):
                done(v.at[side_of(a, planes, 1), rows[b][1]], hr.at[slot(key, item, j)])

    def drain_halo(v, key):
        for j, item in enumerate(ways[key]):
            a, b, planes = item

            @pl.when(exists(a, b))
            def _(key=key, item=item, j=j, a=a, b=b, planes=planes):
                done(v.at[side_of(a, planes, 0), rows[b][0]], hs.at[slot(key, item, j)])

    hand_over(wz, zbr, zfs, zfr)
    done(wx.at[:, 0, 0, pl.ds(0, 70)], xr.at[0])
    for e in range(1, 4):
        at = {"wide": lax.rem(gx + e, 4) * 16 + gy * 2 + core}
        send(wx.at[:, gx, core], wx.at[:, gx, core], xs.at[1], xr.at[1], at)

    get_res.wait()
    ownz.wait()
    by_core(wz, zfr, 120)
    for i, (x0, p) in enumerate(CHUNKS):
        flat = dot(wz[...], res[x0 : x0 + p].reshape(p * CY, NZ), 0, 1)
        n1s[i][:, 0:40, :] = flat[:, 0:120].reshape(NN, CY, 120)
        if p == 4:
            for m in range(NN):
                pack_plane(n1s[i], m, flat[m * CY : m * CY + CY, 120:160])
        pltpu.make_async_copy(n1s[i].at[n], n1r[i].at[n], n1rs.at[i, n]).start()
        for d in range(1, NN):
            v = lax.rem(n + d, NN)
            at = {"narrow": v}
            send(n1s[i].at[v], n1r[i].at[n], n1ss.at[i], n1rs.at[i, n], at)

    hand_over(wy, ybr, yfs, yfr)
    get_dir.wait()
    start_halo(vd, "old")
    tile = first_tile(me)
    two = has_second(me)
    one = jnp.logical_not(two)

    owny.wait()
    by_core(wy, yfr, 120)
    keep(wyr, wy[...])

    for i, (x0, p) in enumerate(CHUNKS):
        for m in range(NN):
            done(n1r[i].at[m], n1rs.at[i, m])
            cols = slice(m * CY, m * CY + CY)
            for x in range(3):
                r = (x0 + x) * CY
                lines[r : r + CY, cols] = n1r[i][m, 0:40, x * CY : x * CY + CY]
            if p == 4:
                r = (x0 + 3) * CY
                lines[r : r + 16, cols] = n1r[i][m, 40:56, 0:40]
                lines[r + 16 : r + 32, cols] = n1r[i][m, 40:56, 40:80]
                lines[r + 32 : r + 40, cols] = n1r[i][m, 40:48, 80:120]
        span = slice(x0 * CY, (x0 + p) * CY)
        t2[span, :] = dot3(split(lines[span, :]), (wyr[0], wyr[1]), 1, 0)
        for x in range(p):
            r = (x0 + x) * CY
            at = 100 * x0 + x
            for j in range(2):
                s1[pl.ds(at + j * 40 * p, 40, stride=p), :] = t2[
                    r : r + CY, 128 * j : 128 * j + 128
                ]
            s1[pl.ds(at + 80 * p, 20, stride=p), :] = jnp.concatenate(
                [t2[r : r + 20, 256:320], t2[r + 20 : r + CY, 256:320]], axis=1
            )

        def send_u(d, carry, i=i, x0=x0, p=p):
            v = lax.rem(me + d, NW)
            at = {"wide": device_of(v)}
            src, dst = 100 * x0 + first_tile(v) * p, 128 * x0 + me * 2 * p
            double = has_second(v)

            @pl.when(double)
            def _():
                send(s1.at[pl.ds(src, 2 * p)], ub.at[pl.ds(dst, 2 * p)], us.at[i], ur.at[i], at)

            @pl.when(jnp.logical_not(double))
            def _():
                send(s1.at[pl.ds(src, p)], ub.at[pl.ds(dst, p)], us.at[i], ur.at[i], at)

            return carry

        lax.fori_loop(1, NW, send_u, 0, unroll=3)

        def keep_u(size, x0=x0, p=p):
            c = pltpu.make_async_copy(
                s1.at[pl.ds(100 * x0 + tile * p, size)],
                ub.at[pl.ds(128 * x0 + me * 2 * p, size)],
                lsem.at[3],
            )
            c.start()
            c.wait()

        @pl.when(two)
        def _(p=p, keep_u=keep_u):
            keep_u(2 * p)

        @pl.when(one)
        def _(p=p, keep_u=keep_u):
            keep_u(p)

    ey = ey_ref[...].reshape(1, NZ)

    def shift_row(t):
        j = lax.div(t, 40)
        c = t - j * 40
        row = jnp.where(j == 0, ey[:, 0:128], ey[:, 128:256])
        tail = ey[:, 256:320]
        row = jnp.where(j == 2, jnp.concatenate([tail, tail], axis=1), row)
        late = c + 20 * lax.div(j, 2)
        low = lax.broadcasted_iota(jnp.int32, (1, 128), 1) < 64
        return row + jnp.where(low, ez_ref[n * CY + c], ez_ref[n * CY + late])

    shift = jnp.concatenate([shift_row(tile), shift_row(jnp.minimum(tile + 1, 99))], axis=1)
    done(wx.at[:, pl.ds(0, 3), 0], xr.at[1])
    send(wx.at[:, :, core], wx.at[:, :, core], xs.at[2], xr.at[2], {"wide": sibling})
    wait_halo(vd, "old")
    along_y(vd, my, ky, 0, CX + 6)
    along_xz(my, ky, first, second, bands, image)

    done(wx.at[:, :, 0], xr.at[2])
    for k in range(5):
        for x in range(CX):
            for g in range(8):
                wxp[k, x * 64 + g * 8 : x * 64 + g * 8 + 8, :] = wx[
                    k, g // 2, g % 2, pl.ds(x, 8, stride=CX), :
                ]
        cols = slice(128 * k, 128 * k + 128)
        wxr[0, :, cols], wxr[1, :, cols] = split(wxp[k])
        wxc[0, cols, :], wxc[1, cols, :] = split(jnp.transpose(wxp[k]))
    keep(wyc, jnp.transpose(wy[...]))
    keep(wzc, jnp.transpose(wz[...]))
    for i, (x0, p) in enumerate(CHUNKS):

        @pl.when(two)
        def _(i=i, p=p):
            done(ub.at[pl.ds(0, 126 * p)], ur.at[i])

        @pl.when(one)
        def _(i=i, p=p):
            done(ub.at[pl.ds(0, 63 * p)], ur.at[i])

    both = jnp.concatenate(
        [
            jnp.concatenate(
                [
                    ub[pl.ds(128 * x0 + k * p + x, 64, stride=2 * p), :]
                    for x0, p in CHUNKS
                    for x in range(p)
                ],
                axis=0,
            )
            for k in range(2)
        ],
        axis=1,
    )
    spectral = dot3((wxc[0], wxc[1]), split(both), 1, 0)
    cols = jnp.concatenate([exc[...], exc[...]], axis=1)
    spectral = split(spectral / (cols + shift))
    for i, (x0, p) in enumerate(CHUNKS):
        span = slice(64 * x0, 64 * (x0 + p))
        inverse = dot3((wxr[0, span, :], wxr[1, span, :]), spectral, 1, 0)
        for x in range(p):
            for k in range(2):
                vb[pl.ds(128 * x0 + k * p + x, 64, stride=2 * p), :] = inverse[
                    x * 64 : x * 64 + 64, 128 * k : 128 * k + 128
                ]

        def back(size, i=i, x0=x0, p=p):
            here = pl.ds(100 * x0 + tile * p, size)

            def send_v(d, carry):
                v = lax.rem(me + d, NW)
                src = vb.at[pl.ds(128 * x0 + v * 2 * p, size)]
                send(src, s2.at[here], vs.at[i], vr.at[i], {"wide": device_of(v)})
                return carry

            lax.fori_loop(1, NW, send_v, 0, unroll=3)
            c = pltpu.make_async_copy(
                vb.at[pl.ds(128 * x0 + me * 2 * p, size)], s2.at[here], lsem.at[5]
            )
            c.start()
            c.wait()

        @pl.when(two)
        def _(p=p, back=back):
            back(2 * p)

        @pl.when(one)
        def _(p=p, back=back):
            back(p)

    for i, (x0, p) in enumerate(CHUNKS):
        @pl.when(two)
        def _(i=i, p=p):
            done(s2.at[pl.ds(0, 98 * p)], vr.at[i])

        @pl.when(one)
        def _(i=i, p=p):
            done(s2.at[pl.ds(0, 99 * p)], vr.at[i])

        for x in range(p):
            r = (x0 + x) * CY
            at = 100 * x0 + x
            for j in range(2):
                t2[r : r + CY, 128 * j : 128 * j + 128] = s2[
                    pl.ds(at + j * 40 * p, 40, stride=p), :
                ]
            b = s2[pl.ds(at + 80 * p, 20, stride=p), :]
            t2[r : r + 20, 256:320] = b[:, 0:64]
            t2[r + 20 : r + CY, 256:320] = b[:, 64:128]
        span = slice(x0 * CY, (x0 + p) * CY)
        lines[span, :] = dot3(split(t2[span, :]), (wyc[0], wyc[1]), 1, 0)
        for m in range(NN):
            cols = slice(m * CY, m * CY + CY)
            for x in range(3):
                r = (x0 + x) * CY
                n2s[i][m, 0:40, x * CY : x * CY + CY] = lines[r : r + CY, cols]
            if p == 4:
                r = (x0 + 3) * CY
                pack_plane(n2s[i], m, lines[r : r + CY, cols])
        own = pltpu.make_async_copy(n2s[i].at[n], n2r[i].at[n], lsem.at[7])
        own.start()
        for d in range(1, NN):
            v = lax.rem(n + d, NN)
            send(n2s[i].at[v], n2r[i].at[n], n2ss.at[i], n2rs.at[i], {"narrow": v})
        own.wait()

    for i, (x0, p) in enumerate(CHUNKS):
        done(n2r[i].at[pl.ds(0, 7)], n2rs.at[i])
        flat = n2r[i][:, 0:40, :].reshape(NZ, 120)
        if p == 4:
            wide4[:, 0:120] = flat
            for m in range(NN):
                r = m * CY
                wide4[r : r + 16, 120:160] = n2r[i][m, 40:56, 0:40]
                wide4[r + 16 : r + 32, 120:160] = n2r[i][m, 40:56, 40:80]
                wide4[r + 32 : r + 40, 120:160] = n2r[i][m, 40:48, 80:120]
            flat = wide4[...]
        vp[3 + x0 : 3 + x0 + p, 8:48, :] = dot3(
            split(jnp.transpose(flat)), (wzc[0], wzc[1]), 1, 0
        ).reshape(p, CY, NZ)
        start_halo(vp, (i, "x"))
        start_halo(vp, (i, "y"))
        if i > 0:
            q0, q = CHUNKS[i - 1]
            wait_halo(vp, (i - 1, "y"))
            along_y(vp, my, ky, 3 + q0, 3 + q0 + q)
    last = len(CHUNKS) - 1
    wait_halo(vp, (last, "y"))
    along_y(vp, my, ky, 3 + CHUNKS[last][0], 3 + CX)
    wait_halo(vp, (last, "x"))
    along_y(vp, my, ky, 0, 3)
    wait_halo(vp, (0, "x"))
    along_y(vp, my, ky, CX + 3, CX + 6)
    along_xz(my, ky, first, second, bands, fresh)

    precond = vp[3:13, 8:48, :].reshape(CX * CY, NZ)
    direction = vd[3:13, 8:48, :].reshape(CX * CY, NZ)
    res2 = res[...].reshape(CX * CY, NZ)
    items = (
        total(res2, precond),
        total(precond, fresh[...]),
        total(precond, image[...]),
        total(direction, image[...]),
    )
    lane = lax.broadcasted_iota(jnp.int32, (1, 128), 1)
    row = jnp.zeros((1, 128), jnp.float32)
    for i, item in enumerate(items):
        row = jnp.where(lane == i, item, row)
    red[0] = row
    rb1[n] = row
    for d in range(1, NN):
        send(red.at[0], rb1.at[n], rs1, rr1, {"narrow": lax.rem(n + d, NN)})
    done(rb1.at[pl.ds(0, 7)], rr1)
    row = jnp.sum(rb1[...], axis=0)
    red[1] = row
    rb2[w] = row

    def send_r(d, carry):
        send(red.at[1], rb2.at[w], rs2, rr2, {"wide": lax.rem(w + d, NW)})
        return carry

    lax.fori_loop(1, NW, send_r, 0)
    done(rb2.at[pl.ds(0, 63)], rr2)
    row = jnp.sum(rb2[...], axis=0)
    now, self_term, cross, curvature = (
        jnp.sum(jnp.where(lane == i, row, 0.0), axis=1, keepdims=True) for i in range(4)
    )
    ratio = now / prev_ref[0]
    curvature = self_term + 2.0 * ratio * cross + ratio * ratio * curvature
    alpha = now / curvature
    get_sol.wait()
    sol2 = sol[...].reshape(CX * CY, NZ)
    direction = precond + ratio * direction
    new_image = fresh[...] + ratio * image[...]
    sol_out[...] = (sol2 + alpha * direction).reshape(CX, CY, NZ)
    res_out[...] = (res2 - alpha * new_image).reshape(CX, CY, NZ)
    dir_out[...] = direction.reshape(CX, CY, NZ)

    by_core(wz, zbs, 160)
    by_core(wz, zfs, 160)
    by_core(wy, ybs, 160)
    by_core(wy, yfs, 160)
    done(wx.at[:, 0, 0, pl.ds(0, 70)], xs.at[0])
    done(wx.at[:, pl.ds(0, 3), 0], xs.at[1])
    done(wx.at[:, :, 0], xs.at[2])
    drain_halo(vd, "old")
    for i in range(len(CHUNKS)):
        drain_halo(vp, (i, "x"))
        drain_halo(vp, (i, "y"))
    for i, (x0, p) in enumerate(CHUNKS):
        done(n1s[i].at[pl.ds(0, 7)], n1ss.at[i])
        done(n2s[i].at[pl.ds(0, 7)], n2ss.at[i])

        @pl.when(two)
        def _(i=i, p=p):
            done(s1.at[pl.ds(0, 98 * p)], us.at[i])
            done(vb.at[pl.ds(0, 126 * p)], vs.at[i])

        @pl.when(one)
        def _(i=i, p=p):
            done(s1.at[pl.ds(0, 99 * p)], us.at[i])
            done(vb.at[pl.ds(0, 63 * p)], vs.at[i])

    done(rb1.at[pl.ds(0, 7)], rs1)
    done(rb2.at[pl.ds(0, 63)], rs2)


def finish(sol, res, direction, sol_out, res_out, dir_out):
    sol_out[...] = sol[...]
    res_out[...] = res[...]
    dir_out[...] = direction[...]


def per_device(sol, res, direction, prev, bx, by, bz, ex, ey, ez):
    f32 = jnp.float32
    brick = jax.ShapeDtypeStruct((CX, CY, NZ), f32)
    vmem = pl.BlockSpec(memory_space=pltpu.VMEM)
    hbm = pl.BlockSpec(memory_space=pltpu.HBM)
    dma = pltpu.SemaphoreType.DMA
    shapes = [
        (CX, CY, NZ),
        (CX, CY, NZ),
        (5, 4, 2, 80, 128),
        (NZ, NZ),
        (NZ, NZ),
        [2, 2, NZ, NZ],
        (NX, 128),
        (16, 56, NZ),
        (16, 56, NZ),
        (16, CY, NZ),
        (16, CY, NZ),
        (CX, CY, NZ),
        (CX, CY, NZ),
        (400, NZ),
        (400, NZ),
        tuple((NN, r, 120) for r in ROWS),
        tuple((NN, r, 120) for r in ROWS),
        (5, NX, 128),
        (NZ, 160),
        [2, NX, NX],
        [2, NX, NX],
        [2, NZ, NZ],
        [2, NZ, NZ],
        [2, NZ, NZ],
        (400, NZ),
        (400, NZ),
        (1000, 128),
        (2 * NX, 128),
        (2 * NX, 128),
        (1000, 128),
        tuple((NN, r, 120) for r in ROWS),
        tuple((NN, r, 120) for r in ROWS),
        (2, 1, 128),
        (NN, 1, 128),
        (NW, 1, 128),
    ]
    sems = [(15,), (3,), (3,), (), (8,), (), (), (), (8,), (), ()]
    k = len(CHUNKS)
    sems += [(2, 12), (2, 12), (k,), (k, 8)] + [(k,)] * 6 + [()] * 4

    def space(s):
        if isinstance(s[0], tuple):
            return [pltpu.VMEM(t, f32) for t in s]
        return pltpu.VMEM(tuple(s), jnp.bfloat16 if isinstance(s, list) else f32)

    far = [
        pltpu.with_memory_space_constraint(a, pltpu.HBM)
        for a in (ex, ey, ez, sol, res, direction, bx, by, bz)
    ]
    outs = pl.pallas_call(
        kernel,
        out_shape=(brick, brick, brick),
        in_specs=[pl.BlockSpec(memory_space=pltpu.SMEM)] + [hbm] * 9,
        out_specs=(vmem, vmem, vmem),
        scratch_shapes=[
            pltpu.VMEM((NX,), f32),
            pltpu.VMEM((NZ,), f32),
            pltpu.SMEM((NZ,), f32),
        ]
        + [space(s) for s in shapes]
        + [dma(s) for s in sems],
        compiler_params=pltpu.CompilerParams(
            collective_id=0, has_side_effects=True, vmem_limit_bytes=28 << 20
        ),
        name="iterate",
    )(prev, *far)
    return pl.pallas_call(
        finish,
        out_shape=(brick, brick, brick),
        in_specs=[vmem] * 3,
        out_specs=(vmem, vmem, vmem),
        compiler_params=pltpu.CompilerParams(vmem_limit_bytes=12 << 20),
        name="finish",
    )(*outs)


def solution(mesh):
    field = P("wide", "narrow", None)
    in_specs = (
        field,
        field,
        field,
        P(),
        P("wide", None),
        P("narrow", None),
        P("narrow", None),
        P(),
        P(),
        P(),
    )
    return jax.shard_map(
        per_device, mesh=mesh, in_specs=in_specs, out_specs=(field, field, field), check_vma=False
    )
```

```python
import functools

import jax
import jax.numpy as jnp
from jax import lax
from jax.experimental import pallas as pl
from jax.experimental.pallas import tpu as pltpu
from jax.sharding import PartitionSpec as P

MASS = (151.0 / 315.0, 397.0 / 1680.0, 1.0 / 42.0, 1.0 / 5040.0)
STIFF = (2.0 / 3.0, -0.125, -0.2, -1.0 / 120.0)
MESH = pl.DeviceIdType.MESH
NW, NN = 64, 8
CX, CY, NZ, NX = 10, 40, 320, 640
CHUNKS = ((0, 3), (6, 4), (3, 3))
ROWS = (40, 56, 40)
FAR = (4, 3, 5, 2, 6, 1, 7)


def dot(a, b, ca, cb):
    return lax.dot_general(
        a,
        b,
        (((ca,), (cb,)), ((), ())),
        precision=lax.Precision.HIGH,
        preferred_element_type=jnp.float32,
    )


def split(x):
    high = x.astype(jnp.bfloat16)
    return high, (x - high.astype(jnp.float32)).astype(jnp.bfloat16)


def dot3(a, b, ca, cb):
    def one(x, y):
        return lax.dot_general(
            x, y, (((ca,), (cb,)), ((), ())), preferred_element_type=jnp.float32
        )

    return one(a[0], b[0]) + one(a[0], b[1]) + one(a[1], b[0])


def keep(ref, x):
    ref[0], ref[1] = split(x)


def has_second(x, core, y):
    return (core == 0) | (y == 2 * x)


def first_tile(x, core, y):
    q = x * 8 + y
    return (1 - core) * 2 * q + core * (64 + q + x + jnp.where(y > 2 * x, 1, 0))


def band(coeffs):
    gap = jnp.abs(
        lax.broadcasted_iota(jnp.int32, (NZ, NZ), 0) - lax.broadcasted_iota(jnp.int32, (NZ, NZ), 1)
    )
    out = jnp.zeros((NZ, NZ), jnp.float32)
    for o in range(4):
        out = jnp.where(gap == o, coeffs[o], out)
    return out


def total(a, b):
    return jnp.sum(jnp.sum(a * b, axis=0, keepdims=True), axis=1, keepdims=True)


def along_y(padded, my, ky, start, stop):
    def step(p, carry):
        c = padded[p, 8:48, :]
        m = MASS[0] * c
        k = STIFF[0] * c
        for o in (1, 2, 3):
            s = padded[p, 8 - o : 48 - o, :] + padded[p, 8 + o : 48 + o, :]
            m += MASS[o] * s
            k += STIFF[o] * s
        my[p] = m
        ky[p] = k
        return carry

    lax.fori_loop(start, stop, step, 0)


def along_xz(my, ky, first, second, bands, out):
    def step(q, carry):
        a = my[q + 3]
        f = MASS[0] * a
        g = STIFF[0] * a + MASS[0] * ky[q + 3]
        for o in (1, 2, 3):
            s = my[q + 3 - o] + my[q + 3 + o]
            t = ky[q + 3 - o] + ky[q + 3 + o]
            f += MASS[o] * s
            g += STIFF[o] * s + MASS[o] * t
        first[q] = g
        second[q] = f
        return carry

    lax.fori_loop(0, CX, step, 0)
    g = split(first[...].reshape(CX * CY, NZ))
    f = split(second[...].reshape(CX * CY, NZ))
    m, k = ((bands[i, 0], bands[i, 1]) for i in range(2))
    out[...] = dot3(g, m, 1, 0) + dot3(f, k, 1, 0)


def pack_plane(dst, m, rows):
    dst[m, 40:56, 0:40] = rows[0:16, :]
    dst[m, 40:56, 40:80] = rows[16:32, :]
    dst[m, 40:48, 80:120] = rows[32:40, :]


def kernel(
    prev_ref,
    ex_hbm,
    ey_hbm,
    ez_hbm,
    sol_ref,
    res_ref,
    dir_ref,
    bx_ref,
    by_ref,
    bz_ref,
    sol_out,
    res_out,
    dir_out,
    ex_ref,
    ey_ref,
    ez_ref,
    sol,
    res,
    wx,
    wy,
    wz,
    bands,
    exc,
    vd,
    vp,
    my,
    ky,
    first,
    second,
    image,
    fresh,
    n1s,
    n1r,
    wxp,
    wide4,
    wxr,
    wxc,
    wyr,
    wyc,
    wzc,
    lines,
    t2,
    s1,
    ub,
    vb,
    s2,
    n2s,
    n2r,
    red,
    rb1,
    rb2,
    lsem,
    xs,
    xr,
    ybs,
    ybr,
    yfs,
    yfr,
    zbs,
    zbr,
    zfs,
    zfr,
    hs,
    hr,
    n1ss,
    n1rs,
    us,
    ur,
    vs,
    vr,
    n2ss,
    n2rs,
    rs1,
    rr1,
    rs2,
    rr2,
):
    w = lax.axis_index("wide")
    n = lax.axis_index("narrow")
    wup, wdn = lax.rem(w + 1, NW), lax.rem(w + NW - 1, NW)
    nup, ndn = lax.rem(n + 1, NN), lax.rem(n + NN - 1, NN)
    core = lax.rem(w, 2)
    sibling = w + 1 - 2 * core
    gx, gy = lax.div(w, 16), lax.rem(lax.div(w, 2), 8)
    me = gx * 16 + core * 8 + gy
    barrier = pltpu.get_barrier_semaphore()
    lines_x = [lax.rem(gx + e, 4) for e in range(4)]
    cores = [core, 1 - core]

    def each_wide(fn):
        def ring(k, carry):
            y = lax.rem(gy + 4 + lax.div(k + 1, 2) * (1 - 2 * lax.rem(k, 2)), 8)
            for e in (2, 1, 3, 0):
                for c in (1, 0):
                    fn(lines_x[e], cores[c], y)
            return carry

        lax.fori_loop(0, 7, ring, 0)
        for e in (2, 1, 3, 0):
            for c in (1, 0):
                if e or c:
                    fn(lines_x[e], cores[c], gy)

    def device(x, c, y):
        return {"wide": x * 16 + y * 2 + c}

    get_res = pltpu.make_async_copy(res_ref, res, lsem.at[8])
    get_dir = pltpu.make_async_copy(dir_ref, vd.at[pl.ds(3, CX), pl.ds(8, CY)], lsem.at[9])
    get_sol = pltpu.make_async_copy(sol_ref, sol, lsem.at[10])
    small = [
        pltpu.make_async_copy(a, b, lsem.at[11 + i])
        for i, (a, b) in enumerate(
            ((ex_hbm, ex_ref), (ey_hbm, ey_ref), (ez_hbm, ez_ref))
        )
    ]
    for c in [get_res, get_dir, *small, get_sol]:
        c.start()

    for v in (vd, vp):
        for p in (0, 1, 2, 13, 14, 15):
            v[p] = jnp.zeros((56, NZ), jnp.float32)
        for p in range(3, 13):
            v[p, 0:8, :] = jnp.zeros((8, NZ), jnp.float32)
            v[p, 48:56, :] = jnp.zeros((8, NZ), jnp.float32)
    ub[...] = jnp.zeros_like(ub)

    def greet(x, c, y):
        pl.semaphore_signal(barrier, inc=1, device_id=device(x, c, y), device_id_type=MESH)

    each_wide(greet)
    for d in FAR:
        pl.semaphore_signal(
            barrier, inc=1, device_id={"narrow": lax.rem(n + d, NN)}, device_id_type=MESH
        )
    for a in (wup, wdn):
        for b in (nup, ndn):
            pl.semaphore_signal(
                barrier, inc=1, device_id={"wide": a, "narrow": b}, device_id_type=MESH
            )

    keep(bands.at[0], band(MASS))
    keep(bands.at[1], band(STIFF))
    for c in small:
        c.wait()
    exc[...] = jnp.transpose(jnp.broadcast_to(ex_ref[...].reshape(1, NX), (128, NX)))

    pl.semaphore_wait(barrier, NW - 1 + NN - 1 + 4)

    def send(src, dst, ssem, rsem, where):
        c = pltpu.make_async_remote_copy(
            src_ref=src,
            dst_ref=dst,
            send_sem=ssem,
            recv_sem=rsem,
            device_id=where,
            device_id_type=MESH,
        )
        c.start()

    def done(ref, sem):
        pltpu.make_async_copy(ref, ref, sem).wait()

    def near(d):
        return core == (d + 1) % 2

    def rows_of(v):
        return pl.ds(pl.multiple_of(v * CY, 8), CY)

    def share(own, whole, ssem, rsem):
        for d in FAR:

            @pl.when(near(d))
            def _(d=d):
                at = {"narrow": lax.rem(n + d, NN)}
                send(own, whole.at[rows_of(n)], ssem, rsem.at[d], at)

    def hand_over(whole, rsem, fsem, gsem):
        for d in FAR:

            @pl.when(near(d))
            def _(d=d):
                m = rows_of(lax.rem(n + NN - d, NN))
                done(whole.at[m], rsem.at[d])
                send(whole.at[m], whole.at[m], fsem, gsem, {"wide": sibling})

    def by_core(whole, sem, first_rows):
        @pl.when(core == 0)
        def _():
            done(whole.at[pl.ds(0, first_rows)], sem)

        @pl.when(core == 1)
        def _():
            done(whole.at[pl.ds(0, 280 - first_rows)], sem)

    ownz = pltpu.make_async_copy(bz_ref, wz.at[rows_of(n)], lsem.at[0])
    owny = pltpu.make_async_copy(by_ref, wy.at[rows_of(n)], lsem.at[1])
    rows_x = pl.ds(gy * CX, CX)
    for k in range(5):
        pltpu.make_async_copy(
            bx_ref.at[:, pl.ds(128 * k, 128)], wx.at[k, gx, core, rows_x], lsem.at[2]
        ).start()
    ownz.start()
    owny.start()
    share(bz_ref, wz, zbs, zbr)
    share(by_ref, wy, ybs, ybr)

    done(wx.at[:, gx, core, rows_x], lsem.at[2])
    for d in FAR:
        at = {"wide": gx * 16 + lax.rem(gy + d, 8) * 2 + core}
        block = wx.at[:, gx, core, rows_x]
        send(block, block, xs.at[0], xr.at[0], at)

    has = {"xu": w < NW - 1, "xd": w > 0, "yu": n < NN - 1, "yd": n > 0}
    spans = {
        "": (pl.ds(3, 10), pl.ds(3, 10)),
        "xu": (pl.ds(10, 3), pl.ds(0, 3)),
        "xd": (pl.ds(3, 3), pl.ds(13, 3)),
    }
    rows = {
        "": (pl.ds(8, 40), pl.ds(8, 40)),
        "yu": (pl.ds(45, 3), pl.ds(5, 3)),
        "yd": (pl.ds(8, 3), pl.ds(48, 3)),
    }
    opposite = {"": "", "xu": "xd", "xd": "xu", "yu": "yd", "yd": "yu"}
    whole_way = [
        ("xu", "", None),
        ("xd", "", None),
        ("xu", "yu", None),
        ("xu", "yd", None),
        ("xd", "yu", None),
        ("xd", "yd", None),
        ("", "yu", (3, 10)),
        ("", "yd", (3, 10)),
    ]
    ways = {"old": whole_way}
    for i, (x0, p) in enumerate(CHUNKS):
        side = ("xd", "xu", None)[i]
        ways[i, "x"] = [(side, b, None) for b in ("", "yu", "yd") if side]
        ways[i, "y"] = [("", b, (3 + x0, p)) for b in ("yu", "yd")]
    slots = {}
    for key, items in ways.items():
        if key != "old":
            for item in items:
                slots[item] = len(slots)

    def slot(key, item, j):
        return (0, j) if key == "old" else (1, slots[item])

    def exists(a, b):
        if a and b:
            return has[a] & has[b]
        return has[a or b]

    def side_of(a, planes, end):
        return pl.ds(*planes) if planes else spans[a][end]

    def start_halo(v, key):
        for j, item in enumerate(ways[key]):
            a, b, planes = item

            @pl.when(exists(a, b))
            def _(key=key, item=item, j=j, a=a, b=b, planes=planes):
                at = {}
                if a:
                    at["wide"] = wup if a == "xu" else wdn
                if b:
                    at["narrow"] = nup if b == "yu" else ndn
                send(
                    v.at[side_of(a, planes, 0), rows[b][0]],
                    v.at[side_of(a, planes, 1), rows[b][1]],
                    hs.at[slot(key, item, j)],
                    hr.at[slot(key, item, j)],
                    at,
                )

    def wait_halo(v, key):
        for j, item in enumerate(ways[key]):
            a, b, planes = item

            @pl.when(exists(opposite[a], opposite[b]))
            def _(key=key, item=item, j=j, a=a, b=b, planes=planes):
                done(v.at[side_of(a, planes, 1), rows[b][1]], hr.at[slot(key, item, j)])

    def drain_halo(v, key):
        for j, item in enumerate(ways[key]):
            a, b, planes = item

            @pl.when(exists(a, b))
            def _(key=key, item=item, j=j, a=a, b=b, planes=planes):
                done(v.at[side_of(a, planes, 0), rows[b][0]], hs.at[slot(key, item, j)])

    hand_over(wz, zbr, zfs, zfr)
    done(wx.at[:, 0, 0, pl.ds(0, 70)], xr.at[0])
    for e in (2, 1, 3):
        at = {"wide": lax.rem(gx + e, 4) * 16 + gy * 2 + core}
        send(wx.at[:, gx, core], wx.at[:, gx, core], xs.at[1], xr.at[1], at)

    get_res.wait()
    ownz.wait()
    by_core(wz, zfr, 120)
    for i, (x0, p) in enumerate(CHUNKS):
        flat = dot(wz[...], res[x0 : x0 + p].reshape(p * CY, NZ), 0, 1)
        n1s[i][:, 0:40, :] = flat[:, 0:120].reshape(NN, CY, 120)
        if p == 4:
            for m in range(NN):
                pack_plane(n1s[i], m, flat[m * CY : m * CY + CY, 120:160])
        pltpu.make_async_copy(n1s[i].at[n], n1r[i].at[n], n1rs.at[i, n]).start()
        for d in FAR:
            v = lax.rem(n + d, NN)
            at = {"narrow": v}
            send(n1s[i].at[v], n1r[i].at[n], n1ss.at[i], n1rs.at[i, n], at)

    hand_over(wy, ybr, yfs, yfr)
    get_dir.wait()
    start_halo(vd, "old")
    tile = first_tile(gx, core, gy)
    two = has_second(gx, core, gy)
    one = jnp.logical_not(two)

    owny.wait()
    by_core(wy, yfr, 120)
    keep(wyr, wy[...])

    for i, (x0, p) in enumerate(CHUNKS):
        for m in range(NN):
            done(n1r[i].at[m], n1rs.at[i, m])
            cols = slice(m * CY, m * CY + CY)
            for x in range(3):
                r = (x0 + x) * CY
                lines[r : r + CY, cols] = n1r[i][m, 0:40, x * CY : x * CY + CY]
            if p == 4:
                r = (x0 + 3) * CY
                lines[r : r + 16, cols] = n1r[i][m, 40:56, 0:40]
                lines[r + 16 : r + 32, cols] = n1r[i][m, 40:56, 40:80]
                lines[r + 32 : r + 40, cols] = n1r[i][m, 40:48, 80:120]
        span = slice(x0 * CY, (x0 + p) * CY)
        t2[span, :] = dot3(split(lines[span, :]), (wyr[0], wyr[1]), 1, 0)
        for x in range(p):
            r = (x0 + x) * CY
            at = 100 * x0 + x
            for j in range(2):
                s1[pl.ds(at + j * 40 * p, 40, stride=p), :] = t2[
                    r : r + CY, 128 * j : 128 * j + 128
                ]
            s1[pl.ds(at + 80 * p, 20, stride=p), :] = jnp.concatenate(
                [t2[r : r + 20, 256:320], t2[r + 20 : r + CY, 256:320]], axis=1
            )

        def send_u(x, c, y, i=i, x0=x0, p=p):
            at = device(x, c, y)
            src, dst = 100 * x0 + first_tile(x, c, y) * p, 128 * x0 + me * 2 * p
            double = has_second(x, c, y)

            @pl.when(double)
            def _():
                send(s1.at[pl.ds(src, 2 * p)], ub.at[pl.ds(dst, 2 * p)], us.at[i], ur.at[i], at)

            @pl.when(jnp.logical_not(double))
            def _():
                send(s1.at[pl.ds(src, p)], ub.at[pl.ds(dst, p)], us.at[i], ur.at[i], at)

        each_wide(send_u)

        def keep_u(size, x0=x0, p=p):
            c = pltpu.make_async_copy(
                s1.at[pl.ds(100 * x0 + tile * p, size)],
                ub.at[pl.ds(128 * x0 + me * 2 * p, size)],
                lsem.at[3],
            )
            c.start()
            c.wait()

        @pl.when(two)
        def _(p=p, keep_u=keep_u):
            keep_u(2 * p)

        @pl.when(one)
        def _(p=p, keep_u=keep_u):
            keep_u(p)

    ey = ey_ref[...].reshape(1, NZ)

    def shift_row(t):
        j = lax.div(t, 40)
        c = t - j * 40
        row = jnp.where(j == 0, ey[:, 0:128], ey[:, 128:256])
        tail = ey[:, 256:320]
        row = jnp.where(j == 2, jnp.concatenate([tail, tail], axis=1), row)
        late = c + 20 * lax.div(j, 2)
        low = lax.broadcasted_iota(jnp.int32, (1, 128), 1) < 64
        return row + jnp.where(low, ez_ref[n * CY + c], ez_ref[n * CY + late])

    shift = jnp.concatenate([shift_row(tile), shift_row(jnp.minimum(tile + 1, 99))], axis=1)
    done(wx.at[:, pl.ds(0, 3), 0], xr.at[1])
    send(wx.at[:, :, core], wx.at[:, :, core], xs.at[2], xr.at[2], {"wide": sibling})
    wait_halo(vd, "old")
    along_y(vd, my, ky, 0, CX + 6)
    along_xz(my, ky, first, second, bands, image)

    done(wx.at[:, :, 0], xr.at[2])
    for k in range(5):
        for x in range(CX):
            for g in range(8):
                wxp[k, x * 64 + g * 8 : x * 64 + g * 8 + 8, :] = wx[
                    k, g // 2, g % 2, pl.ds(x, 8, stride=CX), :
                ]
        cols = slice(128 * k, 128 * k + 128)
        wxr[0, :, cols], wxr[1, :, cols] = split(wxp[k])
        wxc[0, cols, :], wxc[1, cols, :] = split(jnp.transpose(wxp[k]))
    keep(wyc, jnp.transpose(wy[...]))
    keep(wzc, jnp.transpose(wz[...]))
    for i, (x0, p) in enumerate(CHUNKS):

        @pl.when(two)
        def _(i=i, p=p):
            done(ub.at[pl.ds(0, 126 * p)], ur.at[i])

        @pl.when(one)
        def _(i=i, p=p):
            done(ub.at[pl.ds(0, 63 * p)], ur.at[i])

    both = jnp.concatenate(
        [
            jnp.concatenate(
                [
                    ub[pl.ds(128 * x0 + k * p + x, 64, stride=2 * p), :]
                    for x0, p in sorted(CHUNKS)
                    for x in range(p)
                ],
                axis=0,
            )
            for k in range(2)
        ],
        axis=1,
    )
    spectral = dot3((wxc[0], wxc[1]), split(both), 1, 0)
    cols = jnp.concatenate([exc[...], exc[...]], axis=1)
    spectral = split(spectral / (cols + shift))
    for i, (x0, p) in enumerate(CHUNKS):
        span = slice(64 * x0, 64 * (x0 + p))
        inverse = dot3((wxr[0, span, :], wxr[1, span, :]), spectral, 1, 0)
        for x in range(p):
            for k in range(2):
                vb[pl.ds(128 * x0 + k * p + x, 64, stride=2 * p), :] = inverse[
                    x * 64 : x * 64 + 64, 128 * k : 128 * k + 128
                ]

        def back(size, i=i, x0=x0, p=p):
            here = pl.ds(100 * x0 + tile * p, size)

            def send_v(x, c, y):
                src = vb.at[pl.ds(128 * x0 + (x * 16 + c * 8 + y) * 2 * p, size)]
                send(src, s2.at[here], vs.at[i], vr.at[i], device(x, c, y))

            each_wide(send_v)
            c = pltpu.make_async_copy(
                vb.at[pl.ds(128 * x0 + me * 2 * p, size)], s2.at[here], lsem.at[5]
            )
            c.start()
            c.wait()

        @pl.when(two)
        def _(p=p, back=back):
            back(2 * p)

        @pl.when(one)
        def _(p=p, back=back):
            back(p)

    for i, (x0, p) in enumerate(CHUNKS):
        @pl.when(two)
        def _(i=i, p=p):
            done(s2.at[pl.ds(0, 98 * p)], vr.at[i])

        @pl.when(one)
        def _(i=i, p=p):
            done(s2.at[pl.ds(0, 99 * p)], vr.at[i])

        for x in range(p):
            r = (x0 + x) * CY
            at = 100 * x0 + x
            for j in range(2):
                t2[r : r + CY, 128 * j : 128 * j + 128] = s2[
                    pl.ds(at + j * 40 * p, 40, stride=p), :
                ]
            b = s2[pl.ds(at + 80 * p, 20, stride=p), :]
            t2[r : r + 20, 256:320] = b[:, 0:64]
            t2[r + 20 : r + CY, 256:320] = b[:, 64:128]
        span = slice(x0 * CY, (x0 + p) * CY)
        lines[span, :] = dot3(split(t2[span, :]), (wyc[0], wyc[1]), 1, 0)
        for m in range(NN):
            cols = slice(m * CY, m * CY + CY)
            for x in range(3):
                r = (x0 + x) * CY
                n2s[i][m, 0:40, x * CY : x * CY + CY] = lines[r : r + CY, cols]
            if p == 4:
                r = (x0 + 3) * CY
                pack_plane(n2s[i], m, lines[r : r + CY, cols])
        own = pltpu.make_async_copy(n2s[i].at[n], n2r[i].at[n], lsem.at[7])
        own.start()
        for d in FAR:
            v = lax.rem(n + d, NN)
            send(n2s[i].at[v], n2r[i].at[n], n2ss.at[i], n2rs.at[i], {"narrow": v})
        own.wait()

    for i, (x0, p) in enumerate(CHUNKS):
        done(n2r[i].at[pl.ds(0, 7)], n2rs.at[i])
        flat = n2r[i][:, 0:40, :].reshape(NZ, 120)
        if p == 4:
            wide4[:, 0:120] = flat
            for m in range(NN):
                r = m * CY
                wide4[r : r + 16, 120:160] = n2r[i][m, 40:56, 0:40]
                wide4[r + 16 : r + 32, 120:160] = n2r[i][m, 40:56, 40:80]
                wide4[r + 32 : r + 40, 120:160] = n2r[i][m, 40:48, 80:120]
            flat = wide4[...]
        vp[3 + x0 : 3 + x0 + p, 8:48, :] = dot3(
            split(jnp.transpose(flat)), (wzc[0], wzc[1]), 1, 0
        ).reshape(p, CY, NZ)
        start_halo(vp, (i, "x"))
        start_halo(vp, (i, "y"))
        if i == 1:
            wait_halo(vp, (0, "y"))
            along_y(vp, my, ky, 3, 6)

    wait_halo(vp, (1, "y"))
    along_y(vp, my, ky, 9, 13)
    wait_halo(vp, (0, "x"))
    along_y(vp, my, ky, 13, 16)
    wait_halo(vp, (1, "x"))
    along_y(vp, my, ky, 0, 3)
    wait_halo(vp, (2, "y"))
    along_y(vp, my, ky, 6, 9)
    along_xz(my, ky, first, second, bands, fresh)

    precond = vp[3:13, 8:48, :].reshape(CX * CY, NZ)
    direction = vd[3:13, 8:48, :].reshape(CX * CY, NZ)
    res2 = res[...].reshape(CX * CY, NZ)
    items = (
        total(res2, precond),
        total(precond, fresh[...]),
        total(precond, image[...]),
        total(direction, image[...]),
    )
    lane = lax.broadcasted_iota(jnp.int32, (1, 128), 1)
    row = jnp.zeros((1, 128), jnp.float32)
    for i, item in enumerate(items):
        row = jnp.where(lane == i, item, row)
    red[0] = row
    rb1[n] = row
    for d in FAR:
        send(red.at[0], rb1.at[n], rs1, rr1, {"narrow": lax.rem(n + d, NN)})
    done(rb1.at[pl.ds(0, 7)], rr1)
    row = jnp.sum(rb1[...], axis=0)
    red[1] = row
    rb2[w] = row

    def send_r(x, c, y):
        send(red.at[1], rb2.at[w], rs2, rr2, device(x, c, y))

    each_wide(send_r)
    done(rb2.at[pl.ds(0, 63)], rr2)
    row = jnp.sum(rb2[...], axis=0)
    now, self_term, cross, curvature = (
        jnp.sum(jnp.where(lane == i, row, 0.0), axis=1, keepdims=True) for i in range(4)
    )
    ratio = now / prev_ref[0]
    curvature = self_term + 2.0 * ratio * cross + ratio * ratio * curvature
    alpha = now / curvature
    get_sol.wait()
    sol2 = sol[...].reshape(CX * CY, NZ)
    direction = precond + ratio * direction
    new_image = fresh[...] + ratio * image[...]
    sol_out[...] = (sol2 + alpha * direction).reshape(CX, CY, NZ)
    res_out[...] = (res2 - alpha * new_image).reshape(CX, CY, NZ)
    dir_out[...] = direction.reshape(CX, CY, NZ)

    by_core(wz, zbs, 160)
    by_core(wz, zfs, 160)
    by_core(wy, ybs, 160)
    by_core(wy, yfs, 160)
    done(wx.at[:, 0, 0, pl.ds(0, 70)], xs.at[0])
    done(wx.at[:, pl.ds(0, 3), 0], xs.at[1])
    done(wx.at[:, :, 0], xs.at[2])
    drain_halo(vd, "old")
    for i in range(len(CHUNKS)):
        drain_halo(vp, (i, "x"))
        drain_halo(vp, (i, "y"))
    for i, (x0, p) in enumerate(CHUNKS):
        done(n1s[i].at[pl.ds(0, 7)], n1ss.at[i])
        done(n2s[i].at[pl.ds(0, 7)], n2ss.at[i])

        @pl.when(two)
        def _(i=i, p=p):
            done(s1.at[pl.ds(0, 98 * p)], us.at[i])
            done(vb.at[pl.ds(0, 126 * p)], vs.at[i])

        @pl.when(one)
        def _(i=i, p=p):
            done(s1.at[pl.ds(0, 99 * p)], us.at[i])
            done(vb.at[pl.ds(0, 63 * p)], vs.at[i])

    done(rb1.at[pl.ds(0, 7)], rs1)
    done(rb2.at[pl.ds(0, 63)], rs2)


def finish(sol, res, direction, sol_out, res_out, dir_out):
    sol_out[...] = sol[...]
    res_out[...] = res[...]
    dir_out[...] = direction[...]


def per_device(sol, res, direction, prev, bx, by, bz, ex, ey, ez):
    f32 = jnp.float32
    brick = jax.ShapeDtypeStruct((CX, CY, NZ), f32)
    vmem = pl.BlockSpec(memory_space=pltpu.VMEM)
    hbm = pl.BlockSpec(memory_space=pltpu.HBM)
    dma = pltpu.SemaphoreType.DMA
    shapes = [
        (CX, CY, NZ),
        (CX, CY, NZ),
        (5, 4, 2, 80, 128),
        (NZ, NZ),
        (NZ, NZ),
        [2, 2, NZ, NZ],
        (NX, 128),
        (16, 56, NZ),
        (16, 56, NZ),
        (16, CY, NZ),
        (16, CY, NZ),
        (CX, CY, NZ),
        (CX, CY, NZ),
        (400, NZ),
        (400, NZ),
        tuple((NN, r, 120) for r in ROWS),
        tuple((NN, r, 120) for r in ROWS),
        (5, NX, 128),
        (NZ, 160),
        [2, NX, NX],
        [2, NX, NX],
        [2, NZ, NZ],
        [2, NZ, NZ],
        [2, NZ, NZ],
        (400, NZ),
        (400, NZ),
        (1000, 128),
        (2 * NX, 128),
        (2 * NX, 128),
        (1000, 128),
        tuple((NN, r, 120) for r in ROWS),
        tuple((NN, r, 120) for r in ROWS),
        (2, 1, 128),
        (NN, 1, 128),
        (NW, 1, 128),
    ]
    sems = [(15,), (3,), (3,), (), (8,), (), (), (), (8,), (), ()]
    k = len(CHUNKS)
    sems += [(2, 12), (2, 12), (k,), (k, 8)] + [(k,)] * 6 + [()] * 4

    def space(s):
        if isinstance(s[0], tuple):
            return [pltpu.VMEM(t, f32) for t in s]
        return pltpu.VMEM(tuple(s), jnp.bfloat16 if isinstance(s, list) else f32)

    far = [
        pltpu.with_memory_space_constraint(a, pltpu.HBM)
        for a in (ex, ey, ez, sol, res, direction, bx, by, bz)
    ]
    outs = pl.pallas_call(
        kernel,
        out_shape=(brick, brick, brick),
        in_specs=[pl.BlockSpec(memory_space=pltpu.SMEM)] + [hbm] * 9,
        out_specs=(vmem, vmem, vmem),
        scratch_shapes=[
            pltpu.VMEM((NX,), f32),
            pltpu.VMEM((NZ,), f32),
            pltpu.SMEM((NZ,), f32),
        ]
        + [space(s) for s in shapes]
        + [dma(s) for s in sems],
        compiler_params=pltpu.CompilerParams(
            collective_id=0, has_side_effects=True, vmem_limit_bytes=28 << 20
        ),
        name="iterate",
    )(prev, *far)
    return pl.pallas_call(
        finish,
        out_shape=(brick, brick, brick),
        in_specs=[vmem] * 3,
        out_specs=(vmem, vmem, vmem),
        compiler_params=pltpu.CompilerParams(vmem_limit_bytes=12 << 20),
        name="finish",
    )(*outs)


def solution(mesh):
    field = P("wide", "narrow", None)
    in_specs = (
        field,
        field,
        field,
        P(),
        P("wide", None),
        P("narrow", None),
        P("narrow", None),
        P(),
        P(),
        P(),
    )
    return jax.shard_map(
        per_device, mesh=mesh, in_specs=in_specs, out_specs=(field, field, field), check_vma=False
    )
```

```python
import functools

import jax
import jax.numpy as jnp
from jax import lax
from jax.experimental import pallas as pl
from jax.experimental.pallas import tpu as pltpu
from jax.sharding import PartitionSpec as P

MASS = (151.0 / 315.0, 397.0 / 1680.0, 1.0 / 42.0, 1.0 / 5040.0)
STIFF = (2.0 / 3.0, -0.125, -0.2, -1.0 / 120.0)
MESH = pl.DeviceIdType.MESH
NW, NN = 64, 8
CX, CY, NZ, NX = 10, 40, 320, 640
CHUNKS = ((0, 3), (6, 4), (3, 3))
ROWS = (40, 56, 40)
FAR = (4, 3, 5, 2, 6, 1, 7)


def dot(a, b, ca, cb):
    return lax.dot_general(
        a,
        b,
        (((ca,), (cb,)), ((), ())),
        precision=lax.Precision.HIGH,
        preferred_element_type=jnp.float32,
    )


def split(x):
    high = x.astype(jnp.bfloat16)
    return high, (x - high.astype(jnp.float32)).astype(jnp.bfloat16)


def dot3(a, b, ca, cb):
    def one(x, y):
        return lax.dot_general(
            x, y, (((ca,), (cb,)), ((), ())), preferred_element_type=jnp.float32
        )

    return one(a[0], b[0]) + one(a[0], b[1]) + one(a[1], b[0])


def ends(x):
    high, low = split(x)
    return jnp.concatenate([high, low, high], axis=0)


def long_dot(a, b):
    return lax.dot_general(a, b, (((1,), (0,)), ((), ())), preferred_element_type=jnp.float32)


def keep(ref, x):
    ref[0], ref[1] = split(x)


def has_second(x, core, y):
    return (core == 0) | (y == 2 * x)


def first_tile(x, core, y):
    q = x * 8 + y
    return (1 - core) * 2 * q + core * (64 + q + x + jnp.where(y > 2 * x, 1, 0))


def band(coeffs):
    gap = jnp.abs(
        lax.broadcasted_iota(jnp.int32, (NZ, NZ), 0) - lax.broadcasted_iota(jnp.int32, (NZ, NZ), 1)
    )
    out = jnp.zeros((NZ, NZ), jnp.float32)
    for o in range(4):
        out = jnp.where(gap == o, coeffs[o], out)
    return out


def total(a, b):
    return jnp.sum(jnp.sum(a * b, axis=0, keepdims=True), axis=1, keepdims=True)


def along_y(padded, my, ky, start, stop):
    def step(p, carry):
        c = padded[p, 8:48, :]
        m = MASS[0] * c
        k = STIFF[0] * c
        for o in (1, 2, 3):
            s = padded[p, 8 - o : 48 - o, :] + padded[p, 8 + o : 48 + o, :]
            m += MASS[o] * s
            k += STIFF[o] * s
        my[p] = m
        ky[p] = k
        return carry

    lax.fori_loop(start, stop, step, 0)


def along_xz(my, ky, first, second, bands, out):
    def step(q, carry):
        a = my[q + 3]
        f = MASS[0] * a
        g = STIFF[0] * a + MASS[0] * ky[q + 3]
        for o in (1, 2, 3):
            s = my[q + 3 - o] + my[q + 3 + o]
            t = ky[q + 3 - o] + ky[q + 3 + o]
            f += MASS[o] * s
            g += STIFF[o] * s + MASS[o] * t
        first[q] = g
        second[q] = f
        return carry

    lax.fori_loop(0, CX, step, 0)
    g = split(first[...].reshape(CX * CY, NZ))
    f = split(second[...].reshape(CX * CY, NZ))
    m, k = ((bands[i, 0], bands[i, 1]) for i in range(2))
    out[...] = dot3(g, m, 1, 0) + dot3(f, k, 1, 0)


def pack_basis(dst, src):
    dst[0:40, :] = src[:, 0:128]
    dst[40:80, :] = src[:, 128:256]
    dst[80:104, 0:64] = src[0:24, 256:320]
    dst[80:96, 64:128] = src[24:40, 256:320]


def unpack_basis(dst, src):
    for m in range(NN):
        r = m * CY
        dst[r : r + CY, 0:128] = src[m, 0:40, :]
        dst[r : r + CY, 128:256] = src[m, 40:80, :]
        dst[r : r + 24, 256:320] = src[m, 80:104, 0:64]
        dst[r + 24 : r + CY, 256:320] = src[m, 80:96, 64:128]


def pack_plane(dst, m, rows):
    dst[m, 40:56, 0:40] = rows[0:16, :]
    dst[m, 40:56, 40:80] = rows[16:32, :]
    dst[m, 40:48, 80:120] = rows[32:40, :]


def kernel(
    prev_ref,
    ex_hbm,
    ey_hbm,
    ez_hbm,
    sol_ref,
    res_ref,
    dir_ref,
    bx_ref,
    by_ref,
    bz_ref,
    sol_out,
    res_out,
    dir_out,
    ex_ref,
    ey_ref,
    ez_ref,
    sol,
    res,
    wx,
    wy,
    wz,
    bands,
    exc,
    vd,
    vp,
    my,
    ky,
    first,
    second,
    image,
    fresh,
    n1s,
    n1r,
    wxp,
    wide4,
    zraw,
    yraw,
    bzp,
    byp,
    wzp,
    wyp,
    part,
    wxr,
    wxc,
    wyr,
    wyc,
    wzc,
    lines,
    t2,
    s1,
    ub,
    vb,
    s2,
    n2s,
    n2r,
    red,
    rb1,
    rb2,
    lsem,
    xs,
    xr,
    ybs,
    ybr,
    yfs,
    yfr,
    zbs,
    zbr,
    zfs,
    zfr,
    hs,
    hr,
    n1ss,
    n1rs,
    us,
    ur,
    vs,
    vr,
    n2ss,
    n2rs,
    rs1,
    rr1,
    rs2,
    rr2,
):
    w = lax.axis_index("wide")
    n = lax.axis_index("narrow")
    wup, wdn = lax.rem(w + 1, NW), lax.rem(w + NW - 1, NW)
    nup, ndn = lax.rem(n + 1, NN), lax.rem(n + NN - 1, NN)
    core = lax.rem(w, 2)
    sibling = w + 1 - 2 * core
    gx, gy = lax.div(w, 16), lax.rem(lax.div(w, 2), 8)
    me = gx * 16 + core * 8 + gy
    barrier = pltpu.get_barrier_semaphore()
    lines_x = [lax.rem(gx + e, 4) for e in range(4)]
    cores = [core, 1 - core]

    def each_wide(fn):
        def ring(k, carry):
            y = lax.rem(gy + 4 + lax.div(k + 1, 2) * (1 - 2 * lax.rem(k, 2)), 8)
            for e in (2, 1, 3, 0):
                for c in (1, 0):
                    fn(lines_x[e], cores[c], y)
            return carry

        lax.fori_loop(0, 7, ring, 0)
        for e in (2, 1, 3, 0):
            for c in (1, 0):
                if e or c:
                    fn(lines_x[e], cores[c], gy)

    def device(x, c, y):
        return {"wide": x * 16 + y * 2 + c}

    get_res = pltpu.make_async_copy(res_ref, res, lsem.at[8])
    get_dir = pltpu.make_async_copy(dir_ref, vd.at[pl.ds(3, CX), pl.ds(8, CY)], lsem.at[9])
    get_sol = pltpu.make_async_copy(sol_ref, sol, lsem.at[6])
    small = [
        pltpu.make_async_copy(a, b, lsem.at[11 + i])
        for i, (a, b) in enumerate(
            ((ex_hbm, ex_ref), (ey_hbm, ey_ref), (ez_hbm, ez_ref))
        )
    ]
    bases = [
        pltpu.make_async_copy(bz_ref, zraw, lsem.at[0]),
        pltpu.make_async_copy(by_ref, yraw, lsem.at[1]),
    ]
    for c in [*bases, get_res, get_dir, *small, get_sol]:
        c.start()

    def greet(x, c, y):
        pl.semaphore_signal(barrier, inc=1, device_id=device(x, c, y), device_id_type=MESH)

    each_wide(greet)
    for d in FAR:
        pl.semaphore_signal(
            barrier, inc=1, device_id={"narrow": lax.rem(n + d, NN)}, device_id_type=MESH
        )
    for a in (wup, wdn):
        for b in (nup, ndn):
            pl.semaphore_signal(
                barrier, inc=1, device_id={"wide": a, "narrow": b}, device_id_type=MESH
            )

    for c in bases:
        c.wait()
    pack_basis(bzp, zraw)
    pack_basis(byp, yraw)

    pl.semaphore_wait(barrier, NW - 1 + NN - 1 + 4)

    def send(src, dst, ssem, rsem, where):
        c = pltpu.make_async_remote_copy(
            src_ref=src,
            dst_ref=dst,
            send_sem=ssem,
            recv_sem=rsem,
            device_id=where,
            device_id_type=MESH,
        )
        c.start()

    def done(ref, sem):
        pltpu.make_async_copy(ref, ref, sem).wait()

    def near(d):
        return core == (d + 1) % 2

    def share(own, whole, ssem, rsem):
        for d in FAR:

            @pl.when(near(d))
            def _(d=d):
                at = {"narrow": lax.rem(n + d, NN)}
                send(own, whole.at[n], ssem, rsem.at[d], at)

    def hand_over(whole, rsem, fsem, gsem):
        for d in FAR:

            @pl.when(near(d))
            def _(d=d):
                m = lax.rem(n + NN - d, NN)
                done(whole.at[m], rsem.at[d])
                send(whole.at[m], whole.at[m], fsem, gsem, {"wide": sibling})

    def by_core(whole, sem, blocks):
        @pl.when(core == 0)
        def _():
            done(whole.at[pl.ds(0, blocks)], sem)

        @pl.when(core == 1)
        def _():
            done(whole.at[pl.ds(0, 7 - blocks)], sem)

    ownz = pltpu.make_async_copy(bzp, wzp.at[n], lsem.at[14])
    owny = pltpu.make_async_copy(byp, wyp.at[n], lsem.at[10])
    rows_x = pl.ds(gy * CX, CX)
    for k in range(5):
        pltpu.make_async_copy(
            bx_ref.at[:, pl.ds(128 * k, 128)], wx.at[k, gx, core, rows_x], lsem.at[2]
        ).start()
    ownz.start()
    owny.start()
    share(bzp, wzp, zbs, zbr)
    share(byp, wyp, ybs, ybr)

    done(wx.at[:, gx, core, rows_x], lsem.at[2])
    for d in FAR:
        at = {"wide": gx * 16 + lax.rem(gy + d, 8) * 2 + core}
        block = wx.at[:, gx, core, rows_x]
        send(block, block, xs.at[0], xr.at[0], at)

    has = {"xu": w < NW - 1, "xd": w > 0, "yu": n < NN - 1, "yd": n > 0}
    spans = {
        "": (pl.ds(3, 10), pl.ds(3, 10)),
        "xu": (pl.ds(10, 3), pl.ds(0, 3)),
        "xd": (pl.ds(3, 3), pl.ds(13, 3)),
    }
    rows = {
        "": (pl.ds(8, 40), pl.ds(8, 40)),
        "yu": (pl.ds(45, 3), pl.ds(5, 3)),
        "yd": (pl.ds(8, 3), pl.ds(48, 3)),
    }
    opposite = {"": "", "xu": "xd", "xd": "xu", "yu": "yd", "yd": "yu"}
    whole_way = [
        ("xu", "", None),
        ("xd", "", None),
        ("xu", "yu", None),
        ("xu", "yd", None),
        ("xd", "yu", None),
        ("xd", "yd", None),
        ("", "yu", (3, 10)),
        ("", "yd", (3, 10)),
    ]
    ways = {"old": whole_way}
    for i, (x0, p) in enumerate(CHUNKS):
        side = ("xd", "xu", None)[i]
        ways[i, "x"] = [(side, b, None) for b in ("", "yu", "yd") if side]
        ways[i, "y"] = [("", b, (3 + x0, p)) for b in ("yu", "yd")]
    slots = {}
    for key, items in ways.items():
        if key != "old":
            for item in items:
                slots[item] = len(slots)

    def slot(key, item, j):
        return (0, j) if key == "old" else (1, slots[item])

    def exists(a, b):
        if a and b:
            return has[a] & has[b]
        return has[a or b]

    def side_of(a, planes, end):
        return pl.ds(*planes) if planes else spans[a][end]

    def start_halo(v, key):
        for j, item in enumerate(ways[key]):
            a, b, planes = item

            @pl.when(exists(a, b))
            def _(key=key, item=item, j=j, a=a, b=b, planes=planes):
                at = {}
                if a:
                    at["wide"] = wup if a == "xu" else wdn
                if b:
                    at["narrow"] = nup if b == "yu" else ndn
                send(
                    v.at[side_of(a, planes, 0), rows[b][0]],
                    v.at[side_of(a, planes, 1), rows[b][1]],
                    hs.at[slot(key, item, j)],
                    hr.at[slot(key, item, j)],
                    at,
                )

    def wait_halo(v, key):
        for j, item in enumerate(ways[key]):
            a, b, planes = item

            @pl.when(exists(opposite[a], opposite[b]))
            def _(key=key, item=item, j=j, a=a, b=b, planes=planes):
                done(v.at[side_of(a, planes, 1), rows[b][1]], hr.at[slot(key, item, j)])

    def drain_halo(v, key):
        for j, item in enumerate(ways[key]):
            a, b, planes = item

            @pl.when(exists(a, b))
            def _(key=key, item=item, j=j, a=a, b=b, planes=planes):
                done(v.at[side_of(a, planes, 0), rows[b][0]], hs.at[slot(key, item, j)])

    keep(bands.at[0], band(MASS))
    keep(bands.at[1], band(STIFF))
    for c in small:
        c.wait()
    exc[...] = jnp.transpose(jnp.broadcast_to(ex_ref[...].reshape(1, NX), (128, NX)))
    fills = (
        (w == 0, slice(0, 3), slice(0, 56)),
        (w == NW - 1, slice(13, 16), slice(0, 56)),
        (n == 0, slice(0, 16), slice(0, 8)),
        (n == NN - 1, slice(0, 16), slice(48, 56)),
    )
    for edge, ps, rs in fills:

        @pl.when(edge)
        def _(ps=ps, rs=rs):
            for v in (vd, vp):
                v[ps, rs, :] = jnp.zeros((ps.stop - ps.start, rs.stop - rs.start, NZ), jnp.float32)

    hand_over(wzp, zbr, zfs, zfr)
    done(wx.at[:, 0, 0, pl.ds(0, 70)], xr.at[0])
    for e in (2, 1, 3):
        at = {"wide": lax.rem(gx + e, 4) * 16 + gy * 2 + core}
        send(wx.at[:, gx, core], wx.at[:, gx, core], xs.at[1], xr.at[1], at)

    get_res.wait()
    ownz.wait()
    by_core(wzp, zfr, 3)
    unpack_basis(wz, wzp)
    for i, (x0, p) in enumerate(CHUNKS):
        flat = dot(wz[...], res[x0 : x0 + p].reshape(p * CY, NZ), 0, 1)
        n1s[i][:, 0:40, :] = flat[:, 0:120].reshape(NN, CY, 120)
        if p == 4:
            for m in range(NN):
                pack_plane(n1s[i], m, flat[m * CY : m * CY + CY, 120:160])
        pltpu.make_async_copy(n1s[i].at[n], n1r[i].at[n], n1rs.at[i, n]).start()
        for d in FAR:
            v = lax.rem(n + d, NN)
            at = {"narrow": v}
            send(n1s[i].at[v], n1r[i].at[n], n1ss.at[i], n1rs.at[i, n], at)

    hand_over(wyp, ybr, yfs, yfr)
    get_dir.wait()
    start_halo(vd, "old")
    tile = first_tile(gx, core, gy)
    two = has_second(gx, core, gy)
    one = jnp.logical_not(two)

    owny.wait()
    by_core(wyp, yfr, 3)
    unpack_basis(wy, wyp)
    keep(wyr, wy[...])

    for i, (x0, p) in enumerate(CHUNKS):
        for m in range(NN):
            done(n1r[i].at[m], n1rs.at[i, m])
            cols = slice(m * CY, m * CY + CY)
            for x in range(3):
                r = (x0 + x) * CY
                lines[r : r + CY, cols] = n1r[i][m, 0:40, x * CY : x * CY + CY]
            if p == 4:
                r = (x0 + 3) * CY
                lines[r : r + 16, cols] = n1r[i][m, 40:56, 0:40]
                lines[r + 16 : r + 32, cols] = n1r[i][m, 40:56, 40:80]
                lines[r + 32 : r + 40, cols] = n1r[i][m, 40:48, 80:120]
        span = slice(x0 * CY, (x0 + p) * CY)
        t2[span, :] = dot3(split(lines[span, :]), (wyr[0], wyr[1]), 1, 0)
        for x in range(p):
            r = (x0 + x) * CY
            at = 100 * x0 + x
            for j in range(2):
                s1[pl.ds(at + j * 40 * p, 40, stride=p), :] = t2[
                    r : r + CY, 128 * j : 128 * j + 128
                ]
            s1[pl.ds(at + 80 * p, 20, stride=p), :] = jnp.concatenate(
                [t2[r : r + 20, 256:320], t2[r + 20 : r + CY, 256:320]], axis=1
            )

        def send_u(x, c, y, i=i, x0=x0, p=p):
            at = device(x, c, y)
            src, dst = 100 * x0 + first_tile(x, c, y) * p, 128 * x0 + me * 2 * p
            double = has_second(x, c, y)

            @pl.when(double)
            def _():
                send(s1.at[pl.ds(src, 2 * p)], ub.at[pl.ds(dst, 2 * p)], us.at[i], ur.at[i], at)

            @pl.when(jnp.logical_not(double))
            def _():
                send(s1.at[pl.ds(src, p)], ub.at[pl.ds(dst, p)], us.at[i], ur.at[i], at)

        each_wide(send_u)

        def keep_u(size, x0=x0, p=p):
            c = pltpu.make_async_copy(
                s1.at[pl.ds(100 * x0 + tile * p, size)],
                ub.at[pl.ds(128 * x0 + me * 2 * p, size)],
                lsem.at[3],
            )
            c.start()
            c.wait()

        @pl.when(two)
        def _(p=p, keep_u=keep_u):
            keep_u(2 * p)

        @pl.when(one)
        def _(p=p, keep_u=keep_u):
            keep_u(p)

    ey = ey_ref[...].reshape(1, NZ)

    def shift_row(t):
        j = lax.div(t, 40)
        c = t - j * 40
        row = jnp.where(j == 0, ey[:, 0:128], ey[:, 128:256])
        tail = ey[:, 256:320]
        row = jnp.where(j == 2, jnp.concatenate([tail, tail], axis=1), row)
        late = c + 20 * lax.div(j, 2)
        low = lax.broadcasted_iota(jnp.int32, (1, 128), 1) < 64
        return row + jnp.where(low, ez_ref[n * CY + c], ez_ref[n * CY + late])

    shift = jnp.concatenate([shift_row(tile), shift_row(jnp.minimum(tile + 1, 99))], axis=1)
    done(wx.at[:, pl.ds(0, 3), 0], xr.at[1])
    send(wx.at[:, :, core], wx.at[:, :, core], xs.at[2], xr.at[2], {"wide": sibling})
    wait_halo(vd, "old")
    along_y(vd, my, ky, 0, CX + 6)
    along_xz(my, ky, first, second, bands, image)

    done(wx.at[:, :, 0], xr.at[2])
    for k in range(5):
        for x in range(CX):
            for g in range(8):
                wxp[k, x * 64 + g * 8 : x * 64 + g * 8 + 8, :] = wx[
                    k, g // 2, g % 2, pl.ds(x, 8, stride=CX), :
                ]
        cols = slice(128 * k, 128 * k + 128)
        high, low = split(wxp[k])
        wxr[:, 128 * k : 128 * k + 128] = high
        wxr[:, NX + 128 * k : NX + 128 * k + 128] = high
        wxr[:, 2 * NX + 128 * k : 2 * NX + 128 * k + 128] = low
        for i, (x0, p) in enumerate(CHUNKS):
            high, low = split(jnp.transpose(wxp[k, 64 * x0 : 64 * (x0 + p), :]))
            wxc[i][cols, 0 : 64 * p] = high
            wxc[i][cols, 64 * p : 128 * p] = high
            wxc[i][cols, 128 * p : 192 * p] = low
    keep(wyc, jnp.transpose(wy[...]))
    keep(wzc, jnp.transpose(wz[...]))
    spectral = None
    for i, (x0, p) in enumerate(CHUNKS):

        @pl.when(two)
        def _(i=i, p=p):
            done(ub.at[pl.ds(0, 126 * p)], ur.at[i])

        @pl.when(one)
        def _(i=i, x0=x0, p=p):
            for x in range(p):
                ub[pl.ds(128 * x0 + p + x, 64, stride=2 * p), :] = jnp.zeros((64, 128), jnp.float32)
            done(ub.at[pl.ds(0, 63 * p)], ur.at[i])

        if i == len(CHUNKS) - 1:
            pass
        both = jnp.concatenate(
            [
                jnp.concatenate(
                    [
                        ub[pl.ds(128 * x0 + k * p + x, 64, stride=2 * p), :]
                        for x in range(p)
                    ],
                    axis=0,
                )
                for k in range(2)
            ],
            axis=1,
        )
        term = long_dot(wxc[i][...], ends(both))
        if i == 0:
            part[...] = term
        elif i == 1:
            part[...] += term
        else:
            spectral = part[...] + term
    cols = jnp.concatenate([exc[...], exc[...]], axis=1)
    spectral = ends(spectral / (cols + shift))
    for i, (x0, p) in enumerate(CHUNKS):
        span = slice(64 * x0, 64 * (x0 + p))
        inverse = long_dot(wxr[span, :], spectral)
        for x in range(p):
            for k in range(2):
                vb[pl.ds(128 * x0 + k * p + x, 64, stride=2 * p), :] = inverse[
                    x * 64 : x * 64 + 64, 128 * k : 128 * k + 128
                ]

        def back(size, i=i, x0=x0, p=p):
            here = pl.ds(100 * x0 + tile * p, size)

            def send_v(x, c, y):
                src = vb.at[pl.ds(128 * x0 + (x * 16 + c * 8 + y) * 2 * p, size)]
                send(src, s2.at[here], vs.at[i], vr.at[i], device(x, c, y))

            each_wide(send_v)
            c = pltpu.make_async_copy(
                vb.at[pl.ds(128 * x0 + me * 2 * p, size)], s2.at[here], lsem.at[5]
            )
            c.start()
            c.wait()

        @pl.when(two)
        def _(p=p, back=back):
            back(2 * p)

        @pl.when(one)
        def _(p=p, back=back):
            back(p)

    for i, (x0, p) in enumerate(CHUNKS):
        @pl.when(two)
        def _(i=i, p=p):
            done(s2.at[pl.ds(0, 98 * p)], vr.at[i])

        @pl.when(one)
        def _(i=i, p=p):
            done(s2.at[pl.ds(0, 99 * p)], vr.at[i])

        for x in range(p):
            r = (x0 + x) * CY
            at = 100 * x0 + x
            for j in range(2):
                t2[r : r + CY, 128 * j : 128 * j + 128] = s2[
                    pl.ds(at + j * 40 * p, 40, stride=p), :
                ]
            b = s2[pl.ds(at + 80 * p, 20, stride=p), :]
            t2[r : r + 20, 256:320] = b[:, 0:64]
            t2[r + 20 : r + CY, 256:320] = b[:, 64:128]
        span = slice(x0 * CY, (x0 + p) * CY)
        lines[span, :] = dot3(split(t2[span, :]), (wyc[0], wyc[1]), 1, 0)
        for m in range(NN):
            cols = slice(m * CY, m * CY + CY)
            for x in range(3):
                r = (x0 + x) * CY
                n2s[i][m, 0:40, x * CY : x * CY + CY] = lines[r : r + CY, cols]
            if p == 4:
                r = (x0 + 3) * CY
                pack_plane(n2s[i], m, lines[r : r + CY, cols])
        own = pltpu.make_async_copy(n2s[i].at[n], n2r[i].at[n], lsem.at[7])
        own.start()
        for d in FAR:
            v = lax.rem(n + d, NN)
            send(n2s[i].at[v], n2r[i].at[n], n2ss.at[i], n2rs.at[i], {"narrow": v})
        own.wait()

    for i, (x0, p) in enumerate(CHUNKS):
        done(n2r[i].at[pl.ds(0, 7)], n2rs.at[i])
        flat = n2r[i][:, 0:40, :].reshape(NZ, 120)
        if p == 4:
            wide4[:, 0:120] = flat
            for m in range(NN):
                r = m * CY
                wide4[r : r + 16, 120:160] = n2r[i][m, 40:56, 0:40]
                wide4[r + 16 : r + 32, 120:160] = n2r[i][m, 40:56, 40:80]
                wide4[r + 32 : r + 40, 120:160] = n2r[i][m, 40:48, 80:120]
            flat = wide4[...]
        vp[3 + x0 : 3 + x0 + p, 8:48, :] = dot3(
            split(jnp.transpose(flat)), (wzc[0], wzc[1]), 1, 0
        ).reshape(p, CY, NZ)
        start_halo(vp, (i, "x"))
        start_halo(vp, (i, "y"))
        if i == 1:
            wait_halo(vp, (0, "y"))
            along_y(vp, my, ky, 3, 6)

    wait_halo(vp, (1, "y"))
    along_y(vp, my, ky, 9, 13)
    wait_halo(vp, (0, "x"))
    along_y(vp, my, ky, 13, 16)
    wait_halo(vp, (1, "x"))
    along_y(vp, my, ky, 0, 3)
    precond = vp[3:13, 8:48, :].reshape(CX * CY, NZ)
    direction = vd[3:13, 8:48, :].reshape(CX * CY, NZ)
    early = (
        total(res[...].reshape(CX * CY, NZ), precond),
        total(precond, image[...]),
        total(direction, image[...]),
    )
    wait_halo(vp, (2, "y"))
    along_y(vp, my, ky, 6, 9)
    along_xz(my, ky, first, second, bands, fresh)

    precond = vp[3:13, 8:48, :].reshape(CX * CY, NZ)
    direction = vd[3:13, 8:48, :].reshape(CX * CY, NZ)
    res2 = res[...].reshape(CX * CY, NZ)
    items = (early[0], total(precond, fresh[...]), early[1], early[2])
    lane = lax.broadcasted_iota(jnp.int32, (1, 128), 1)
    row = jnp.zeros((1, 128), jnp.float32)
    for i, item in enumerate(items):
        row = jnp.where(lane == i, item, row)
    red[0] = row
    rb1[n] = row
    for d in FAR:
        send(red.at[0], rb1.at[n], rs1, rr1, {"narrow": lax.rem(n + d, NN)})
    done(rb1.at[pl.ds(0, 7)], rr1)
    row = jnp.sum(rb1[...], axis=0)
    red[1] = row
    rb2[w] = row

    def send_r(x, c, y):
        send(red.at[1], rb2.at[w], rs2, rr2, device(x, c, y))

    each_wide(send_r)
    done(rb2.at[pl.ds(0, 63)], rr2)
    row = jnp.sum(rb2[...], axis=0)
    now, self_term, cross, curvature = (
        jnp.sum(jnp.where(lane == i, row, 0.0), axis=1, keepdims=True) for i in range(4)
    )
    ratio = now / prev_ref[0]
    curvature = self_term + 2.0 * ratio * cross + ratio * ratio * curvature
    alpha = now / curvature
    get_sol.wait()
    sol2 = sol[...].reshape(CX * CY, NZ)
    direction = precond + ratio * direction
    new_image = fresh[...] + ratio * image[...]
    sol_out[...] = (sol2 + alpha * direction).reshape(CX, CY, NZ)
    res_out[...] = (res2 - alpha * new_image).reshape(CX, CY, NZ)
    dir_out[...] = direction.reshape(CX, CY, NZ)

    by_core(wzp, zbs, 4)
    by_core(wzp, zfs, 4)
    by_core(wyp, ybs, 4)
    by_core(wyp, yfs, 4)
    done(wx.at[:, 0, 0, pl.ds(0, 70)], xs.at[0])
    done(wx.at[:, pl.ds(0, 3), 0], xs.at[1])
    done(wx.at[:, :, 0], xs.at[2])
    drain_halo(vd, "old")
    for i in range(len(CHUNKS)):
        drain_halo(vp, (i, "x"))
        drain_halo(vp, (i, "y"))
    for i, (x0, p) in enumerate(CHUNKS):
        done(n1s[i].at[pl.ds(0, 7)], n1ss.at[i])
        done(n2s[i].at[pl.ds(0, 7)], n2ss.at[i])

        @pl.when(two)
        def _(i=i, p=p):
            done(s1.at[pl.ds(0, 98 * p)], us.at[i])
            done(vb.at[pl.ds(0, 126 * p)], vs.at[i])

        @pl.when(one)
        def _(i=i, p=p):
            done(s1.at[pl.ds(0, 99 * p)], us.at[i])
            done(vb.at[pl.ds(0, 63 * p)], vs.at[i])

    done(rb1.at[pl.ds(0, 7)], rs1)
    done(rb2.at[pl.ds(0, 63)], rs2)


def finish(sol, res, direction, sol_out, res_out, dir_out, sems):
    pairs = ((sol, sol_out), (res, res_out), (direction, dir_out))
    copies = [pltpu.make_async_copy(a, b, sems.at[i]) for i, (a, b) in enumerate(pairs)]
    for c in copies:
        c.start()
    for c in copies:
        c.wait()


def per_device(sol, res, direction, prev, bx, by, bz, ex, ey, ez):
    f32 = jnp.float32
    brick = jax.ShapeDtypeStruct((CX, CY, NZ), f32)
    vmem = pl.BlockSpec(memory_space=pltpu.VMEM)
    hbm = pl.BlockSpec(memory_space=pltpu.HBM)
    dma = pltpu.SemaphoreType.DMA
    shapes = [
        (CX, CY, NZ),
        (CX, CY, NZ),
        (5, 4, 2, 80, 128),
        (NZ, NZ),
        (NZ, NZ),
        [2, 2, NZ, NZ],
        (NX, 128),
        (16, 56, NZ),
        (16, 56, NZ),
        (16, CY, NZ),
        (16, CY, NZ),
        (CX, CY, NZ),
        (CX, CY, NZ),
        (400, NZ),
        (400, NZ),
        tuple((NN, r, 120) for r in ROWS),
        tuple((NN, r, 120) for r in ROWS),
        (5, NX, 128),
        (NZ, 160),
        (CY, NZ),
        (CY, NZ),
        (104, 128),
        (104, 128),
        (NN, 104, 128),
        (NN, 104, 128),
        (NX, 256),
        [NX, 3 * NX],
        tuple([NX, 192 * p] for _, p in CHUNKS),
        [2, NZ, NZ],
        [2, NZ, NZ],
        [2, NZ, NZ],
        (400, NZ),
        (400, NZ),
        (1000, 128),
        (2 * NX, 128),
        (2 * NX, 128),
        (1000, 128),
        tuple((NN, r, 120) for r in ROWS),
        tuple((NN, r, 120) for r in ROWS),
        (2, 1, 128),
        (NN, 1, 128),
        (NW, 1, 128),
    ]
    sems = [(15,), (3,), (3,), (), (8,), (), (), (), (8,), (), ()]
    k = len(CHUNKS)
    sems += [(2, 12), (2, 12), (k,), (k, 8)] + [(k,)] * 6 + [()] * 4

    def space(s):
        if isinstance(s[0], (tuple, list)):
            return [space(t) for t in s]
        return pltpu.VMEM(tuple(s), jnp.bfloat16 if isinstance(s, list) else f32)

    far = [
        pltpu.with_memory_space_constraint(a, pltpu.HBM)
        for a in (ex, ey, ez, sol, res, direction, bx, by, bz)
    ]
    outs = pl.pallas_call(
        kernel,
        out_shape=(brick, brick, brick),
        in_specs=[pl.BlockSpec(memory_space=pltpu.SMEM)] + [hbm] * 9,
        out_specs=(vmem, vmem, vmem),
        scratch_shapes=[
            pltpu.VMEM((NX,), f32),
            pltpu.VMEM((NZ,), f32),
            pltpu.SMEM((NZ,), f32),
        ]
        + [space(s) for s in shapes]
        + [dma(s) for s in sems],
        compiler_params=pltpu.CompilerParams(
            collective_id=0, has_side_effects=True, vmem_limit_bytes=28 << 20
        ),
        name="iterate",
    )(prev, *far)
    return pl.pallas_call(
        finish,
        out_shape=(brick, brick, brick),
        in_specs=[vmem] * 3,
        out_specs=(hbm, hbm, hbm),
        scratch_shapes=[dma((3,))],
        compiler_params=pltpu.CompilerParams(vmem_limit_bytes=12 << 20),
        name="finish",
    )(*outs)


def solution(mesh):
    field = P("wide", "narrow", None)
    in_specs = (
        field,
        field,
        field,
        P(),
        P("wide", None),
        P("narrow", None),
        P("narrow", None),
        P(),
        P(),
        P(),
    )
    return jax.shard_map(
        per_device, mesh=mesh, in_specs=in_specs, out_specs=(field, field, field), check_vma=False
    )
```

```python
import functools

import jax
import jax.numpy as jnp
from jax import lax
from jax.experimental import pallas as pl
from jax.experimental.pallas import tpu as pltpu
from jax.sharding import PartitionSpec as P

MASS = (151.0 / 315.0, 397.0 / 1680.0, 1.0 / 42.0, 1.0 / 5040.0)
STIFF = (2.0 / 3.0, -0.125, -0.2, -1.0 / 120.0)
MESH = pl.DeviceIdType.MESH
NW, NN = 64, 8
CX, CY, NZ, NX = 10, 40, 320, 640
CHUNKS = ((0, 3), (6, 4), (3, 3))
ROWS = (40, 56, 40)
FAR = (4, 3, 5, 2, 6, 1, 7)


def dot(a, b, ca, cb):
    return lax.dot_general(
        a,
        b,
        (((ca,), (cb,)), ((), ())),
        precision=lax.Precision.HIGH,
        preferred_element_type=jnp.float32,
    )


def split(x):
    high = x.astype(jnp.bfloat16)
    return high, (x - high.astype(jnp.float32)).astype(jnp.bfloat16)


def dot3(a, b, ca, cb):
    def one(x, y):
        return lax.dot_general(
            x, y, (((ca,), (cb,)), ((), ())), preferred_element_type=jnp.float32
        )

    return one(a[0], b[0]) + one(a[0], b[1]) + one(a[1], b[0])


def ends(x):
    high, low = split(x)
    return jnp.concatenate([high, low, high], axis=0)


def long_dot(a, b):
    return lax.dot_general(a, b, (((1,), (0,)), ((), ())), preferred_element_type=jnp.float32)


def keep(ref, x):
    ref[0], ref[1] = split(x)


def has_second(x, core, y):
    return (core == 0) | (y == 2 * x)


def first_tile(x, core, y):
    q = x * 8 + y
    return (1 - core) * 2 * q + core * (64 + q + x + jnp.where(y > 2 * x, 1, 0))


def band(coeffs):
    gap = jnp.abs(
        lax.broadcasted_iota(jnp.int32, (NZ, NZ), 0) - lax.broadcasted_iota(jnp.int32, (NZ, NZ), 1)
    )
    out = jnp.zeros((NZ, NZ), jnp.float32)
    for o in range(4):
        out = jnp.where(gap == o, coeffs[o], out)
    return out


def total(a, b):
    return jnp.sum(jnp.sum(a * b, axis=0, keepdims=True), axis=1, keepdims=True)


def along_y(padded, my, ky, start, stop):
    def step(p, carry):
        c = padded[p, 8:48, :]
        m = MASS[0] * c
        k = STIFF[0] * c
        for o in (1, 2, 3):
            s = padded[p, 8 - o : 48 - o, :] + padded[p, 8 + o : 48 + o, :]
            m += MASS[o] * s
            k += STIFF[o] * s
        my[p] = m
        ky[p] = k
        return carry

    lax.fori_loop(start, stop, step, 0)


def along_xz(my, ky, first, second, bands, out):
    def step(q, carry):
        a = my[q + 3]
        f = MASS[0] * a
        g = STIFF[0] * a + MASS[0] * ky[q + 3]
        for o in (1, 2, 3):
            s = my[q + 3 - o] + my[q + 3 + o]
            t = ky[q + 3 - o] + ky[q + 3 + o]
            f += MASS[o] * s
            g += STIFF[o] * s + MASS[o] * t
        first[q] = g
        second[q] = f
        return carry

    lax.fori_loop(0, CX, step, 0)
    g = split(first[...].reshape(CX * CY, NZ))
    f = split(second[...].reshape(CX * CY, NZ))
    m, k = ((bands[i, 0], bands[i, 1]) for i in range(2))
    out[...] = dot3(g, m, 1, 0) + dot3(f, k, 1, 0)


def pack_basis(dst, src):
    dst[0:40, :] = src[:, 0:128]
    dst[40:80, :] = src[:, 128:256]
    dst[80:104, 0:64] = src[0:24, 256:320]
    dst[80:96, 64:128] = src[24:40, 256:320]


def unpack_basis(dst, src):
    for m in range(NN):
        r = m * CY
        dst[r : r + CY, 0:128] = src[m, 0:40, :]
        dst[r : r + CY, 128:256] = src[m, 40:80, :]
        dst[r : r + 24, 256:320] = src[m, 80:104, 0:64]
        dst[r + 24 : r + CY, 256:320] = src[m, 80:96, 64:128]


def pack_plane(dst, m, rows):
    dst[m, 40:56, 0:40] = rows[0:16, :]
    dst[m, 40:56, 40:80] = rows[16:32, :]
    dst[m, 40:48, 80:120] = rows[32:40, :]


def kernel(
    prev_ref,
    ex_hbm,
    ey_hbm,
    ez_hbm,
    sol_ref,
    res_ref,
    dir_ref,
    bx_ref,
    by_ref,
    bz_ref,
    sol_out,
    res_out,
    dir_out,
    ex_ref,
    ey_ref,
    ez_ref,
    sol,
    res,
    wx,
    wy,
    wz,
    bands,
    exc,
    vd,
    vp,
    my,
    ky,
    first,
    second,
    image,
    fresh,
    n1s,
    n1r,
    wxp,
    wide4,
    zraw,
    yraw,
    bzp,
    byp,
    wzp,
    wyp,
    part,
    wxr,
    wxc,
    wyr,
    wyc,
    wzc,
    lines,
    t2,
    s1,
    ub,
    vb,
    s2,
    n2s,
    n2r,
    red,
    rb1,
    rb2,
    lsem,
    xs,
    xr,
    ybs,
    ybr,
    yfs,
    yfr,
    zbs,
    zbr,
    zfs,
    zfr,
    hs,
    hr,
    n1ss,
    n1rs,
    us,
    ur,
    vs,
    vr,
    n2ss,
    n2rs,
    rs1,
    rr1,
    rs2,
    rr2,
):
    w = lax.axis_index("wide")
    n = lax.axis_index("narrow")
    wup, wdn = lax.rem(w + 1, NW), lax.rem(w + NW - 1, NW)
    nup, ndn = lax.rem(n + 1, NN), lax.rem(n + NN - 1, NN)
    core = lax.rem(w, 2)
    sibling = w + 1 - 2 * core
    gx, gy = lax.div(w, 16), lax.rem(lax.div(w, 2), 8)
    me = gx * 16 + core * 8 + gy
    barrier = pltpu.get_barrier_semaphore()
    lines_x = [lax.rem(gx + e, 4) for e in range(4)]
    cores = [core, 1 - core]

    def each_wide(fn):
        def ring(k, carry):
            y = lax.rem(gy + 4 + lax.div(k + 1, 2) * (1 - 2 * lax.rem(k, 2)), 8)
            for e in (2, 1, 3, 0):
                for c in (1, 0):
                    fn(lines_x[e], cores[c], y)
            return carry

        lax.fori_loop(0, 7, ring, 0)
        for e in (2, 1, 3, 0):
            for c in (1, 0):
                if e or c:
                    fn(lines_x[e], cores[c], gy)

    def device(x, c, y):
        return {"wide": x * 16 + y * 2 + c}

    get_res = pltpu.make_async_copy(res_ref, res, lsem.at[8])
    get_dir = pltpu.make_async_copy(dir_ref, vd.at[pl.ds(3, CX), pl.ds(8, CY)], lsem.at[9])
    get_sol = pltpu.make_async_copy(sol_ref, sol, lsem.at[6])
    small = [
        pltpu.make_async_copy(a, b, lsem.at[11 + i])
        for i, (a, b) in enumerate(
            ((ex_hbm, ex_ref), (ey_hbm, ey_ref), (ez_hbm, ez_ref))
        )
    ]
    bases = [
        pltpu.make_async_copy(bz_ref, zraw, lsem.at[0]),
        pltpu.make_async_copy(by_ref, yraw, lsem.at[1]),
    ]
    for c in [*bases, get_res, get_dir, *small, get_sol]:
        c.start()

    def greet(x, c, y):
        pl.semaphore_signal(barrier, inc=1, device_id=device(x, c, y), device_id_type=MESH)

    each_wide(greet)
    for d in FAR:
        pl.semaphore_signal(
            barrier, inc=1, device_id={"narrow": lax.rem(n + d, NN)}, device_id_type=MESH
        )
    for a in (wup, wdn):
        for b in (nup, ndn):
            pl.semaphore_signal(
                barrier, inc=1, device_id={"wide": a, "narrow": b}, device_id_type=MESH
            )

    for c in bases:
        c.wait()
    pack_basis(bzp, zraw)
    pack_basis(byp, yraw)

    pl.semaphore_wait(barrier, NW - 1 + NN - 1 + 4)

    def send(src, dst, ssem, rsem, where):
        c = pltpu.make_async_remote_copy(
            src_ref=src,
            dst_ref=dst,
            send_sem=ssem,
            recv_sem=rsem,
            device_id=where,
            device_id_type=MESH,
        )
        c.start()

    def done(ref, sem):
        pltpu.make_async_copy(ref, ref, sem).wait()

    def near(d):
        return core == (d + 1) % 2

    def share(own, whole, ssem, rsem):
        for d in FAR:

            @pl.when(near(d))
            def _(d=d):
                at = {"narrow": lax.rem(n + d, NN)}
                send(own, whole.at[n], ssem, rsem.at[d], at)

    def hand_over(whole, rsem, fsem, gsem):
        for d in FAR:

            @pl.when(near(d))
            def _(d=d):
                m = lax.rem(n + NN - d, NN)
                done(whole.at[m], rsem.at[d])
                send(whole.at[m], whole.at[m], fsem, gsem, {"wide": sibling})

    def by_core(whole, sem, blocks):
        @pl.when(core == 0)
        def _():
            done(whole.at[pl.ds(0, blocks)], sem)

        @pl.when(core == 1)
        def _():
            done(whole.at[pl.ds(0, 7 - blocks)], sem)

    ownz = pltpu.make_async_copy(bzp, wzp.at[n], lsem.at[14])
    owny = pltpu.make_async_copy(byp, wyp.at[n], lsem.at[10])
    rows_x = pl.ds(gy * CX, CX)
    for k in range(5):
        pltpu.make_async_copy(
            bx_ref.at[:, pl.ds(128 * k, 128)], wx.at[k, gx, core, rows_x], lsem.at[2]
        ).start()
    ownz.start()
    owny.start()
    share(bzp, wzp, zbs, zbr)
    share(byp, wyp, ybs, ybr)

    done(wx.at[:, gx, core, rows_x], lsem.at[2])
    for d in FAR:
        at = {"wide": gx * 16 + lax.rem(gy + d, 8) * 2 + core}
        block = wx.at[:, gx, core, rows_x]
        send(block, block, xs.at[0], xr.at[0], at)

    has = {"xu": w < NW - 1, "xd": w > 0, "yu": n < NN - 1, "yd": n > 0}
    spans = {
        "": (pl.ds(3, 10), pl.ds(3, 10)),
        "xu": (pl.ds(10, 3), pl.ds(0, 3)),
        "xd": (pl.ds(3, 3), pl.ds(13, 3)),
    }
    rows = {
        "": (pl.ds(8, 40), pl.ds(8, 40)),
        "yu": (pl.ds(45, 3), pl.ds(5, 3)),
        "yd": (pl.ds(8, 3), pl.ds(48, 3)),
    }
    opposite = {"": "", "xu": "xd", "xd": "xu", "yu": "yd", "yd": "yu"}
    whole_way = [
        ("xu", "", None),
        ("xd", "", None),
        ("xu", "yu", None),
        ("xu", "yd", None),
        ("xd", "yu", None),
        ("xd", "yd", None),
        ("", "yu", (3, 10)),
        ("", "yd", (3, 10)),
    ]
    ways = {"old": whole_way}
    for i, (x0, p) in enumerate(CHUNKS):
        side = ("xd", "xu", None)[i]
        ways[i, "x"] = [(side, b, None) for b in ("", "yu", "yd") if side]
        ways[i, "y"] = [("", b, (3 + x0, p)) for b in ("yu", "yd")]
    slots = {}
    for key, items in ways.items():
        if key != "old":
            for item in items:
                slots[item] = len(slots)

    def slot(key, item, j):
        return (0, j) if key == "old" else (1, slots[item])

    def exists(a, b):
        if a and b:
            return has[a] & has[b]
        return has[a or b]

    def side_of(a, planes, end):
        return pl.ds(*planes) if planes else spans[a][end]

    def start_halo(v, key):
        for j, item in enumerate(ways[key]):
            a, b, planes = item

            @pl.when(exists(a, b))
            def _(key=key, item=item, j=j, a=a, b=b, planes=planes):
                at = {}
                if a:
                    at["wide"] = wup if a == "xu" else wdn
                if b:
                    at["narrow"] = nup if b == "yu" else ndn
                send(
                    v.at[side_of(a, planes, 0), rows[b][0]],
                    v.at[side_of(a, planes, 1), rows[b][1]],
                    hs.at[slot(key, item, j)],
                    hr.at[slot(key, item, j)],
                    at,
                )

    def wait_halo(v, key):
        for j, item in enumerate(ways[key]):
            a, b, planes = item

            @pl.when(exists(opposite[a], opposite[b]))
            def _(key=key, item=item, j=j, a=a, b=b, planes=planes):
                done(v.at[side_of(a, planes, 1), rows[b][1]], hr.at[slot(key, item, j)])

    def drain_halo(v, key):
        for j, item in enumerate(ways[key]):
            a, b, planes = item

            @pl.when(exists(a, b))
            def _(key=key, item=item, j=j, a=a, b=b, planes=planes):
                done(v.at[side_of(a, planes, 0), rows[b][0]], hs.at[slot(key, item, j)])

    keep(bands.at[0], band(MASS))
    keep(bands.at[1], band(STIFF))
    for c in small:
        c.wait()
    exc[...] = jnp.transpose(jnp.broadcast_to(ex_ref[...].reshape(1, NX), (128, NX)))
    fills = (
        (w == 0, slice(0, 3), slice(0, 56)),
        (w == NW - 1, slice(13, 16), slice(0, 56)),
        (n == 0, slice(0, 16), slice(0, 8)),
        (n == NN - 1, slice(0, 16), slice(48, 56)),
    )
    for edge, ps, rs in fills:

        @pl.when(edge)
        def _(ps=ps, rs=rs):
            for v in (vd, vp):
                v[ps, rs, :] = jnp.zeros((ps.stop - ps.start, rs.stop - rs.start, NZ), jnp.float32)

    hand_over(wzp, zbr, zfs, zfr)
    done(wx.at[:, 0, 0, pl.ds(0, 70)], xr.at[0])
    for e in (2, 1, 3):
        at = {"wide": lax.rem(gx + e, 4) * 16 + gy * 2 + core}
        send(wx.at[:, gx, core], wx.at[:, gx, core], xs.at[1], xr.at[1], at)

    get_res.wait()
    ownz.wait()
    by_core(wzp, zfr, 3)
    unpack_basis(wz, wzp)
    for i, (x0, p) in enumerate(CHUNKS):
        flat = dot(wz[...], res[x0 : x0 + p].reshape(p * CY, NZ), 0, 1)
        n1s[i][:, 0:40, :] = flat[:, 0:120].reshape(NN, CY, 120)
        if p == 4:
            for m in range(NN):
                pack_plane(n1s[i], m, flat[m * CY : m * CY + CY, 120:160])
        pltpu.make_async_copy(n1s[i].at[n], n1r[i].at[n], n1rs.at[i, n]).start()
        for d in FAR:
            v = lax.rem(n + d, NN)
            at = {"narrow": v}
            send(n1s[i].at[v], n1r[i].at[n], n1ss.at[i], n1rs.at[i, n], at)

    hand_over(wyp, ybr, yfs, yfr)
    get_dir.wait()
    start_halo(vd, "old")
    tile = first_tile(gx, core, gy)
    two = has_second(gx, core, gy)
    one = jnp.logical_not(two)

    owny.wait()
    by_core(wyp, yfr, 3)
    unpack_basis(wy, wyp)
    keep(wyr, wy[...])

    for i, (x0, p) in enumerate(CHUNKS):
        for m in range(NN):
            done(n1r[i].at[m], n1rs.at[i, m])
            cols = slice(m * CY, m * CY + CY)
            for x in range(3):
                r = (x0 + x) * CY
                lines[r : r + CY, cols] = n1r[i][m, 0:40, x * CY : x * CY + CY]
            if p == 4:
                r = (x0 + 3) * CY
                lines[r : r + 16, cols] = n1r[i][m, 40:56, 0:40]
                lines[r + 16 : r + 32, cols] = n1r[i][m, 40:56, 40:80]
                lines[r + 32 : r + 40, cols] = n1r[i][m, 40:48, 80:120]
        span = slice(x0 * CY, (x0 + p) * CY)
        t2[span, :] = dot3(split(lines[span, :]), (wyr[0], wyr[1]), 1, 0)
        for x in range(p):
            r = (x0 + x) * CY
            at = 100 * x0 + x
            for j in range(2):
                s1[pl.ds(at + j * 40 * p, 40, stride=p), :] = t2[
                    r : r + CY, 128 * j : 128 * j + 128
                ]
            s1[pl.ds(at + 80 * p, 20, stride=p), :] = jnp.concatenate(
                [t2[r : r + 20, 256:320], t2[r + 20 : r + CY, 256:320]], axis=1
            )

        def send_u(x, c, y, i=i, x0=x0, p=p):
            at = device(x, c, y)
            src, dst = 100 * x0 + first_tile(x, c, y) * p, 128 * x0 + me * 2 * p
            double = has_second(x, c, y)

            @pl.when(double)
            def _():
                send(s1.at[pl.ds(src, 2 * p)], ub.at[pl.ds(dst, 2 * p)], us.at[i], ur.at[i], at)

            @pl.when(jnp.logical_not(double))
            def _():
                send(s1.at[pl.ds(src, p)], ub.at[pl.ds(dst, p)], us.at[i], ur.at[i], at)

        each_wide(send_u)

        def keep_u(size, x0=x0, p=p):
            c = pltpu.make_async_copy(
                s1.at[pl.ds(100 * x0 + tile * p, size)],
                ub.at[pl.ds(128 * x0 + me * 2 * p, size)],
                lsem.at[3],
            )
            c.start()
            c.wait()

        @pl.when(two)
        def _(p=p, keep_u=keep_u):
            keep_u(2 * p)

        @pl.when(one)
        def _(p=p, keep_u=keep_u):
            keep_u(p)

    ey = ey_ref[...].reshape(1, NZ)

    def shift_row(t):
        j = lax.div(t, 40)
        c = t - j * 40
        row = jnp.where(j == 0, ey[:, 0:128], ey[:, 128:256])
        tail = ey[:, 256:320]
        row = jnp.where(j == 2, jnp.concatenate([tail, tail], axis=1), row)
        late = c + 20 * lax.div(j, 2)
        low = lax.broadcasted_iota(jnp.int32, (1, 128), 1) < 64
        return row + jnp.where(low, ez_ref[n * CY + c], ez_ref[n * CY + late])

    shift = jnp.concatenate([shift_row(tile), shift_row(jnp.minimum(tile + 1, 99))], axis=1)
    done(wx.at[:, pl.ds(0, 3), 0], xr.at[1])
    send(wx.at[:, :, core], wx.at[:, :, core], xs.at[2], xr.at[2], {"wide": sibling})
    wait_halo(vd, "old")
    along_y(vd, my, ky, 0, CX + 6)
    along_xz(my, ky, first, second, bands, image)

    done(wx.at[:, :, 0], xr.at[2])
    for k in range(5):
        for x in range(CX):
            for g in range(8):
                wxp[k, x * 64 + g * 8 : x * 64 + g * 8 + 8, :] = wx[
                    k, g // 2, g % 2, pl.ds(x, 8, stride=CX), :
                ]
        cols = slice(128 * k, 128 * k + 128)
        high, low = split(wxp[k])
        wxr[:, 128 * k : 128 * k + 128] = high
        wxr[:, NX + 128 * k : NX + 128 * k + 128] = high
        wxr[:, 2 * NX + 128 * k : 2 * NX + 128 * k + 128] = low
        for i, (x0, p) in enumerate(CHUNKS):
            high, low = split(jnp.transpose(wxp[k, 64 * x0 : 64 * (x0 + p), :]))
            wxc[i][cols, 0 : 64 * p] = high
            wxc[i][cols, 64 * p : 128 * p] = high
            wxc[i][cols, 128 * p : 192 * p] = low
    keep(wyc, jnp.transpose(wy[...]))
    keep(wzc, jnp.transpose(wz[...]))
    spectral = None
    for i, (x0, p) in enumerate(CHUNKS):

        @pl.when(two)
        def _(i=i, p=p):
            done(ub.at[pl.ds(0, 126 * p)], ur.at[i])

        @pl.when(one)
        def _(i=i, x0=x0, p=p):
            for x in range(p):
                ub[pl.ds(128 * x0 + p + x, 64, stride=2 * p), :] = jnp.zeros((64, 128), jnp.float32)
            done(ub.at[pl.ds(0, 63 * p)], ur.at[i])

        if i == len(CHUNKS) - 1:
            pass
        both = jnp.concatenate(
            [
                jnp.concatenate(
                    [
                        ub[pl.ds(128 * x0 + k * p + x, 64, stride=2 * p), :]
                        for x in range(p)
                    ],
                    axis=0,
                )
                for k in range(2)
            ],
            axis=1,
        )
        term = long_dot(wxc[i][...], ends(both))
        if i == 0:
            part[...] = term
        elif i == 1:
            part[...] += term
        else:
            spectral = part[...] + term
    cols = jnp.concatenate([exc[...], exc[...]], axis=1)
    spectral = ends(spectral / (cols + shift))
    for i, (x0, p) in enumerate(CHUNKS):
        span = slice(64 * x0, 64 * (x0 + p))
        inverse = long_dot(wxr[span, :], spectral)
        for x in range(p):
            for k in range(2):
                vb[pl.ds(128 * x0 + k * p + x, 64, stride=2 * p), :] = inverse[
                    x * 64 : x * 64 + 64, 128 * k : 128 * k + 128
                ]

        def back(size, i=i, x0=x0, p=p):
            here = pl.ds(100 * x0 + tile * p, size)

            def send_v(x, c, y):
                src = vb.at[pl.ds(128 * x0 + (x * 16 + c * 8 + y) * 2 * p, size)]
                send(src, s2.at[here], vs.at[i], vr.at[i], device(x, c, y))

            each_wide(send_v)
            c = pltpu.make_async_copy(
                vb.at[pl.ds(128 * x0 + me * 2 * p, size)], s2.at[here], lsem.at[5]
            )
            c.start()
            c.wait()

        @pl.when(two)
        def _(p=p, back=back):
            back(2 * p)

        @pl.when(one)
        def _(p=p, back=back):
            back(p)

    for i, (x0, p) in enumerate(CHUNKS):
        @pl.when(two)
        def _(i=i, p=p):
            done(s2.at[pl.ds(0, 98 * p)], vr.at[i])

        @pl.when(one)
        def _(i=i, p=p):
            done(s2.at[pl.ds(0, 99 * p)], vr.at[i])

        for x in range(p):
            r = (x0 + x) * CY
            at = 100 * x0 + x
            for j in range(2):
                t2[r : r + CY, 128 * j : 128 * j + 128] = s2[
                    pl.ds(at + j * 40 * p, 40, stride=p), :
                ]
            b = s2[pl.ds(at + 80 * p, 20, stride=p), :]
            t2[r : r + 20, 256:320] = b[:, 0:64]
            t2[r + 20 : r + CY, 256:320] = b[:, 64:128]
        span = slice(x0 * CY, (x0 + p) * CY)
        lines[span, :] = dot3(split(t2[span, :]), (wyc[0], wyc[1]), 1, 0)
        for m in range(NN):
            cols = slice(m * CY, m * CY + CY)
            for x in range(3):
                r = (x0 + x) * CY
                n2s[i][m, 0:40, x * CY : x * CY + CY] = lines[r : r + CY, cols]
            if p == 4:
                r = (x0 + 3) * CY
                pack_plane(n2s[i], m, lines[r : r + CY, cols])
        own = pltpu.make_async_copy(n2s[i].at[n], n2r[i].at[n], lsem.at[7])
        own.start()
        for d in FAR:
            v = lax.rem(n + d, NN)
            send(n2s[i].at[v], n2r[i].at[n], n2ss.at[i], n2rs.at[i], {"narrow": v})
        own.wait()

    for i, (x0, p) in enumerate(CHUNKS):
        done(n2r[i].at[pl.ds(0, 7)], n2rs.at[i])
        flat = n2r[i][:, 0:40, :].reshape(NZ, 120)
        if p == 4:
            wide4[:, 0:120] = flat
            for m in range(NN):
                r = m * CY
                wide4[r : r + 16, 120:160] = n2r[i][m, 40:56, 0:40]
                wide4[r + 16 : r + 32, 120:160] = n2r[i][m, 40:56, 40:80]
                wide4[r + 32 : r + 40, 120:160] = n2r[i][m, 40:48, 80:120]
            flat = wide4[...]
        vp[3 + x0 : 3 + x0 + p, 8:48, :] = dot3(
            split(jnp.transpose(flat)), (wzc[0], wzc[1]), 1, 0
        ).reshape(p, CY, NZ)
        start_halo(vp, (i, "x"))
        start_halo(vp, (i, "y"))
        if i == 1:
            wait_halo(vp, (0, "y"))
            along_y(vp, my, ky, 3, 6)

    wait_halo(vp, (1, "y"))
    along_y(vp, my, ky, 9, 13)
    wait_halo(vp, (0, "x"))
    along_y(vp, my, ky, 13, 16)
    wait_halo(vp, (1, "x"))
    along_y(vp, my, ky, 0, 3)
    precond = vp[3:13, 8:48, :].reshape(CX * CY, NZ)
    direction = vd[3:13, 8:48, :].reshape(CX * CY, NZ)
    early = (
        total(res[...].reshape(CX * CY, NZ), precond),
        total(precond, image[...]),
        total(direction, image[...]),
    )
    wait_halo(vp, (2, "y"))
    along_y(vp, my, ky, 6, 9)
    along_xz(my, ky, first, second, bands, fresh)

    precond = vp[3:13, 8:48, :].reshape(CX * CY, NZ)
    direction = vd[3:13, 8:48, :].reshape(CX * CY, NZ)
    res2 = res[...].reshape(CX * CY, NZ)
    items = (early[0], total(precond, fresh[...]), early[1], early[2])
    lane = lax.broadcasted_iota(jnp.int32, (1, 128), 1)
    row = jnp.zeros((1, 128), jnp.float32)
    for i, item in enumerate(items):
        row = jnp.where(lane == i, item, row)
    red[0] = row
    rb1[n] = row
    for d in FAR:
        send(red.at[0], rb1.at[n], rs1, rr1, {"narrow": lax.rem(n + d, NN)})
    done(rb1.at[pl.ds(0, 7)], rr1)
    row = jnp.sum(rb1[...], axis=0)
    red[1] = row
    rb2[w] = row

    def send_r(x, c, y):
        send(red.at[1], rb2.at[w], rs2, rr2, device(x, c, y))

    each_wide(send_r)
    done(rb2.at[pl.ds(0, 63)], rr2)
    row = jnp.sum(rb2[...], axis=0)
    now, self_term, cross, curvature = (
        jnp.sum(jnp.where(lane == i, row, 0.0), axis=1, keepdims=True) for i in range(4)
    )
    ratio = now / prev_ref[0]
    curvature = self_term + 2.0 * ratio * cross + ratio * ratio * curvature
    alpha = now / curvature
    get_sol.wait()
    sol2 = sol[...].reshape(CX * CY, NZ)
    direction = precond + ratio * direction
    new_image = fresh[...] + ratio * image[...]
    sol_out[...] = (sol2 + alpha * direction).reshape(CX, CY, NZ)
    res_out[...] = (res2 - alpha * new_image).reshape(CX, CY, NZ)
    dir_out[...] = direction.reshape(CX, CY, NZ)

    by_core(wzp, zbs, 4)
    by_core(wzp, zfs, 4)
    by_core(wyp, ybs, 4)
    by_core(wyp, yfs, 4)
    done(wx.at[:, 0, 0, pl.ds(0, 70)], xs.at[0])
    done(wx.at[:, pl.ds(0, 3), 0], xs.at[1])
    done(wx.at[:, :, 0], xs.at[2])
    drain_halo(vd, "old")
    for i in range(len(CHUNKS)):
        drain_halo(vp, (i, "x"))
        drain_halo(vp, (i, "y"))
    for i, (x0, p) in enumerate(CHUNKS):
        done(n1s[i].at[pl.ds(0, 7)], n1ss.at[i])
        done(n2s[i].at[pl.ds(0, 7)], n2ss.at[i])

        @pl.when(two)
        def _(i=i, p=p):
            done(s1.at[pl.ds(0, 98 * p)], us.at[i])
            done(vb.at[pl.ds(0, 126 * p)], vs.at[i])

        @pl.when(one)
        def _(i=i, p=p):
            done(s1.at[pl.ds(0, 99 * p)], us.at[i])
            done(vb.at[pl.ds(0, 63 * p)], vs.at[i])

    done(rb1.at[pl.ds(0, 7)], rs1)
    done(rb2.at[pl.ds(0, 63)], rs2)


def finish(sol, res, direction, sol_out, res_out, dir_out, sems):
    pairs = ((sol, sol_out), (res, res_out), (direction, dir_out))
    copies = [pltpu.make_async_copy(a, b, sems.at[i]) for i, (a, b) in enumerate(pairs)]
    for c in copies:
        c.start()
    for c in copies:
        c.wait()


def per_device(sol, res, direction, prev, bx, by, bz, ex, ey, ez):
    f32 = jnp.float32
    brick = jax.ShapeDtypeStruct((CX, CY, NZ), f32)
    vmem = pl.BlockSpec(memory_space=pltpu.VMEM)
    hbm = pl.BlockSpec(memory_space=pltpu.HBM)
    dma = pltpu.SemaphoreType.DMA
    shapes = [
        (CX, CY, NZ),
        (CX, CY, NZ),
        (5, 4, 2, 80, 128),
        (NZ, NZ),
        (NZ, NZ),
        [2, 2, NZ, NZ],
        (NX, 128),
        (16, 56, NZ),
        (16, 56, NZ),
        (16, CY, NZ),
        (16, CY, NZ),
        (CX, CY, NZ),
        (CX, CY, NZ),
        (400, NZ),
        (400, NZ),
        tuple((NN, r, 120) for r in ROWS),
        tuple((NN, r, 120) for r in ROWS),
        (5, NX, 128),
        (NZ, 160),
        (CY, NZ),
        (CY, NZ),
        (104, 128),
        (104, 128),
        (NN, 104, 128),
        (NN, 104, 128),
        (NX, 256),
        [NX, 3 * NX],
        tuple([NX, 192 * p] for _, p in CHUNKS),
        [2, NZ, NZ],
        [2, NZ, NZ],
        [2, NZ, NZ],
        (400, NZ),
        (400, NZ),
        (1040, 128),
        (2 * NX + 16, 128),
        (2 * NX + 16, 128),
        (1040, 128),
        tuple((NN, r, 120) for r in ROWS),
        tuple((NN, r, 120) for r in ROWS),
        (2, 1, 128),
        (NN, 1, 128),
        (NW, 1, 128),
    ]
    sems = [(15,), (3,), (3,), (), (8,), (), (), (), (8,), (), ()]
    k = len(CHUNKS)
    sems += [(2, 12), (2, 12), (k,), (k, 8)] + [(k,)] * 6 + [()] * 4

    def space(s):
        if isinstance(s[0], (tuple, list)):
            return [space(t) for t in s]
        return pltpu.VMEM(tuple(s), jnp.bfloat16 if isinstance(s, list) else f32)

    far = [
        pltpu.with_memory_space_constraint(a, pltpu.HBM)
        for a in (ex, ey, ez, sol, res, direction, bx, by, bz)
    ]
    outs = pl.pallas_call(
        kernel,
        out_shape=(brick, brick, brick),
        in_specs=[pl.BlockSpec(memory_space=pltpu.SMEM)] + [hbm] * 9,
        out_specs=(vmem, vmem, vmem),
        scratch_shapes=[
            pltpu.VMEM((NX,), f32),
            pltpu.VMEM((NZ,), f32),
            pltpu.SMEM((NZ,), f32),
        ]
        + [space(s) for s in shapes]
        + [dma(s) for s in sems],
        compiler_params=pltpu.CompilerParams(
            collective_id=0, has_side_effects=True, vmem_limit_bytes=28 << 20
        ),
        name="iterate",
    )(prev, *far)
    return pl.pallas_call(
        finish,
        out_shape=(brick, brick, brick),
        in_specs=[vmem] * 3,
        out_specs=(hbm, hbm, hbm),
        scratch_shapes=[dma((3,))],
        compiler_params=pltpu.CompilerParams(vmem_limit_bytes=12 << 20),
        name="finish",
    )(*outs)


def solution(mesh):
    field = P("wide", "narrow", None)
    in_specs = (
        field,
        field,
        field,
        P(),
        P("wide", None),
        P("narrow", None),
        P("narrow", None),
        P(),
        P(),
        P(),
    )
    return jax.shard_map(
        per_device, mesh=mesh, in_specs=in_specs, out_specs=(field, field, field), check_vma=False
    )
```
